512 devices in a mesh: seq: 64 (over z, y), exp: 8 (over x, core).
Axes of the slice: x: 4, y: 4, z: 16, core: 2. Of those that a mesh axis runs over, the one named last changes fastest.
Arguments:
- queries: bfloat16 [16384, 6144], P('seq', 'exp'), may hold values from -6 to 6
- keys: bfloat16 [16384, 6144], P('seq', 'exp'), may hold values from -6 to 6
- values: bfloat16 [16384, 6144], P('seq', 'exp'), may hold values from -6 to 6
- selections: int32 [64, 8, 5], P('seq'), may hold values from 0 to 255
- router: bfloat16 [6144, 8], P(None, 'exp'), may hold values from -0.0390625 to 0.0390625
- w_up: bfloat16 [8, 9216, 6144], P('exp', 'seq'), may hold values from -0.15625 to 0.15625
- w_down: bfloat16 [8, 6144, 9216], P('exp', 'seq'), may hold values from -0.125 to 0.125
Outputs:
- layer_out: bfloat16 [16384, 6144], P('seq', 'exp')
The draws below stay inside these ranges and needn't reach their ends.
Inputs may be any that keep to these rules, and one draw needn't show every extreme that they name: `selections`: entries are positions inside the block of 256 tokens; different experts may pick the same token and an expert may pick a token twice.
All inputs are finite; a program needn't handle non-finite values.
Results may differ from the reference program's by a relative error of at most 0.018.
Values may be sent and summed in bfloat16 or wider, within the bound.
No kernel may reach another device: no remote copies, remote signals or barrier semaphores. Data moves between devices by JAX's collectives and lax.ppermute only.
A program may use at most 128 MiB of HBM per device.

```python
import jax
import jax.numpy as jnp
from jax import lax

D = 6144
HEADS = 64
HEAD = 96
FF = 9216
L_DEV = 256
CAP = 5
EXPERTS = 8
BLOCKS = 64
SEQ_LEN = 16384


def plant(entries, key, least, top_value):
    longest = entries.shape.index(max(entries.shape))
    spots = []
    for shift in (0, 1):
        where = [jax.random.randint(jax.random.fold_in(key, axis), (), 0, length) for axis, length in enumerate(entries.shape)]
        where[longest] = (where[longest] + shift) % entries.shape[longest]
        spots.append(tuple(where))
    return entries.at[spots[0]].set(least).at[spots[1]].set(top_value)


def level_of(own_key, shape, pieces, least, largest):
    level, own = 1.0, jax.random.fold_in(own_key, 6)
    for axis_at, parts in pieces:
        heights = jnp.exp(jax.random.uniform(jax.random.fold_in(own, axis_at), (parts,), jnp.float32, least / len(pieces), largest / len(pieces)))
        level = level * jnp.repeat(heights, shape[axis_at] // parts).reshape([-1 if axis == axis_at else 1 for axis in range(len(shape))])
    return level


def noise(key, shape, spread, most, split=(), kind=jnp.bfloat16):
    factor_of = level_of(key, shape, split, -0.22, 0.18) if split else 1.0
    entries = jax.random.normal(key, shape, jnp.float32) * spread * factor_of
    return jnp.minimum(jnp.maximum(entries, -most), most).astype(kind)


def setup_inputs(seed: int = 0) -> dict:
    seeds = jax.random.split(jax.random.key(seed), 8)
    queries = noise(seeds[0], (SEQ_LEN, D), 1.0, 6.0, ((0, 64), (1, 8)))
    keys = noise(seeds[1], (SEQ_LEN, D), 1.0, 6.0, ((0, 64), (1, 8)))
    values = noise(seeds[2], (SEQ_LEN, D), 1.0, 6.0, ((0, 64), (1, 8)))
    selections = plant(jax.random.randint(seeds[3], (BLOCKS, EXPERTS, CAP), 0, L_DEV), jax.random.fold_in(seeds[3], 1), 0, L_DEV - 1).astype(jnp.int32)
    router = noise(seeds[4], (D, EXPERTS), (4 * D) ** -0.5, 0.0390625, ((1, 8),))
    w_up = noise(seeds[5], (EXPERTS, FF, D), (D // 4) ** -0.5, 0.15625, ((0, 8), (1, 64)))
    w_down = noise(seeds[6], (EXPERTS, D, FF), (FF // 4) ** -0.5, 0.125, ((0, 8), (1, 64)))
    return {"queries": queries, "keys": keys, "values": values, "selections": selections, "router": router, "w_up": w_up, "w_down": w_down}


def reference(queries, keys, values, selections, router, w_up, w_down):
    blocks = selections.shape[0]
    length = queries.shape[0] // blocks
    query_heads = queries.reshape(blocks, length, HEADS, HEAD)
    key_heads = keys.reshape(blocks, length, HEADS, HEAD)
    value_heads = values.reshape(blocks, length, HEADS, HEAD)
    causal = jnp.arange(length)[:, None] >= jnp.arange(length)[None, :]

    def block_step(carried, inputs):
        query_block, key_block, value_block = inputs
        query_float = query_block.astype(jnp.float32)
        key_float = key_block.astype(jnp.float32)
        value_float = value_block.astype(jnp.float32)
        state = jnp.einsum('lhd,lhe->hde', key_float, value_float).astype(jnp.bfloat16)
        before = carried.astype(jnp.bfloat16).astype(jnp.float32)
        scores = jnp.einsum('qhd,khd->hqk', query_float, key_float)
        scores = jnp.where(causal[None], scores, 0.0).astype(jnp.bfloat16).astype(jnp.float32)
        inner = jnp.einsum('hqk,khe->qhe', scores, value_float)
        outer = jnp.einsum('qhd,hde->qhe', query_float, before)
        mixed = inner + outer
        power = lax.optimization_barrier(jnp.mean(mixed * mixed, axis=-1, keepdims=True))
        normed = (mixed * lax.rsqrt(power + 1e-06)).astype(jnp.bfloat16)
        return (carried + state.astype(jnp.float32), normed.reshape(length, HEADS * HEAD))
    initial = jnp.zeros((HEADS, HEAD, HEAD), jnp.float32)
    unused, attn = lax.scan(block_step, initial, (query_heads, key_heads, value_heads))
    attn = attn.reshape(blocks * length, HEADS * HEAD)
    offsets = (jnp.arange(blocks, dtype=jnp.int32) * length)[:, None]
    running = attn.astype(jnp.float32)
    for expert in range(EXPERTS):
        where = (selections[:, expert, :] + offsets).reshape(-1).astype(jnp.int32)
        picked_rows = attn[where]
        gate_value = jax.nn.sigmoid(jnp.dot(picked_rows, router[:, expert:expert + 1], preferred_element_type=jnp.float32))
        hidden = jax.nn.silu(jnp.dot(picked_rows, w_up[expert].T, preferred_element_type=jnp.float32)).astype(jnp.bfloat16)
        expert_out = jnp.dot(hidden, w_down[expert].T, preferred_element_type=jnp.float32)
        weighted = (gate_value * expert_out).astype(jnp.bfloat16)
        running = running.at[where].add(weighted.astype(jnp.float32))
    return running.astype(jnp.bfloat16)
```

```python
import jax
import jax.numpy as jnp
from jax import lax
from jax.experimental import pallas as pl
from jax.experimental.pallas import tpu as pltpu
from jax.sharding import Mesh, PartitionSpec as P

HEAD = 96
LANES = 128
SLOTS = 32
INTERPRET = False
BF16 = jnp.bfloat16
F32 = jnp.float32


def call(kernel, out, *args, scratch=(), name=None):
    return pl.pallas_call(
        kernel,
        out_shape=out,
        scratch_shapes=list(scratch),
        compiler_params=pltpu.CompilerParams(vmem_limit_bytes=48 * 2**20),
        interpret=INTERPRET,
        name=name,
    )(*args)


def tile_heads(tile):
    first = tile * LANES // HEAD
    return first, (first + 1) * HEAD - tile * LANES


def head_window(head):
    first, last = head * HEAD // LANES, (head * HEAD + HEAD - 1) // LANES
    return first * LANES, (last + 1) * LANES, head * HEAD - first * LANES


def chunk_rows(tile, third):
    upper, kind = divmod(tile, 3)
    return upper * 32 * 16 + kind * 3 + third


def state_kernel(k_ref, v_ref, out_ref, grand, rows):
    grand[...] = lax.dot_general(
        k_ref[...], v_ref[...], (((0,), (0,)), ((), ())), preferred_element_type=F32
    )
    rows[...] = jnp.zeros_like(rows)
    lane = lax.broadcasted_iota(jnp.int32, (HEAD, LANES), 1)
    for tile in range(6):
        head, split = tile_heads(tile)
        at = slice(tile * LANES, (tile + 1) * LANES)
        one = grand[head * HEAD : (head + 1) * HEAD, at]
        two = grand[(head + 1) * HEAD : (head + 2) * HEAD, at]
        block = jnp.where(lane < split, one, two)
        for third in range(3):
            rows[pl.ds(chunk_rows(tile, third), 32, stride=16), :] = block[third * 32 : third * 32 + 32]
    out_ref[...] = rows[...].reshape(64, 16, LANES).astype(BF16)


def prefix_kernel(in_ref, out_ref):
    total = jnp.zeros((16, LANES), F32)
    for block in range(in_ref.shape[0]):
        out_ref[block] = total.astype(BF16)
        total = total + in_ref[block].astype(F32)


def inner_kernel(q_ref, k_ref, v_ref, out_ref):
    length = q_ref.shape[0]
    out_ref[...] = jnp.zeros_like(out_ref)
    below = lax.broadcasted_iota(jnp.int32, (length, length), 0) >= lax.broadcasted_iota(
        jnp.int32, (length, length), 1
    )
    for head in range(8):
        start, stop, low = head_window(head)
        lane = lax.broadcasted_iota(jnp.int32, (1, stop - start), 1)
        mine = (lane >= low) & (lane < low + HEAD)
        q = q_ref[:, start:stop] * mine.astype(F32).astype(BF16)
        scores = lax.dot_general(
            q, k_ref[:, start:stop], (((1,), (1,)), ((), ())), preferred_element_type=F32
        )
        scores = jnp.where(below, scores, 0.0).astype(BF16)
        mixed = jnp.dot(scores, v_ref[:, start:stop], preferred_element_type=F32)
        out_ref[:, start:stop] = jnp.where(mine, mixed, out_ref[:, start:stop])


def attn_kernel(q_ref, inner_ref, p_ref, sel_ref, attn_ref, pay_ref, rows, wide, normed, picks):
    length = q_ref.shape[0]
    rows[...] = p_ref[...].astype(F32).reshape(64 * 16, LANES)
    wide[...] = jnp.zeros_like(wide)
    lane = lax.broadcasted_iota(jnp.int32, (32, LANES), 1)
    for tile in range(6):
        head, split = tile_heads(tile)
        at = slice(tile * LANES, (tile + 1) * LANES)
        for third in range(3):
            block = rows[pl.ds(chunk_rows(tile, third), 32, stride=16), :]
            low = head * HEAD + third * 32
            wide[low : low + 32, at] = jnp.where(lane < split, block, 0.0).astype(BF16)
            low = low + HEAD
            wide[low : low + 32, at] = jnp.where(lane < split, 0.0, block).astype(BF16)
    normed[...] = inner_ref[...] + jnp.dot(q_ref[...], wide[...], preferred_element_type=F32)
    for head in range(8):
        start, stop, low = head_window(head)
        lane = lax.broadcasted_iota(jnp.int32, (1, stop - start), 1)
        mine = (lane >= low) & (lane < low + HEAD)
        mixed = normed[:, start:stop]
        power = jnp.sum(jnp.where(mine, mixed * mixed, 0.0), axis=-1, keepdims=True) / HEAD
        normed[:, start:stop] = jnp.where(mine, mixed * lax.rsqrt(power + 1e-06), mixed)
    attn = normed[...].astype(BF16)
    attn_ref[...] = attn
    place = lax.broadcasted_iota(jnp.int32, (40, length), 1)
    chosen = jnp.where(place == sel_ref[...], 1.0, 0.0).astype(BF16)
    picked = jnp.dot(chosen, attn, preferred_element_type=F32)
    picks[...] = jnp.zeros_like(picks)
    for i in range(5):
        for tile in range(6):
            picks[pl.ds(i * 6 + tile, 8, stride=SLOTS), :] = picked[
                i * 8 : i * 8 + 8, tile * LANES : (tile + 1) * LANES
            ]
    pay = picks[...].reshape(8, SLOTS, LANES).astype(BF16)
    for copy in range(8):
        pay_ref[copy * 8 : copy * 8 + 8] = pay


def up_kernel(x_ref, w_ref, r_ref, out_ref, rows, picked):
    rows[...] = x_ref[...].astype(F32).reshape(64 * SLOTS, LANES)
    for i in range(5):
        for tile in range(6):
            piece = rows[pl.ds(i * 6 + tile, 64, stride=SLOTS), :]
            picked[i * 64 : i * 64 + 64, tile * LANES : (tile + 1) * LANES] = piece.astype(BF16)
    x = picked[...]
    units = w_ref.shape[0]
    out_ref[:, :units] = lax.dot_general(
        x, w_ref[...], (((1,), (1,)), ((), ())), preferred_element_type=F32
    ).astype(BF16)
    column = jnp.broadcast_to(r_ref[...].astype(F32), (LANES, x.shape[1])).astype(BF16)
    out_ref[:, units:] = lax.dot_general(
        x, column, (((1,), (1,)), ((), ())), preferred_element_type=F32
    ).astype(BF16)


def act_kernel(in_ref, out_ref):
    units = out_ref.shape[1]
    total = in_ref[0].astype(F32)
    for part in range(1, 8):
        total = total + in_ref[part].astype(F32)
    gate = jax.nn.sigmoid(total[:, units : units + 1])
    up = total[:, :units]
    out_ref[...] = (up / (1.0 + jnp.exp(-up)) * gate).astype(BF16)


def down_kernel(h_ref, w_ref, out_ref, rows):
    y = lax.dot_general(
        h_ref[...], w_ref[...], (((1,), (1,)), ((), ())), preferred_element_type=F32
    )
    for slot in (30, 31):
        rows[pl.ds(slot, 64, stride=SLOTS), :] = jnp.zeros((64, LANES), F32)
    for i in range(5):
        for tile in range(6):
            rows[pl.ds(i * 6 + tile, 64, stride=SLOTS), :] = y[
                i * 64 : i * 64 + 64, tile * LANES : (tile + 1) * LANES
            ]
    out_ref[...] = rows[...].reshape(64, SLOTS, LANES).astype(BF16)


def add_kernel(attn_ref, y_ref, sel_ref, out_ref, rows, weighted):
    length = attn_ref.shape[0]
    total = y_ref[0:8].astype(F32)
    for part in range(1, 8):
        total = total + y_ref[part * 8 : part * 8 + 8].astype(F32)
    rows[...] = total.reshape(8 * SLOTS, LANES)
    weighted[...] = jnp.zeros_like(weighted)
    for i in range(5):
        for tile in range(6):
            weighted[i * 8 : i * 8 + 8, tile * LANES : (tile + 1) * LANES] = rows[
                pl.ds(i * 6 + tile, 8, stride=SLOTS), :
            ]
    place = lax.broadcasted_iota(jnp.int32, (length, LANES), 0)
    chosen = jnp.where(place == sel_ref[...], 1.0, 0.0).astype(BF16)
    added = jnp.dot(chosen, weighted[...].astype(BF16), preferred_element_type=F32)
    out_ref[...] = (attn_ref[...].astype(F32) + added).astype(BF16)


def shape(dims, dtype=BF16):
    return jax.ShapeDtypeStruct(dims, dtype)


def body(queries, keys, values, selections, router, w_up, w_down):
    length, width = queries.shape
    parts = lax.axis_size("p")
    seq = ("r", "c")
    swap = [(c * parts + p, p * parts + c) for c in range(parts) for p in range(parts)]
    turn = [
        ((r * parts + c) * parts + p, (c * parts + p) * parts + r)
        for r in range(parts)
        for c in range(parts)
        for p in range(parts)
    ]

    up_here = lax.ppermute(w_up[0], ("c", "p"), swap)
    router_here = lax.ppermute(router.reshape(parts, width), ("c", "p"), swap)
    units, full = up_here.shape
    up_cut = up_here.reshape(units, parts, width).transpose(1, 0, 2)
    up_mine = lax.all_to_all(up_cut, "p", 0, 0, tiled=True).reshape(parts * units, width)
    router_mine = lax.dynamic_slice_in_dim(router_here, lax.axis_index("p"), 1, 0)
    columns, hidden = w_down[0].shape
    group = hidden // parts
    down_cut = w_down[0].reshape(columns, parts, group).transpose(1, 0, 2)
    down_near = lax.all_to_all(down_cut, "c", 0, 0, tiled=True)
    down_mine = lax.ppermute(down_near, ("r", "c", "p"), turn).reshape(parts * columns, group)

    sel = selections[0].T.reshape(-1)
    sel_column = sel[:, None]
    sel_row = jnp.pad(sel, (0, LANES - sel.shape[0]), constant_values=-1)[None]

    state = call(
        state_kernel,
        shape((64, 16, LANES)),
        keys,
        values,
        scratch=[pltpu.VMEM((width, width), F32), pltpu.VMEM((64 * 16, LANES), F32)],
        name="state",
    )
    chunks = lax.all_to_all(state, seq, 0, 0, tiled=True)
    inner = call(inner_kernel, shape((length, width), F32), queries, keys, values, name="inner")
    before = call(prefix_kernel, shape((64, 16, LANES)), chunks, name="prefix")
    before = lax.all_to_all(before, seq, 0, 0, tiled=True)
    attn, pay = call(
        attn_kernel,
        (shape((length, width)), shape((64, SLOTS, LANES))),
        queries,
        inner,
        before,
        sel_column,
        scratch=[
            pltpu.VMEM((64 * 16, LANES), F32),
            pltpu.VMEM((width, width), BF16),
            pltpu.VMEM((length, width), F32),
            pltpu.VMEM((8 * SLOTS, LANES), F32),
        ],
        name="attn",
    )
    arrived = lax.all_to_all(pay, seq, 0, 0, tiled=True)
    partial = call(
        up_kernel,
        shape((320, group + LANES)),
        arrived,
        up_mine,
        router_mine,
        scratch=[pltpu.VMEM((64 * SLOTS, LANES), F32), pltpu.VMEM((320, width), BF16)],
        name="up",
    )
    sums = lax.all_to_all(partial.reshape(parts, 40, group + LANES), "p", 0, 0, tiled=True)
    act = call(act_kernel, shape((40, group)), sums, name="act")
    act = lax.all_gather(act, "p", axis=0, tiled=True)
    out = call(
        down_kernel,
        shape((64, SLOTS, LANES)),
        act,
        down_mine,
        scratch=[pltpu.VMEM((64 * SLOTS, LANES), F32)],
        name="down",
    )
    back = lax.all_to_all(out, seq, 0, 0, tiled=True)
    return call(
        add_kernel,
        shape((length, width)),
        attn,
        back,
        sel_row,
        scratch=[pltpu.VMEM((8 * SLOTS, LANES), F32), pltpu.VMEM((LANES, width), F32)],
        name="add",
    )


def solution(mesh):
    parts = mesh.devices.shape[1]
    split = Mesh(mesh.devices.reshape(-1, parts, parts), ("r", "c", "p"))
    seq = ("r", "c")
    placed = (
        P(seq, "p"),
        P(seq, "p"),
        P(seq, "p"),
        P(seq, None, None),
        P(None, "p"),
        P("p", seq, None),
        P("p", seq, None),
    )
    return jax.shard_map(
        body, mesh=split, in_specs=placed, out_specs=P(seq, "p"), check_vma=False
    )
```

```python
import jax
import jax.numpy as jnp
from jax import lax
from jax.experimental import pallas as pl
from jax.experimental.pallas import tpu as pltpu
from jax.sharding import Mesh, PartitionSpec as P

HEAD = 96
LANES = 128
SLOTS = 32
INTERPRET = False
BF16 = jnp.bfloat16
F32 = jnp.float32


SMEM = pltpu.SMEM
VMEM = pltpu.VMEM
HBM = pltpu.HBM


def call(kernel, out, *args, scratch=(), spaces=None, name=None):
    specs = {}
    if spaces:
        ins, outs = spaces
        specs["in_specs"] = [pl.BlockSpec(memory_space=space) for space in ins]
        specs["out_specs"] = (
            [pl.BlockSpec(memory_space=space) for space in outs]
            if isinstance(outs, list)
            else pl.BlockSpec(memory_space=outs)
        )
    return pl.pallas_call(
        kernel,
        out_shape=out,
        scratch_shapes=list(scratch),
        compiler_params=pltpu.CompilerParams(vmem_limit_bytes=16 * 2**20),
        interpret=INTERPRET,
        name=name,
        **specs,
    )(*args)


def tile_heads(tile):
    first = tile * LANES // HEAD
    return first, (first + 1) * HEAD - tile * LANES


def head_window(head):
    first, last = head * HEAD // LANES, (head * HEAD + HEAD - 1) // LANES
    return first * LANES, (last + 1) * LANES, head * HEAD - first * LANES


def chunk_rows(tile, third):
    upper, kind = divmod(tile, 3)
    return upper * 32 * 16 + kind * 3 + third


def state_kernel(k_ref, v_ref, out_ref, grand, rows):
    grand[...] = lax.dot_general(
        k_ref[...], v_ref[...], (((0,), (0,)), ((), ())), preferred_element_type=F32
    )
    rows[...] = jnp.zeros_like(rows)
    lane = lax.broadcasted_iota(jnp.int32, (HEAD, LANES), 1)
    for tile in range(6):
        head, split = tile_heads(tile)
        at = slice(tile * LANES, (tile + 1) * LANES)
        one = grand[head * HEAD : (head + 1) * HEAD, at]
        two = grand[(head + 1) * HEAD : (head + 2) * HEAD, at]
        block = jnp.where(lane < split, one, two)
        for third in range(3):
            rows[pl.ds(chunk_rows(tile, third), 32, stride=16), :] = block[third * 32 : third * 32 + 32]
    out_ref[...] = rows[...].reshape(64, 16, LANES).astype(BF16)


def prefix_kernel(in_ref, out_ref):
    total = jnp.zeros((16, LANES), F32)
    for block in range(in_ref.shape[0]):
        out_ref[block] = total.astype(BF16)
        total = total + in_ref[block].astype(F32)


def inner_kernel(q_ref, k_ref, v_ref, out_ref):
    length = q_ref.shape[0]
    out_ref[...] = jnp.zeros_like(out_ref)
    below = lax.broadcasted_iota(jnp.int32, (length, length), 0) >= lax.broadcasted_iota(
        jnp.int32, (length, length), 1
    )
    for head in range(8):
        start, stop, low = head_window(head)
        lane = lax.broadcasted_iota(jnp.int32, (1, stop - start), 1)
        mine = (lane >= low) & (lane < low + HEAD)
        q = q_ref[:, start:stop] * mine.astype(F32).astype(BF16)
        scores = lax.dot_general(
            q, k_ref[:, start:stop], (((1,), (1,)), ((), ())), preferred_element_type=F32
        )
        scores = jnp.where(below, scores, 0.0).astype(BF16)
        mixed = jnp.dot(scores, v_ref[:, start:stop], preferred_element_type=F32)
        out_ref[:, start:stop] = jnp.where(mine, mixed, out_ref[:, start:stop])


def attn_kernel(q_ref, inner_ref, p_ref, sel_ref, attn_ref, pay_ref, rows, wide, normed, picks):
    length = q_ref.shape[0]
    rows[...] = p_ref[...].astype(F32).reshape(64 * 16, LANES)
    wide[...] = jnp.zeros_like(wide)
    lane = lax.broadcasted_iota(jnp.int32, (32, LANES), 1)
    for tile in range(6):
        head, split = tile_heads(tile)
        at = slice(tile * LANES, (tile + 1) * LANES)
        for third in range(3):
            block = rows[pl.ds(chunk_rows(tile, third), 32, stride=16), :]
            low = head * HEAD + third * 32
            wide[low : low + 32, at] = jnp.where(lane < split, block, 0.0).astype(BF16)
            low = low + HEAD
            wide[low : low + 32, at] = jnp.where(lane < split, 0.0, block).astype(BF16)
    normed[...] = inner_ref[...] + jnp.dot(q_ref[...], wide[...], preferred_element_type=F32)
    for head in range(8):
        start, stop, low = head_window(head)
        lane = lax.broadcasted_iota(jnp.int32, (1, stop - start), 1)
        mine = (lane >= low) & (lane < low + HEAD)
        mixed = normed[:, start:stop]
        power = jnp.sum(jnp.where(mine, mixed * mixed, 0.0), axis=-1, keepdims=True) / HEAD
        normed[:, start:stop] = jnp.where(mine, mixed * lax.rsqrt(power + 1e-06), mixed)
    attn = normed[...].astype(BF16)
    attn_ref[...] = attn
    place = lax.broadcasted_iota(jnp.int32, (40, length), 1)
    chosen = jnp.where(place == sel_ref[...], 1.0, 0.0).astype(BF16)
    picked = jnp.dot(chosen, attn, preferred_element_type=F32)
    picks[...] = jnp.zeros_like(picks)
    for i in range(5):
        for tile in range(6):
            picks[pl.ds(i * 6 + tile, 8, stride=SLOTS), :] = picked[
                i * 8 : i * 8 + 8, tile * LANES : (tile + 1) * LANES
            ]
    pay_ref[...] = picks[...].reshape(8, SLOTS, LANES).astype(BF16)


def cut_up_kernel(place_ref, w_ref, *refs):
    outs, sems = refs[:8], refs[8]
    width = outs[0].shape[1]
    copies = []
    for k, out in enumerate(outs):
        low = pl.multiple_of((place_ref[0] ^ k) * width, LANES)
        copies.append(pltpu.make_async_copy(w_ref.at[:, pl.ds(low, width)], out, sems.at[k]))
        copies[-1].start()
    for copy in copies:
        copy.wait()


def cut_down_kernel(place_ref, w_ref, *refs):
    outs, cut, sems = refs[:8], refs[8], refs[9]
    run = w_ref.shape[1] // 64
    for part in range(8):
        for group in range(8):
            low = (group * 8 + part) * run
            cut[part, :, group * run : (group + 1) * run] = w_ref[:, low : low + run]
    copies = []
    for k, out in enumerate(outs):
        copies.append(pltpu.make_async_copy(cut.at[place_ref[0] ^ k], out, sems.at[k]))
        copies[-1].start()
    for copy in copies:
        copy.wait()


def fetch(place_ref, pieces, whole, sems):
    copies = []
    for k, piece in enumerate(pieces):
        rows = piece.shape[0]
        low = pl.multiple_of((place_ref[0] ^ k) * rows, 16)
        copies.append(pltpu.make_async_copy(piece, whole.at[pl.ds(low, rows), :], sems.at[k]))
        copies[-1].start()
    return copies


def up_kernel(place_ref, x_ref, *refs):
    pieces, out_ref, rows, picked, whole, sems = refs[:8], *refs[8:]
    copies = fetch(place_ref, pieces, whole, sems)
    rows[...] = x_ref[...].astype(F32).reshape(64 * SLOTS, LANES)
    picked[320:] = jnp.zeros((64, picked.shape[1]), BF16)
    for i in range(5):
        for tile in range(6):
            piece = rows[pl.ds(i * 6 + tile, 64, stride=SLOTS), :]
            picked[i * 64 : i * 64 + 64, tile * LANES : (tile + 1) * LANES] = piece.astype(BF16)
    for copy in copies:
        copy.wait()
    out_ref[...] = lax.dot_general(
        whole[...], picked[...], (((1,), (1,)), ((), ())), preferred_element_type=F32
    ).astype(BF16)


def act_kernel(in_ref, out_ref):
    up = in_ref[0].astype(F32)
    for part in range(1, 8):
        up = up + in_ref[part].astype(F32)
    out_ref[...] = (up / (1.0 + jnp.exp(-up))).astype(BF16)


def down_kernel(place_ref, h_ref, *refs):
    pieces, out_ref, rows, whole, sems = refs[:8], *refs[8:]
    copies = fetch(place_ref, pieces, whole, sems)
    for slot in (30, 31):
        rows[pl.ds(slot, 64, stride=SLOTS), :] = jnp.zeros((64, LANES), F32)
    for copy in copies:
        copy.wait()
    y = lax.dot_general(
        h_ref[...], whole[...], (((0,), (1,)), ((), ())), preferred_element_type=F32
    )
    for i in range(5):
        for tile in range(6):
            rows[pl.ds(i * 6 + tile, 64, stride=SLOTS), :] = y[
                i * 64 : i * 64 + 64, tile * LANES : (tile + 1) * LANES
            ]
    out_ref[...] = rows[...].reshape(64, SLOTS, LANES).astype(BF16)


def weigh_kernel(y_ref, row_ref, router_ref, out_ref):
    products = jnp.zeros((SLOTS, LANES), F32)
    for part in range(8):
        products = products + row_ref[part].astype(F32) * router_ref[part].astype(F32)
    one = lax.broadcasted_iota(jnp.int32, (SLOTS, SLOTS), 0) // 6
    two = lax.broadcasted_iota(jnp.int32, (SLOTS, SLOTS), 1) // 6
    alike = jnp.where(one == two, 1.0, 0.0)
    sums = jnp.dot(
        alike, products, preferred_element_type=F32, precision=lax.Precision.HIGHEST
    )
    gate = jax.nn.sigmoid(jnp.sum(sums, axis=-1, keepdims=True))
    for group in range(8):
        total = y_ref[group * 8].astype(F32)
        for part in range(1, 8):
            total = total + y_ref[group * 8 + part].astype(F32)
        out_ref[group] = (total * gate).astype(BF16)


def add_kernel(attn_ref, y_ref, sel_ref, out_ref, rows, weighted):
    length = attn_ref.shape[0]
    rows[...] = y_ref[...].astype(F32).reshape(8 * SLOTS, LANES)
    weighted[...] = jnp.zeros_like(weighted)
    for i in range(5):
        for tile in range(6):
            weighted[i * 8 : i * 8 + 8, tile * LANES : (tile + 1) * LANES] = rows[
                pl.ds(i * 6 + tile, 8, stride=SLOTS), :
            ]
    place = lax.broadcasted_iota(jnp.int32, (length, LANES), 0)
    chosen = jnp.where(place == sel_ref[...], 1.0, 0.0).astype(BF16)
    added = jnp.dot(chosen, weighted[...].astype(BF16), preferred_element_type=F32)
    out_ref[...] = (attn_ref[...].astype(F32) + added).astype(BF16)


def shape(dims, dtype=BF16):
    return jax.ShapeDtypeStruct(dims, dtype)


def exchange(pieces, first, last):
    count = len(pieces)
    return [
        lax.ppermute(pieces[k], "c", [(c, c ^ k) for c in range(count)])
        for k in range(first, last)
    ]


def body(queries, keys, values, selections, router, w_up, w_down):
    length, width = queries.shape
    parts = lax.axis_size("p")
    seq = ("r", "c")
    units = w_up.shape[1]
    columns = w_down.shape[1]
    group = w_down.shape[2] // parts
    place = lax.axis_index("c").astype(jnp.int32).reshape(1)
    sel = selections[0].T.reshape(-1)
    sel_column = sel[:, None]
    sel_row = jnp.pad(sel, (0, LANES - sel.shape[0]), constant_values=-1)[None]
    router_rows = jnp.tile(router.reshape(parts, 6, LANES), (1, 5, 1))
    router_rows = jnp.pad(router_rows, ((0, 0), (0, SLOTS - 30), (0, 0)))

    state = call(
        state_kernel,
        shape((64, 16, LANES)),
        keys,
        values,
        scratch=[pltpu.VMEM((width, width), F32), pltpu.VMEM((64 * 16, LANES), F32)],
        name="state",
    )
    w_up, state = lax.optimization_barrier((w_up, state))
    chunks = lax.all_to_all(state, seq, 0, 0, tiled=True)
    up_pieces = call(
        cut_up_kernel,
        [shape((units, width))] * 8,
        place,
        w_up[0],
        scratch=[pltpu.SemaphoreType.DMA((8,))],
        spaces=([SMEM, HBM], [HBM] * 8),
        name="cut_up",
    )
    up_first = exchange(up_pieces, 1, 5)
    inner = call(inner_kernel, shape((length, width), F32), queries, keys, values, name="inner")
    chunks, inner, up_first = lax.optimization_barrier((chunks, inner, up_first))
    before = call(prefix_kernel, shape((64, 16, LANES)), chunks, name="prefix")
    w_down, up_pieces, before = lax.optimization_barrier((w_down, up_pieces, before))
    before = lax.all_to_all(before, seq, 0, 0, tiled=True)
    up_last = exchange(up_pieces, 5, 8)
    down_pieces = call(
        cut_down_kernel,
        [shape((columns, group))] * 8,
        place,
        w_down[0],
        scratch=[pltpu.VMEM((8, columns, group), BF16), pltpu.SemaphoreType.DMA((8,))],
        spaces=([SMEM, VMEM], [HBM] * 8),
        name="cut_down",
    )
    before, up_last, down_pieces = lax.optimization_barrier((before, up_last, down_pieces))
    down_moved = exchange(down_pieces, 1, 8)
    attn, pay = call(
        attn_kernel,
        (shape((length, width)), shape((8, SLOTS, LANES))),
        queries,
        inner,
        before,
        sel_column,
        scratch=[
            pltpu.VMEM((64 * 16, LANES), F32),
            pltpu.VMEM((width, width), BF16),
            pltpu.VMEM((length, width), F32),
            pltpu.VMEM((8 * SLOTS, LANES), F32),
        ],
        name="attn",
    )
    whole_rows = lax.all_to_all(pay, "p", 0, 0, tiled=True)
    arrived = lax.all_to_all(jnp.tile(whole_rows, (8, 1, 1)), seq, 0, 0, tiled=True)
    arrived, down_moved = lax.optimization_barrier((arrived, down_moved))
    partial = call(
        up_kernel,
        shape((8 * units, 384)),
        place,
        arrived,
        up_pieces[0],
        *up_first,
        *up_last,
        scratch=[
            pltpu.VMEM((64 * SLOTS, LANES), F32),
            pltpu.VMEM((384, width), BF16),
            pltpu.VMEM((8 * units, width), BF16),
            pltpu.SemaphoreType.DMA((8,)),
        ],
        spaces=([SMEM, VMEM] + [HBM] * 8, VMEM),
        name="up",
    )
    sums = lax.all_to_all(partial.reshape(8, units, 384), "c", 0, 0, tiled=True)
    act = call(act_kernel, shape((units, 384)), sums, name="act")
    act = lax.all_gather(act, "r", axis=0, tiled=True)
    out = call(
        down_kernel,
        shape((64, SLOTS, LANES)),
        place,
        act,
        down_pieces[0],
        *down_moved,
        scratch=[
            pltpu.VMEM((64 * SLOTS, LANES), F32),
            pltpu.VMEM((8 * columns, group), BF16),
            pltpu.SemaphoreType.DMA((8,)),
        ],
        spaces=([SMEM, VMEM] + [HBM] * 8, VMEM),
        name="down",
    )
    back = lax.all_to_all(out, seq, 0, 0, tiled=True)
    weighted = call(
        weigh_kernel, shape((8, SLOTS, LANES)), back, whole_rows, router_rows, name="weigh"
    )
    weighted = lax.all_to_all(weighted, "p", 0, 0, tiled=True)
    return call(
        add_kernel,
        shape((length, width)),
        attn,
        weighted,
        sel_row,
        scratch=[pltpu.VMEM((8 * SLOTS, LANES), F32), pltpu.VMEM((LANES, width), F32)],
        name="add",
    )


def solution(mesh):
    parts = mesh.devices.shape[1]
    split = Mesh(mesh.devices.reshape(-1, parts, parts), ("r", "c", "p"))
    seq = ("r", "c")
    placed = (
        P(seq, "p"),
        P(seq, "p"),
        P(seq, "p"),
        P(seq, None, None),
        P(None, "p"),
        P("p", seq, None),
        P("p", seq, None),
    )
    return jax.shard_map(
        body, mesh=split, in_specs=placed, out_specs=P(seq, "p"), check_vma=False
    )
```

```python
import jax
import jax.numpy as jnp
from jax import lax
from jax.experimental import pallas as pl
from jax.experimental.pallas import tpu as pltpu
from jax.sharding import Mesh, PartitionSpec as P

HEAD = 96
LANES = 128
SLOTS = 32
INTERPRET = False
BF16 = jnp.bfloat16
F32 = jnp.float32


SMEM = pltpu.SMEM
VMEM = pltpu.VMEM
HBM = pltpu.HBM


def call(kernel, out, *args, scratch=(), spaces=None, name=None):
    specs = {}
    if spaces:
        ins, outs = spaces
        specs["in_specs"] = [pl.BlockSpec(memory_space=space) for space in ins]
        specs["out_specs"] = (
            [pl.BlockSpec(memory_space=space) for space in outs]
            if isinstance(outs, list)
            else pl.BlockSpec(memory_space=outs)
        )
    return pl.pallas_call(
        kernel,
        out_shape=out,
        scratch_shapes=list(scratch),
        compiler_params=pltpu.CompilerParams(vmem_limit_bytes=16 * 2**20),
        interpret=INTERPRET,
        name=name,
        **specs,
    )(*args)


def tile_heads(tile):
    first = tile * LANES // HEAD
    return first, (first + 1) * HEAD - tile * LANES


def head_window(head):
    first, last = head * HEAD // LANES, (head * HEAD + HEAD - 1) // LANES
    return first * LANES, (last + 1) * LANES, head * HEAD - first * LANES


def chunk_rows(tile, third):
    upper, kind = divmod(tile, 3)
    return upper * 32 * 16 + kind * 3 + third


def state_kernel(k_ref, v_ref, out_ref, grand, rows):
    grand[...] = lax.dot_general(
        k_ref[...], v_ref[...], (((0,), (0,)), ((), ())), preferred_element_type=F32
    )
    rows[...] = jnp.zeros_like(rows)
    lane = lax.broadcasted_iota(jnp.int32, (HEAD, LANES), 1)
    for tile in range(6):
        head, split = tile_heads(tile)
        at = slice(tile * LANES, (tile + 1) * LANES)
        one = grand[head * HEAD : (head + 1) * HEAD, at]
        two = grand[(head + 1) * HEAD : (head + 2) * HEAD, at]
        block = jnp.where(lane < split, one, two)
        for third in range(3):
            rows[pl.ds(chunk_rows(tile, third), 32, stride=16), :] = block[third * 32 : third * 32 + 32]
    out_ref[...] = rows[...].reshape(64, 16, LANES).astype(BF16)


def prefix_kernel(in_ref, out_ref):
    total = jnp.zeros((16, LANES), F32)
    for block in range(in_ref.shape[0]):
        out_ref[block] = total.astype(BF16)
        total = total + in_ref[block].astype(F32)


def inner_kernel(q_ref, k_ref, v_ref, out_ref):
    length = q_ref.shape[0]
    out_ref[...] = jnp.zeros_like(out_ref)
    below = lax.broadcasted_iota(jnp.int32, (length, length), 0) >= lax.broadcasted_iota(
        jnp.int32, (length, length), 1
    )
    for head in range(8):
        start, stop, low = head_window(head)
        lane = lax.broadcasted_iota(jnp.int32, (1, stop - start), 1)
        mine = (lane >= low) & (lane < low + HEAD)
        q = q_ref[:, start:stop] * mine.astype(F32).astype(BF16)
        scores = lax.dot_general(
            q, k_ref[:, start:stop], (((1,), (1,)), ((), ())), preferred_element_type=F32
        )
        scores = jnp.where(below, scores, 0.0).astype(BF16)
        mixed = jnp.dot(scores, v_ref[:, start:stop], preferred_element_type=F32)
        out_ref[:, start:stop] = jnp.where(mine, mixed, out_ref[:, start:stop])


def attn_kernel(q_ref, inner_ref, p_ref, sel_ref, attn_ref, pay_ref, rows, wide, normed, picks):
    length = q_ref.shape[0]
    rows[...] = p_ref[...].astype(F32).reshape(64 * 16, LANES)
    wide[...] = jnp.zeros_like(wide)
    lane = lax.broadcasted_iota(jnp.int32, (32, LANES), 1)
    for tile in range(6):
        head, split = tile_heads(tile)
        at = slice(tile * LANES, (tile + 1) * LANES)
        for third in range(3):
            block = rows[pl.ds(chunk_rows(tile, third), 32, stride=16), :]
            low = head * HEAD + third * 32
            wide[low : low + 32, at] = jnp.where(lane < split, block, 0.0).astype(BF16)
            low = low + HEAD
            wide[low : low + 32, at] = jnp.where(lane < split, 0.0, block).astype(BF16)
    normed[...] = inner_ref[...] + jnp.dot(q_ref[...], wide[...], preferred_element_type=F32)
    for head in range(8):
        start, stop, low = head_window(head)
        lane = lax.broadcasted_iota(jnp.int32, (1, stop - start), 1)
        mine = (lane >= low) & (lane < low + HEAD)
        mixed = normed[:, start:stop]
        power = jnp.sum(jnp.where(mine, mixed * mixed, 0.0), axis=-1, keepdims=True) / HEAD
        normed[:, start:stop] = jnp.where(mine, mixed * lax.rsqrt(power + 1e-06), mixed)
    attn = normed[...].astype(BF16)
    attn_ref[...] = attn
    place = lax.broadcasted_iota(jnp.int32, (40, length), 1)
    chosen = jnp.where(place == sel_ref[...], 1.0, 0.0).astype(BF16)
    picked = jnp.dot(chosen, attn, preferred_element_type=F32)
    picks[...] = jnp.zeros_like(picks)
    for i in range(5):
        for tile in range(6):
            picks[pl.ds(i * 6 + tile, 8, stride=SLOTS), :] = picked[
                i * 8 : i * 8 + 8, tile * LANES : (tile + 1) * LANES
            ]
    pay_ref[...] = picks[...].reshape(8, SLOTS, LANES).astype(BF16)


def cut_up_kernel(place_ref, w_ref, *refs):
    outs, sems = refs[:8], refs[8]
    width = outs[0].shape[1]
    copies = []
    for k, out in enumerate(outs):
        low = pl.multiple_of((place_ref[0] ^ k) * width, LANES)
        copies.append(pltpu.make_async_copy(w_ref.at[:, pl.ds(low, width)], out, sems.at[k]))
        copies[-1].start()
    for copy in copies:
        copy.wait()


def cut_down_kernel(place_ref, w_ref, *refs):
    outs, cut, sems = refs[:8], refs[8], refs[9]
    run = w_ref.shape[1] // 64
    for part in range(8):
        for group in range(8):
            low = (group * 8 + part) * run
            cut[part, :, group * run : (group + 1) * run] = w_ref[:, low : low + run]
    copies = []
    for k, out in enumerate(outs):
        copies.append(pltpu.make_async_copy(cut.at[place_ref[0] ^ k], out, sems.at[k]))
        copies[-1].start()
    for copy in copies:
        copy.wait()


def fetch(place_ref, pieces, whole, sems):
    copies = []
    for k, piece in enumerate(pieces):
        rows = piece.shape[0]
        low = pl.multiple_of((place_ref[0] ^ k) * rows, 16)
        copies.append(pltpu.make_async_copy(piece, whole.at[pl.ds(low, rows), :], sems.at[k]))
        copies[-1].start()
    return copies


def up_kernel(place_ref, x_ref, *refs):
    pieces, out_ref, rows, picked, whole, sems = refs[:8], *refs[8:]
    copies = fetch(place_ref, pieces, whole, sems)
    rows[...] = x_ref[...].astype(F32).reshape(64 * SLOTS, LANES)
    picked[320:] = jnp.zeros((64, picked.shape[1]), BF16)
    for i in range(5):
        for tile in range(6):
            piece = rows[pl.ds(i * 6 + tile, 64, stride=SLOTS), :]
            picked[i * 64 : i * 64 + 64, tile * LANES : (tile + 1) * LANES] = piece.astype(BF16)
    for copy in copies:
        copy.wait()
    out_ref[...] = lax.dot_general(
        whole[...], picked[...], (((1,), (1,)), ((), ())), preferred_element_type=F32
    ).astype(BF16)


def act_kernel(in_ref, out_ref):
    up = in_ref[0].astype(F32)
    for part in range(1, 8):
        up = up + in_ref[part].astype(F32)
    out_ref[...] = (up / (1.0 + jnp.exp(-up))).astype(BF16)


def down_kernel(place_ref, h_ref, *refs):
    pieces, out_ref, rows, whole, sems = refs[:8], *refs[8:]
    copies = fetch(place_ref, pieces, whole, sems)
    for slot in (30, 31):
        rows[pl.ds(slot, 64, stride=SLOTS), :] = jnp.zeros((64, LANES), F32)
    for copy in copies:
        copy.wait()
    y = lax.dot_general(
        h_ref[...], whole[...], (((0,), (1,)), ((), ())), preferred_element_type=F32
    )
    for i in range(5):
        for tile in range(6):
            rows[pl.ds(i * 6 + tile, 64, stride=SLOTS), :] = y[
                i * 64 : i * 64 + 64, tile * LANES : (tile + 1) * LANES
            ]
    out_ref[...] = rows[...].reshape(64, SLOTS, LANES).astype(BF16)


def weigh_kernel(y_ref, row_ref, router_ref, out_ref):
    products = jnp.zeros((SLOTS, LANES), F32)
    for part in range(8):
        products = products + row_ref[part].astype(F32) * router_ref[part].astype(F32)
    one = lax.broadcasted_iota(jnp.int32, (SLOTS, SLOTS), 0) // 6
    two = lax.broadcasted_iota(jnp.int32, (SLOTS, SLOTS), 1) // 6
    alike = jnp.where(one == two, 1.0, 0.0)
    sums = jnp.dot(
        alike, products, preferred_element_type=F32, precision=lax.Precision.HIGHEST
    )
    gate = jax.nn.sigmoid(jnp.sum(sums, axis=-1, keepdims=True))
    for group in range(8):
        total = y_ref[group * 8].astype(F32)
        for part in range(1, 8):
            total = total + y_ref[group * 8 + part].astype(F32)
        out_ref[group] = (total * gate).astype(BF16)


def add_kernel(attn_ref, y_ref, sel_ref, out_ref, rows, weighted):
    length = attn_ref.shape[0]
    rows[...] = y_ref[...].astype(F32).reshape(8 * SLOTS, LANES)
    weighted[...] = jnp.zeros_like(weighted)
    for i in range(5):
        for tile in range(6):
            weighted[i * 8 : i * 8 + 8, tile * LANES : (tile + 1) * LANES] = rows[
                pl.ds(i * 6 + tile, 8, stride=SLOTS), :
            ]
    place = lax.broadcasted_iota(jnp.int32, (length, LANES), 0)
    chosen = jnp.where(place == sel_ref[...], 1.0, 0.0).astype(BF16)
    added = jnp.dot(chosen, weighted[...].astype(BF16), preferred_element_type=F32)
    out_ref[...] = (attn_ref[...].astype(F32) + added).astype(BF16)


def shape(dims, dtype=BF16):
    return jax.ShapeDtypeStruct(dims, dtype)


def exchange(pieces, first, last):
    count = len(pieces)
    return [
        lax.ppermute(pieces[k], "c", [(c, c ^ k) for c in range(count)])
        for k in range(first, last)
    ]


def body(queries, keys, values, selections, router, w_up, w_down):
    length, width = queries.shape
    parts = lax.axis_size("p")
    seq = ("r", "c")
    units = w_up.shape[1]
    columns = w_down.shape[1]
    group = w_down.shape[2] // parts
    place = lax.axis_index("c").astype(jnp.int32).reshape(1)
    sel = selections[0].T.reshape(-1)
    sel_column = sel[:, None]
    sel_row = jnp.pad(sel, (0, LANES - sel.shape[0]), constant_values=-1)[None]
    router_rows = jnp.tile(router.reshape(parts, 6, LANES), (1, 5, 1))
    router_rows = jnp.pad(router_rows, ((0, 0), (0, SLOTS - 30), (0, 0)))

    state = call(
        state_kernel,
        shape((64, 16, LANES)),
        keys,
        values,
        scratch=[pltpu.VMEM((width, width), F32), pltpu.VMEM((64 * 16, LANES), F32)],
        name="state",
    )
    w_up, state = lax.optimization_barrier((w_up, state))
    chunks = lax.all_to_all(state, seq, 0, 0, tiled=True)
    up_pieces = call(
        cut_up_kernel,
        [shape((units, width))] * 8,
        place,
        w_up[0],
        scratch=[pltpu.SemaphoreType.DMA((8,))],
        spaces=([SMEM, HBM], [HBM] * 8),
        name="cut_up",
    )
    up_first = exchange(up_pieces, 1, 3)
    inner = call(inner_kernel, shape((length, width), F32), queries, keys, values, name="inner")
    chunks, inner, up_first = lax.optimization_barrier((chunks, inner, up_first))
    before = call(prefix_kernel, shape((64, 16, LANES)), chunks, name="prefix")
    w_down, up_pieces, before = lax.optimization_barrier((w_down, up_pieces, before))
    before = lax.all_to_all(before, seq, 0, 0, tiled=True)
    up_next = exchange(up_pieces, 3, 6)
    down_pieces = call(
        cut_down_kernel,
        [shape((columns, group))] * 8,
        place,
        w_down[0],
        scratch=[pltpu.VMEM((8, columns, group), BF16), pltpu.SemaphoreType.DMA((8,))],
        spaces=([SMEM, VMEM], [HBM] * 8),
        name="cut_down",
    )
    before, up_next, up_pieces, down_pieces = lax.optimization_barrier(
        (before, up_next, up_pieces, down_pieces)
    )
    attn, pay = call(
        attn_kernel,
        (shape((length, width)), shape((8, SLOTS, LANES))),
        queries,
        inner,
        before,
        sel_column,
        scratch=[
            pltpu.VMEM((64 * 16, LANES), F32),
            pltpu.VMEM((width, width), BF16),
            pltpu.VMEM((length, width), F32),
            pltpu.VMEM((8 * SLOTS, LANES), F32),
        ],
        name="attn",
    )
    up_pieces, down_pieces, pay = lax.optimization_barrier((up_pieces, down_pieces, pay))
    up_cross = exchange(up_pieces, 6, 7)
    whole_rows = lax.all_to_all(pay, "p", 0, 0, tiled=True)
    whole_rows, up_cross, up_pieces, down_pieces = lax.optimization_barrier(
        (whole_rows, up_cross, up_pieces, down_pieces)
    )
    up_last = exchange(up_pieces, 7, 8)
    down_first = exchange(down_pieces, 1, 5)
    arrived = lax.all_to_all(jnp.tile(whole_rows, (8, 1, 1)), seq, 0, 0, tiled=True)
    arrived, up_last, down_first = lax.optimization_barrier((arrived, up_last, down_first))
    partial = call(
        up_kernel,
        shape((8 * units, 384)),
        place,
        arrived,
        up_pieces[0],
        *up_first,
        *up_next,
        *up_cross,
        *up_last,
        scratch=[
            pltpu.VMEM((64 * SLOTS, LANES), F32),
            pltpu.VMEM((384, width), BF16),
            pltpu.VMEM((8 * units, width), BF16),
            pltpu.SemaphoreType.DMA((8,)),
        ],
        spaces=([SMEM, VMEM] + [HBM] * 8, VMEM),
        name="up",
    )
    partial, down_pieces = lax.optimization_barrier((partial, down_pieces))
    down_last = exchange(down_pieces, 5, 8)
    sums = lax.all_to_all(partial.reshape(8, units, 384), "c", 0, 0, tiled=True)
    sums, down_last = lax.optimization_barrier((sums, down_last))
    act = call(act_kernel, shape((units, 384)), sums, name="act")
    act = lax.all_gather(act, "r", axis=0, tiled=True)
    out = call(
        down_kernel,
        shape((64, SLOTS, LANES)),
        place,
        act,
        down_pieces[0],
        *down_first,
        *down_last,
        scratch=[
            pltpu.VMEM((64 * SLOTS, LANES), F32),
            pltpu.VMEM((8 * columns, group), BF16),
            pltpu.SemaphoreType.DMA((8,)),
        ],
        spaces=([SMEM, VMEM] + [HBM] * 8, VMEM),
        name="down",
    )
    back = lax.all_to_all(out, seq, 0, 0, tiled=True)
    weighted = call(
        weigh_kernel, shape((8, SLOTS, LANES)), back, whole_rows, router_rows, name="weigh"
    )
    weighted = lax.all_to_all(weighted, "p", 0, 0, tiled=True)
    return call(
        add_kernel,
        shape((length, width)),
        attn,
        weighted,
        sel_row,
        scratch=[pltpu.VMEM((8 * SLOTS, LANES), F32), pltpu.VMEM((LANES, width), F32)],
        name="add",
    )


def solution(mesh):
    parts = mesh.devices.shape[1]
    split = Mesh(mesh.devices.reshape(-1, parts, parts), ("r", "c", "p"))
    seq = ("r", "c")
    placed = (
        P(seq, "p"),
        P(seq, "p"),
        P(seq, "p"),
        P(seq, None, None),
        P(None, "p"),
        P("p", seq, None),
        P("p", seq, None),
    )
    return jax.shard_map(
        body, mesh=split, in_specs=placed, out_specs=P(seq, "p"), check_vma=False
    )
```

```python
import jax
import jax.numpy as jnp
from jax import lax
from jax.experimental import pallas as pl
from jax.experimental.pallas import tpu as pltpu
from jax.sharding import Mesh, PartitionSpec as P

HEAD = 96
LANES = 128
SLOTS = 32
INTERPRET = False
BF16 = jnp.bfloat16
F32 = jnp.float32


HBM = pltpu.HBM


def call(kernel, out, *args, scratch=(), spaces=None, name=None):
    specs = {}
    if spaces:
        ins, outs = spaces
        specs["in_specs"] = [pl.BlockSpec(memory_space=space) for space in ins]
        specs["out_specs"] = (
            [pl.BlockSpec(memory_space=space) for space in outs]
            if isinstance(outs, list)
            else pl.BlockSpec(memory_space=outs)
        )
    return pl.pallas_call(
        kernel,
        out_shape=out,
        scratch_shapes=list(scratch),
        compiler_params=pltpu.CompilerParams(vmem_limit_bytes=16 * 2**20),
        interpret=INTERPRET,
        name=name,
        **specs,
    )(*args)


def tile_heads(tile):
    first = tile * LANES // HEAD
    return first, (first + 1) * HEAD - tile * LANES


def head_window(head):
    first, last = head * HEAD // LANES, (head * HEAD + HEAD - 1) // LANES
    return first * LANES, (last + 1) * LANES, head * HEAD - first * LANES


def chunk_rows(tile, third):
    upper, kind = divmod(tile, 3)
    return upper * 32 * 16 + kind * 3 + third


def state_kernel(k_ref, v_ref, out_ref, grand, rows):
    grand[...] = lax.dot_general(
        k_ref[...], v_ref[...], (((0,), (0,)), ((), ())), preferred_element_type=F32
    )
    rows[...] = jnp.zeros_like(rows)
    lane = lax.broadcasted_iota(jnp.int32, (HEAD, LANES), 1)
    for tile in range(6):
        head, split = tile_heads(tile)
        at = slice(tile * LANES, (tile + 1) * LANES)
        one = grand[head * HEAD : (head + 1) * HEAD, at]
        two = grand[(head + 1) * HEAD : (head + 2) * HEAD, at]
        block = jnp.where(lane < split, one, two)
        for third in range(3):
            rows[pl.ds(chunk_rows(tile, third), 32, stride=16), :] = block[third * 32 : third * 32 + 32]
    out_ref[...] = rows[...].reshape(64, 16, LANES).astype(BF16)


def prefix_kernel(in_ref, out_ref):
    total = jnp.zeros((16, LANES), F32)
    for block in range(in_ref.shape[0]):
        out_ref[block] = total.astype(BF16)
        total = total + in_ref[block].astype(F32)


def inner_kernel(q_ref, k_ref, v_ref, out_ref):
    length = q_ref.shape[0]
    out_ref[...] = jnp.zeros_like(out_ref)
    below = lax.broadcasted_iota(jnp.int32, (length, length), 0) >= lax.broadcasted_iota(
        jnp.int32, (length, length), 1
    )
    for head in range(8):
        start, stop, low = head_window(head)
        lane = lax.broadcasted_iota(jnp.int32, (1, stop - start), 1)
        mine = (lane >= low) & (lane < low + HEAD)
        q = q_ref[:, start:stop] * mine.astype(F32).astype(BF16)
        scores = lax.dot_general(
            q, k_ref[:, start:stop], (((1,), (1,)), ((), ())), preferred_element_type=F32
        )
        scores = jnp.where(below, scores, 0.0).astype(BF16)
        mixed = jnp.dot(scores, v_ref[:, start:stop], preferred_element_type=F32)
        out_ref[:, start:stop] = jnp.where(mine, mixed, out_ref[:, start:stop])


def attn_kernel(q_ref, inner_ref, p_ref, sel_ref, attn_ref, pay_ref, rows, wide, normed, picks):
    length = q_ref.shape[0]
    rows[...] = p_ref[...].astype(F32).reshape(64 * 16, LANES)
    wide[...] = jnp.zeros_like(wide)
    lane = lax.broadcasted_iota(jnp.int32, (32, LANES), 1)
    for tile in range(6):
        head, split = tile_heads(tile)
        at = slice(tile * LANES, (tile + 1) * LANES)
        for third in range(3):
            block = rows[pl.ds(chunk_rows(tile, third), 32, stride=16), :]
            low = head * HEAD + third * 32
            wide[low : low + 32, at] = jnp.where(lane < split, block, 0.0).astype(BF16)
            low = low + HEAD
            wide[low : low + 32, at] = jnp.where(lane < split, 0.0, block).astype(BF16)
    normed[...] = inner_ref[...] + jnp.dot(q_ref[...], wide[...], preferred_element_type=F32)
    for head in range(8):
        start, stop, low = head_window(head)
        lane = lax.broadcasted_iota(jnp.int32, (1, stop - start), 1)
        mine = (lane >= low) & (lane < low + HEAD)
        mixed = normed[:, start:stop]
        power = jnp.sum(jnp.where(mine, mixed * mixed, 0.0), axis=-1, keepdims=True) / HEAD
        normed[:, start:stop] = jnp.where(mine, mixed * lax.rsqrt(power + 1e-06), mixed)
    attn = normed[...].astype(BF16)
    attn_ref[...] = attn
    place = lax.broadcasted_iota(jnp.int32, (40, length), 1)
    chosen = jnp.where(place == sel_ref[...], 1.0, 0.0).astype(BF16)
    picked = jnp.dot(chosen, attn, preferred_element_type=F32)
    picks[...] = jnp.zeros_like(picks)
    for i in range(5):
        for tile in range(6):
            picks[pl.ds(i * 6 + tile, 8, stride=SLOTS), :] = picked[
                i * 8 : i * 8 + 8, tile * LANES : (tile + 1) * LANES
            ]
    pay_ref[...] = picks[...].reshape(8, SLOTS, LANES).astype(BF16)


def cut_up_kernel(w_ref, out_ref, sems):
    width = out_ref.shape[2]
    copies = []
    for part in range(8):
        source = w_ref.at[:, part * width : (part + 1) * width]
        copies.append(pltpu.make_async_copy(source, out_ref.at[part], sems.at[part]))
        copies[-1].start()
    for copy in copies:
        copy.wait()


def cut_down_kernel(w_ref, out_ref):
    run = w_ref.shape[1] // 64
    for part in range(8):
        for group in range(8):
            low = (group * 8 + part) * run
            out_ref[part, :, group * run : (group + 1) * run] = w_ref[:, low : low + run]


def up_kernel(x_ref, w_ref, out_ref, rows, picked):
    rows[...] = x_ref[...].astype(F32).reshape(64 * SLOTS, LANES)
    picked[320:] = jnp.zeros((64, picked.shape[1]), BF16)
    for i in range(5):
        for tile in range(6):
            piece = rows[pl.ds(i * 6 + tile, 64, stride=SLOTS), :]
            picked[i * 64 : i * 64 + 64, tile * LANES : (tile + 1) * LANES] = piece.astype(BF16)
    out_ref[...] = lax.dot_general(
        w_ref[...], picked[...], (((1,), (1,)), ((), ())), preferred_element_type=F32
    ).astype(BF16)


def act_kernel(in_ref, out_ref):
    up = in_ref[0].astype(F32)
    for part in range(1, 8):
        up = up + in_ref[part].astype(F32)
    out_ref[...] = (up / (1.0 + jnp.exp(-up))).astype(BF16)


def down_kernel(h_ref, w_ref, out_ref, rows):
    for slot in (30, 31):
        rows[pl.ds(slot, 64, stride=SLOTS), :] = jnp.zeros((64, LANES), F32)
    y = lax.dot_general(
        h_ref[...], w_ref[...], (((0,), (1,)), ((), ())), preferred_element_type=F32
    )
    for i in range(5):
        for tile in range(6):
            rows[pl.ds(i * 6 + tile, 64, stride=SLOTS), :] = y[
                i * 64 : i * 64 + 64, tile * LANES : (tile + 1) * LANES
            ]
    out_ref[...] = rows[...].reshape(64, SLOTS, LANES).astype(BF16)


def weigh_kernel(y_ref, row_ref, router_ref, out_ref):
    products = jnp.zeros((SLOTS, LANES), F32)
    for part in range(8):
        products = products + row_ref[part].astype(F32) * router_ref[part].astype(F32)
    one = lax.broadcasted_iota(jnp.int32, (SLOTS, SLOTS), 0) // 6
    two = lax.broadcasted_iota(jnp.int32, (SLOTS, SLOTS), 1) // 6
    alike = jnp.where(one == two, 1.0, 0.0)
    sums = jnp.dot(
        alike, products, preferred_element_type=F32, precision=lax.Precision.HIGHEST
    )
    gate = jax.nn.sigmoid(jnp.sum(sums, axis=-1, keepdims=True))
    for group in range(8):
        total = y_ref[group * 8].astype(F32)
        for part in range(1, 8):
            total = total + y_ref[group * 8 + part].astype(F32)
        out_ref[group] = (total * gate).astype(BF16)


def add_kernel(attn_ref, y_ref, sel_ref, out_ref, rows, weighted):
    length = attn_ref.shape[0]
    rows[...] = y_ref[...].astype(F32).reshape(8 * SLOTS, LANES)
    weighted[...] = jnp.zeros_like(weighted)
    for i in range(5):
        for tile in range(6):
            weighted[i * 8 : i * 8 + 8, tile * LANES : (tile + 1) * LANES] = rows[
                pl.ds(i * 6 + tile, 8, stride=SLOTS), :
            ]
    place = lax.broadcasted_iota(jnp.int32, (length, LANES), 0)
    chosen = jnp.where(place == sel_ref[...], 1.0, 0.0).astype(BF16)
    added = jnp.dot(chosen, weighted[...].astype(BF16), preferred_element_type=F32)
    out_ref[...] = (attn_ref[...].astype(F32) + added).astype(BF16)


def shape(dims, dtype=BF16):
    return jax.ShapeDtypeStruct(dims, dtype)


def body(queries, keys, values, selections, router, w_up, w_down):
    length, width = queries.shape
    parts = lax.axis_size("p")
    seq = ("r", "c")
    units = w_up.shape[1]
    columns = w_down.shape[1]
    group = w_down.shape[2] // parts
    sel = selections[0].T.reshape(-1)
    sel_column = sel[:, None]
    sel_row = jnp.pad(sel, (0, LANES - sel.shape[0]), constant_values=-1)[None]
    router_rows = jnp.tile(router.reshape(parts, 6, LANES), (1, 5, 1))
    router_rows = jnp.pad(router_rows, ((0, 0), (0, SLOTS - 30), (0, 0)))

    state = call(
        state_kernel,
        shape((64, 16, LANES)),
        keys,
        values,
        scratch=[pltpu.VMEM((width, width), F32), pltpu.VMEM((64 * 16, LANES), F32)],
        name="state",
    )
    w_up, w_down, state = lax.optimization_barrier((w_up, w_down, state))
    chunks = lax.all_to_all(state, seq, 0, 0, tiled=True)
    inner = call(inner_kernel, shape((length, width), F32), queries, keys, values, name="inner")
    up_cut = call(
        cut_up_kernel,
        shape((8, units, width)),
        w_up[0],
        scratch=[pltpu.SemaphoreType.DMA((8,))],
        spaces=([HBM], HBM),
        name="cut_up",
    )
    chunks, inner, up_cut = lax.optimization_barrier((chunks, inner, up_cut))
    before = call(prefix_kernel, shape((64, 16, LANES)), chunks, name="prefix")
    before, w_down = lax.optimization_barrier((before, w_down))
    before = lax.all_to_all(before, seq, 0, 0, tiled=True)
    down_cut = call(cut_down_kernel, shape((8, columns, group)), w_down[0], name="cut_down")
    before, down_cut = lax.optimization_barrier((before, down_cut))
    attn, pay = call(
        attn_kernel,
        (shape((length, width)), shape((8, SLOTS, LANES))),
        queries,
        inner,
        before,
        sel_column,
        scratch=[
            pltpu.VMEM((64 * 16, LANES), F32),
            pltpu.VMEM((width, width), BF16),
            pltpu.VMEM((length, width), F32),
            pltpu.VMEM((8 * SLOTS, LANES), F32),
        ],
        name="attn",
    )
    whole_rows = lax.all_to_all(pay, "p", 0, 0, tiled=True)
    near_rows = lax.all_to_all(whole_rows, "c", 0, 0, tiled=True)
    near_rows, up_cut = lax.optimization_barrier((near_rows, up_cut))
    up_mine = lax.all_to_all(up_cut, "c", 0, 0, tiled=True).reshape(8 * units, width)
    arrived = lax.all_gather(near_rows, "r", axis=0, tiled=True)
    partial = call(
        up_kernel,
        shape((8 * units, 384)),
        arrived,
        up_mine,
        scratch=[pltpu.VMEM((64 * SLOTS, LANES), F32), pltpu.VMEM((384, width), BF16)],
        name="up",
    )
    sums = lax.all_to_all(partial.reshape(8, units, 384), "c", 0, 0, tiled=True)
    act = call(act_kernel, shape((units, 384)), sums, name="act")
    act, down_cut = lax.optimization_barrier((act, down_cut))
    down_mine = lax.all_to_all(down_cut, "c", 0, 0, tiled=True).reshape(8 * columns, group)
    act = lax.all_gather(act, "r", axis=0, tiled=True)
    out = call(
        down_kernel,
        shape((64, SLOTS, LANES)),
        act,
        down_mine,
        scratch=[pltpu.VMEM((64 * SLOTS, LANES), F32)],
        name="down",
    )
    back = lax.all_to_all(out, seq, 0, 0, tiled=True)
    weighted = call(
        weigh_kernel, shape((8, SLOTS, LANES)), back, whole_rows, router_rows, name="weigh"
    )
    weighted = lax.all_to_all(weighted, "p", 0, 0, tiled=True)
    return call(
        add_kernel,
        shape((length, width)),
        attn,
        weighted,
        sel_row,
        scratch=[pltpu.VMEM((8 * SLOTS, LANES), F32), pltpu.VMEM((LANES, width), F32)],
        name="add",
    )


def solution(mesh):
    parts = mesh.devices.shape[1]
    split = Mesh(mesh.devices.reshape(-1, parts, parts), ("r", "c", "p"))
    seq = ("r", "c")
    placed = (
        P(seq, "p"),
        P(seq, "p"),
        P(seq, "p"),
        P(seq, None, None),
        P(None, "p"),
        P("p", seq, None),
        P("p", seq, None),
    )
    return jax.shard_map(
        body, mesh=split, in_specs=placed, out_specs=P(seq, "p"), check_vma=False
    )
```

```python
import functools

import jax
import jax.numpy as jnp
from jax import lax
from jax.experimental import pallas as pl
from jax.experimental.pallas import tpu as pltpu
from jax.sharding import Mesh, PartitionSpec as P

HEAD = 96
LANES = 128
SLOTS = 32
INTERPRET = False
BF16 = jnp.bfloat16
F32 = jnp.float32


HBM = pltpu.HBM
SMEM = pltpu.SMEM
VMEM = pltpu.VMEM


def call(kernel, out, *args, scratch=(), spaces=None, name=None):
    specs = {}
    if spaces:
        ins, outs = spaces
        specs["in_specs"] = [pl.BlockSpec(memory_space=space) for space in ins]
        specs["out_specs"] = (
            [pl.BlockSpec(memory_space=space) for space in outs]
            if isinstance(outs, list)
            else pl.BlockSpec(memory_space=outs)
        )
    return pl.pallas_call(
        kernel,
        out_shape=out,
        scratch_shapes=list(scratch),
        compiler_params=pltpu.CompilerParams(vmem_limit_bytes=16 * 2**20),
        interpret=INTERPRET,
        name=name,
        **specs,
    )(*args)


def tile_heads(tile):
    first = tile * LANES // HEAD
    return first, (first + 1) * HEAD - tile * LANES


def head_window(head):
    first, last = head * HEAD // LANES, (head * HEAD + HEAD - 1) // LANES
    return first * LANES, (last + 1) * LANES, head * HEAD - first * LANES


def chunk_rows(tile, third):
    upper, kind = divmod(tile, 3)
    return upper * 32 * 16 + kind * 3 + third


def state_kernel(k_ref, v_ref, out_ref, grand, rows):
    grand[...] = lax.dot_general(
        k_ref[...], v_ref[...], (((0,), (0,)), ((), ())), preferred_element_type=F32
    )
    rows[...] = jnp.zeros_like(rows)
    lane = lax.broadcasted_iota(jnp.int32, (HEAD, LANES), 1)
    for tile in range(6):
        head, split = tile_heads(tile)
        at = slice(tile * LANES, (tile + 1) * LANES)
        one = grand[head * HEAD : (head + 1) * HEAD, at]
        two = grand[(head + 1) * HEAD : (head + 2) * HEAD, at]
        block = jnp.where(lane < split, one, two)
        for third in range(3):
            rows[pl.ds(chunk_rows(tile, third), 32, stride=16), :] = block[third * 32 : third * 32 + 32]
    out_ref[...] = rows[...].reshape(64, 16, LANES).astype(BF16)


def prefix_kernel(in_ref, out_ref):
    total = jnp.zeros((16, LANES), F32)
    for block in range(in_ref.shape[0]):
        out_ref[block] = total.astype(BF16)
        total = total + in_ref[block].astype(F32)


def inner_kernel(q_ref, k_ref, v_ref, out_ref):
    length = q_ref.shape[0]
    out_ref[...] = jnp.zeros_like(out_ref)
    below = lax.broadcasted_iota(jnp.int32, (length, length), 0) >= lax.broadcasted_iota(
        jnp.int32, (length, length), 1
    )
    for head in range(8):
        start, stop, low = head_window(head)
        lane = lax.broadcasted_iota(jnp.int32, (1, stop - start), 1)
        mine = (lane >= low) & (lane < low + HEAD)
        q = q_ref[:, start:stop] * mine.astype(F32).astype(BF16)
        scores = lax.dot_general(
            q, k_ref[:, start:stop], (((1,), (1,)), ((), ())), preferred_element_type=F32
        )
        scores = jnp.where(below, scores, 0.0).astype(BF16)
        mixed = jnp.dot(scores, v_ref[:, start:stop], preferred_element_type=F32)
        out_ref[:, start:stop] = jnp.where(mine, mixed, out_ref[:, start:stop])


def attn_kernel(q_ref, inner_ref, p_ref, sel_ref, attn_ref, pay_ref, rows, wide, normed, picks):
    length = q_ref.shape[0]
    rows[...] = p_ref[...].astype(F32).reshape(64 * 16, LANES)
    wide[...] = jnp.zeros_like(wide)
    lane = lax.broadcasted_iota(jnp.int32, (32, LANES), 1)
    for tile in range(6):
        head, split = tile_heads(tile)
        at = slice(tile * LANES, (tile + 1) * LANES)
        for third in range(3):
            block = rows[pl.ds(chunk_rows(tile, third), 32, stride=16), :]
            low = head * HEAD + third * 32
            wide[low : low + 32, at] = jnp.where(lane < split, block, 0.0).astype(BF16)
            low = low + HEAD
            wide[low : low + 32, at] = jnp.where(lane < split, 0.0, block).astype(BF16)
    normed[...] = inner_ref[...] + jnp.dot(q_ref[...], wide[...], preferred_element_type=F32)
    for head in range(8):
        start, stop, low = head_window(head)
        lane = lax.broadcasted_iota(jnp.int32, (1, stop - start), 1)
        mine = (lane >= low) & (lane < low + HEAD)
        mixed = normed[:, start:stop]
        power = jnp.sum(jnp.where(mine, mixed * mixed, 0.0), axis=-1, keepdims=True) / HEAD
        normed[:, start:stop] = jnp.where(mine, mixed * lax.rsqrt(power + 1e-06), mixed)
    attn = normed[...].astype(BF16)
    attn_ref[...] = attn
    place = lax.broadcasted_iota(jnp.int32, (40, length), 1)
    chosen = jnp.where(place == sel_ref[...], 1.0, 0.0).astype(BF16)
    picked = jnp.dot(chosen, attn, preferred_element_type=F32)
    picks[...] = jnp.zeros_like(picks)
    for i in range(5):
        for tile in range(6):
            picks[pl.ds(i * 6 + tile, 8, stride=SLOTS), :] = picked[
                i * 8 : i * 8 + 8, tile * LANES : (tile + 1) * LANES
            ]
    pay_ref[...] = picks[...].reshape(8, SLOTS, LANES).astype(BF16)


def piece_of(k, outs):
    for first, out in zip((4, 2, 1, 0), outs):
        if k >= first:
            return out.at[k - first]


def cut_up_kernel(order_ref, w_ref, *refs):
    outs, sems = refs[:4], refs[4]
    width = outs[0].shape[2]
    copies = []
    for k in range(8):
        low = pl.multiple_of(order_ref[k] * width, LANES)
        source = w_ref.at[:, pl.ds(low, width)]
        copies.append(pltpu.make_async_copy(source, piece_of(k, outs), sems.at[k]))
        copies[-1].start()
    for copy in copies:
        copy.wait()


def cut_down_kernel(order_ref, w_ref, *refs):
    outs, cut, sems = refs[:4], refs[4], refs[5]
    run = w_ref.shape[1] // 64
    for part in range(8):
        for group in range(8):
            low = (group * 8 + part) * run
            cut[part, :, group * run : (group + 1) * run] = w_ref[:, low : low + run]
    copies = []
    for k in range(8):
        source = cut.at[order_ref[k]]
        copies.append(pltpu.make_async_copy(source, piece_of(k, outs), sems.at[k]))
        copies[-1].start()
    for copy in copies:
        copy.wait()


def join_kernel(plan, *refs):
    out, sems = refs[-2:]
    copies = []
    for n, (which, row) in enumerate(plan):
        copies.append(pltpu.make_async_copy(refs[which].at[row], out.at[n], sems.at[n]))
        copies[-1].start()
    for copy in copies:
        copy.wait()


def fetch(order_ref, held, first, second, third, whole, sems):
    rows = held.shape[1]
    copies = []
    for k in range(8):
        one, two, three = k >> 2, k >> 1 & 1, k & 1
        if three:
            source = third.at[one * 2 + two]
        elif two:
            source = second.at[one * 2]
        elif one:
            source = first.at[0]
        else:
            source = held.at[0]
        low = pl.multiple_of(order_ref[k] * rows, 16)
        copies.append(pltpu.make_async_copy(source, whole.at[pl.ds(low, rows), :], sems.at[k]))
        copies[-1].start()
    return copies


def up_kernel(order_ref, x_ref, w0, w1, w2, w3, out_ref, rows, picked, whole, sems):
    copies = fetch(order_ref, w0, w1, w2, w3, whole, sems)
    rows[...] = x_ref[...].astype(F32).reshape(64 * SLOTS, LANES)
    picked[320:] = jnp.zeros((64, picked.shape[1]), BF16)
    for i in range(5):
        for tile in range(6):
            piece = rows[pl.ds(i * 6 + tile, 64, stride=SLOTS), :]
            picked[i * 64 : i * 64 + 64, tile * LANES : (tile + 1) * LANES] = piece.astype(BF16)
    for copy in copies:
        copy.wait()
    out_ref[...] = lax.dot_general(
        whole[...], picked[...], (((1,), (1,)), ((), ())), preferred_element_type=F32
    ).astype(BF16)


def act_kernel(in_ref, out_ref):
    up = in_ref[0].astype(F32)
    for part in range(1, 8):
        up = up + in_ref[part].astype(F32)
    out_ref[...] = (up / (1.0 + jnp.exp(-up))).astype(BF16)


def down_kernel(order_ref, h_ref, w0, w1, w2, w3, out_ref, rows, whole, sems):
    copies = fetch(order_ref, w0, w1, w2, w3, whole, sems)
    for slot in (30, 31):
        rows[pl.ds(slot, 64, stride=SLOTS), :] = jnp.zeros((64, LANES), F32)
    for copy in copies:
        copy.wait()
    y = lax.dot_general(
        h_ref[...], whole[...], (((0,), (1,)), ((), ())), preferred_element_type=F32
    )
    for i in range(5):
        for tile in range(6):
            rows[pl.ds(i * 6 + tile, 64, stride=SLOTS), :] = y[
                i * 64 : i * 64 + 64, tile * LANES : (tile + 1) * LANES
            ]
    out_ref[...] = rows[...].reshape(64, SLOTS, LANES).astype(BF16)


def weigh_kernel(y_ref, row_ref, router_ref, out_ref):
    products = jnp.zeros((SLOTS, LANES), F32)
    for part in range(8):
        products = products + row_ref[part].astype(F32) * router_ref[part].astype(F32)
    one = lax.broadcasted_iota(jnp.int32, (SLOTS, SLOTS), 0) // 6
    two = lax.broadcasted_iota(jnp.int32, (SLOTS, SLOTS), 1) // 6
    alike = jnp.where(one == two, 1.0, 0.0)
    sums = jnp.dot(
        alike, products, preferred_element_type=F32, precision=lax.Precision.HIGHEST
    )
    gate = jax.nn.sigmoid(jnp.sum(sums, axis=-1, keepdims=True))
    for group in range(8):
        total = y_ref[group * 8].astype(F32)
        for part in range(1, 8):
            total = total + y_ref[group * 8 + part].astype(F32)
        out_ref[group] = (total * gate).astype(BF16)


def add_kernel(attn_ref, y_ref, sel_ref, out_ref, rows, weighted):
    length = attn_ref.shape[0]
    rows[...] = y_ref[...].astype(F32).reshape(8 * SLOTS, LANES)
    weighted[...] = jnp.zeros_like(weighted)
    for i in range(5):
        for tile in range(6):
            weighted[i * 8 : i * 8 + 8, tile * LANES : (tile + 1) * LANES] = rows[
                pl.ds(i * 6 + tile, 8, stride=SLOTS), :
            ]
    place = lax.broadcasted_iota(jnp.int32, (length, LANES), 0)
    chosen = jnp.where(place == sel_ref[...], 1.0, 0.0).astype(BF16)
    added = jnp.dot(chosen, weighted[...].astype(BF16), preferred_element_type=F32)
    out_ref[...] = (attn_ref[...].astype(F32) + added).astype(BF16)


def shape(dims, dtype=BF16):
    return jax.ShapeDtypeStruct(dims, dtype)


def neighbour(place, mask):
    code = place ^ (place >> 1 & 1)
    code = code ^ mask
    return code ^ (code >> 1 & 1)


def swap_with(array, mask):
    return lax.ppermute(array, "c", [(c, neighbour(c, mask)) for c in range(8)])


def order_of(masks):
    place = lax.axis_index("c").astype(jnp.int32)
    masks = [
        (k >> 2) * masks[0] + (k >> 1 & 1) * masks[1] + (k & 1) * masks[2] for k in range(8)
    ]
    return neighbour(place, jnp.asarray(masks, jnp.int32))


UP_MASKS = (1, 2, 4)
DOWN_MASKS = (4, 1, 2)


def join(plan, *arrays):
    return call(
        functools.partial(join_kernel, plan),
        shape((len(plan), *arrays[0].shape[1:])),
        *arrays,
        scratch=[pltpu.SemaphoreType.DMA((len(plan),))],
        spaces=([HBM] * len(arrays), HBM),
        name="join",
    )


def second_half(held, first):
    return join([(0, 0), (0, 1), (1, 2), (1, 3)], held, first)


def third_half(held, first, second):
    return join([(0, 0), (2, 1), (1, 1), (2, 3)], held, first, second)


def body(queries, keys, values, selections, router, w_up, w_down):
    length, width = queries.shape
    parts = lax.axis_size("p")
    seq = ("r", "c")
    units = w_up.shape[1]
    columns = w_down.shape[1]
    group = w_down.shape[2] // parts
    sel = selections[0].T.reshape(-1)
    sel_column = sel[:, None]
    sel_row = jnp.pad(sel, (0, LANES - sel.shape[0]), constant_values=-1)[None]
    router_rows = jnp.tile(router.reshape(parts, 6, LANES), (1, 5, 1))
    router_rows = jnp.pad(router_rows, ((0, 0), (0, SLOTS - 30), (0, 0)))

    state = call(
        state_kernel,
        shape((64, 16, LANES)),
        keys,
        values,
        scratch=[pltpu.VMEM((width, width), F32), pltpu.VMEM((64 * 16, LANES), F32)],
        name="state",
    )
    up_order, down_order = order_of(UP_MASKS), order_of(DOWN_MASKS)
    w_up, w_down, state = lax.optimization_barrier((w_up, w_down, state))
    chunks = lax.all_to_all(state, seq, 0, 0, tiled=True)
    inner = call(inner_kernel, shape((length, width), F32), queries, keys, values, name="inner")
    up_0 = call(
        cut_up_kernel,
        [shape((n, units, width)) for n in (4, 2, 1, 1)],
        up_order,
        w_up[0],
        scratch=[pltpu.SemaphoreType.DMA((8,))],
        spaces=([SMEM, HBM], [HBM] * 4),
        name="cut_up",
    )
    up_1 = swap_with(up_0[0], UP_MASKS[0])
    down_0 = call(
        cut_down_kernel,
        [shape((n, columns, group)) for n in (4, 2, 1, 1)],
        down_order,
        w_down[0],
        scratch=[pltpu.VMEM((8, columns, group), BF16), pltpu.SemaphoreType.DMA((8,))],
        spaces=([SMEM, VMEM], [HBM] * 4),
        name="cut_down",
    )
    chunks, inner, up_0, up_1, down_0 = lax.optimization_barrier(
        (chunks, inner, up_0, up_1, down_0)
    )
    before = call(prefix_kernel, shape((64, 16, LANES)), chunks, name="prefix")
    before, up_0, up_1, down_0 = lax.optimization_barrier((before, up_0, up_1, down_0))
    before = lax.all_to_all(before, seq, 0, 0, tiled=True)
    up_2 = swap_with(second_half(up_0[1], up_1), UP_MASKS[1])
    down_1 = swap_with(down_0[0], DOWN_MASKS[0])
    before, up_0, up_1, up_2, down_0, down_1 = lax.optimization_barrier(
        (before, up_0, up_1, up_2, down_0, down_1)
    )
    attn, pay = call(
        attn_kernel,
        (shape((length, width)), shape((8, SLOTS, LANES))),
        queries,
        inner,
        before,
        sel_column,
        scratch=[
            pltpu.VMEM((64 * 16, LANES), F32),
            pltpu.VMEM((width, width), BF16),
            pltpu.VMEM((length, width), F32),
            pltpu.VMEM((8 * SLOTS, LANES), F32),
        ],
        name="attn",
    )
    pay, up_0, up_1, up_2, down_0, down_1 = lax.optimization_barrier(
        (pay, up_0, up_1, up_2, down_0, down_1)
    )
    whole_rows = lax.all_to_all(pay, "p", 0, 0, tiled=True)
    up_3 = swap_with(third_half(up_0[2], up_1, up_2), UP_MASKS[2])
    down_2 = swap_with(second_half(down_0[1], down_1), DOWN_MASKS[1])
    near_rows = lax.all_to_all(whole_rows, "c", 0, 0, tiled=True)
    near_rows, up_3, down_0, down_1, down_2 = lax.optimization_barrier(
        (near_rows, up_3, down_0, down_1, down_2)
    )
    down_3 = swap_with(third_half(down_0[2], down_1, down_2), DOWN_MASKS[2])
    arrived = lax.all_gather(near_rows, "r", axis=0, tiled=True)
    arrived, down_3 = lax.optimization_barrier((arrived, down_3))
    partial = call(
        up_kernel,
        shape((8 * units, 384)),
        up_order,
        arrived,
        up_0[3],
        up_1,
        up_2,
        up_3,
        scratch=[
            pltpu.VMEM((64 * SLOTS, LANES), F32),
            pltpu.VMEM((384, width), BF16),
            pltpu.VMEM((8 * units, width), BF16),
            pltpu.SemaphoreType.DMA((8,)),
        ],
        spaces=([SMEM, VMEM] + [HBM] * 4, VMEM),
        name="up",
    )
    sums = lax.all_to_all(partial.reshape(8, units, 384), "c", 0, 0, tiled=True)
    act = call(act_kernel, shape((units, 384)), sums, name="act")
    act = lax.all_gather(act, "r", axis=0, tiled=True)
    out = call(
        down_kernel,
        shape((64, SLOTS, LANES)),
        down_order,
        act,
        down_0[3],
        down_1,
        down_2,
        down_3,
        scratch=[
            pltpu.VMEM((64 * SLOTS, LANES), F32),
            pltpu.VMEM((8 * columns, group), BF16),
            pltpu.SemaphoreType.DMA((8,)),
        ],
        spaces=([SMEM, VMEM] + [HBM] * 4, VMEM),
        name="down",
    )
    back = lax.all_to_all(out, seq, 0, 0, tiled=True)
    weighted = call(
        weigh_kernel, shape((8, SLOTS, LANES)), back, whole_rows, router_rows, name="weigh"
    )
    weighted = lax.all_to_all(weighted, "p", 0, 0, tiled=True)
    return call(
        add_kernel,
        shape((length, width)),
        attn,
        weighted,
        sel_row,
        scratch=[pltpu.VMEM((8 * SLOTS, LANES), F32), pltpu.VMEM((LANES, width), F32)],
        name="add",
    )


def solution(mesh):
    parts = mesh.devices.shape[1]
    split = Mesh(mesh.devices.reshape(-1, parts, parts), ("r", "c", "p"))
    seq = ("r", "c")
    placed = (
        P(seq, "p"),
        P(seq, "p"),
        P(seq, "p"),
        P(seq, None, None),
        P(None, "p"),
        P("p", seq, None),
        P("p", seq, None),
    )
    return jax.shard_map(
        body, mesh=split, in_specs=placed, out_specs=P(seq, "p"), check_vma=False
    )
```

```python
import jax
import jax.numpy as jnp
from jax import lax
from jax.experimental import pallas as pl
from jax.experimental.pallas import tpu as pltpu
from jax.sharding import Mesh, PartitionSpec as P

HEAD = 96
LANES = 128
SLOTS = 32
INTERPRET = False
BF16 = jnp.bfloat16
F32 = jnp.float32


HBM = pltpu.HBM


def call(kernel, out, *args, scratch=(), spaces=None, name=None):
    specs = {}
    if spaces:
        ins, outs = spaces
        specs["in_specs"] = [pl.BlockSpec(memory_space=space) for space in ins]
        specs["out_specs"] = (
            [pl.BlockSpec(memory_space=space) for space in outs]
            if isinstance(outs, list)
            else pl.BlockSpec(memory_space=outs)
        )
    return pl.pallas_call(
        kernel,
        out_shape=out,
        scratch_shapes=list(scratch),
        compiler_params=pltpu.CompilerParams(vmem_limit_bytes=16 * 2**20),
        interpret=INTERPRET,
        name=name,
        **specs,
    )(*args)


def tile_heads(tile):
    first = tile * LANES // HEAD
    return first, (first + 1) * HEAD - tile * LANES


def head_window(head):
    first, last = head * HEAD // LANES, (head * HEAD + HEAD - 1) // LANES
    return first * LANES, (last + 1) * LANES, head * HEAD - first * LANES


def chunk_rows(tile, third):
    upper, kind = divmod(tile, 3)
    return upper * 32 * 16 + kind * 3 + third


def state_kernel(k_ref, v_ref, out_ref, grand, rows):
    grand[...] = lax.dot_general(
        k_ref[...], v_ref[...], (((0,), (0,)), ((), ())), preferred_element_type=F32
    )
    rows[...] = jnp.zeros_like(rows)
    lane = lax.broadcasted_iota(jnp.int32, (HEAD, LANES), 1)
    for tile in range(6):
        head, split = tile_heads(tile)
        at = slice(tile * LANES, (tile + 1) * LANES)
        one = grand[head * HEAD : (head + 1) * HEAD, at]
        two = grand[(head + 1) * HEAD : (head + 2) * HEAD, at]
        block = jnp.where(lane < split, one, two)
        for third in range(3):
            rows[pl.ds(chunk_rows(tile, third), 32, stride=16), :] = block[third * 32 : third * 32 + 32]
    out_ref[...] = rows[...].reshape(64, 16, LANES).astype(BF16)


def prefix_kernel(in_ref, out_ref):
    total = jnp.zeros((16, LANES), F32)
    for block in range(in_ref.shape[0]):
        out_ref[block] = total.astype(BF16)
        total = total + in_ref[block].astype(F32)


def inner_kernel(q_ref, k_ref, v_ref, out_ref):
    length = q_ref.shape[0]
    out_ref[...] = jnp.zeros_like(out_ref)
    below = lax.broadcasted_iota(jnp.int32, (length, length), 0) >= lax.broadcasted_iota(
        jnp.int32, (length, length), 1
    )
    for head in range(8):
        start, stop, low = head_window(head)
        lane = lax.broadcasted_iota(jnp.int32, (1, stop - start), 1)
        mine = (lane >= low) & (lane < low + HEAD)
        q = q_ref[:, start:stop] * mine.astype(F32).astype(BF16)
        scores = lax.dot_general(
            q, k_ref[:, start:stop], (((1,), (1,)), ((), ())), preferred_element_type=F32
        )
        scores = jnp.where(below, scores, 0.0).astype(BF16)
        mixed = jnp.dot(scores, v_ref[:, start:stop], preferred_element_type=F32)
        out_ref[:, start:stop] = jnp.where(mine, mixed, out_ref[:, start:stop])


def attn_kernel(q_ref, inner_ref, p_ref, sel_ref, attn_ref, pay_ref, rows, wide, normed, picks):
    length = q_ref.shape[0]
    rows[...] = p_ref[...].astype(F32).reshape(64 * 16, LANES)
    wide[...] = jnp.zeros_like(wide)
    lane = lax.broadcasted_iota(jnp.int32, (32, LANES), 1)
    for tile in range(6):
        head, split = tile_heads(tile)
        at = slice(tile * LANES, (tile + 1) * LANES)
        for third in range(3):
            block = rows[pl.ds(chunk_rows(tile, third), 32, stride=16), :]
            low = head * HEAD + third * 32
            wide[low : low + 32, at] = jnp.where(lane < split, block, 0.0).astype(BF16)
            low = low + HEAD
            wide[low : low + 32, at] = jnp.where(lane < split, 0.0, block).astype(BF16)
    normed[...] = inner_ref[...] + jnp.dot(q_ref[...], wide[...], preferred_element_type=F32)
    for head in range(8):
        start, stop, low = head_window(head)
        lane = lax.broadcasted_iota(jnp.int32, (1, stop - start), 1)
        mine = (lane >= low) & (lane < low + HEAD)
        mixed = normed[:, start:stop]
        power = jnp.sum(jnp.where(mine, mixed * mixed, 0.0), axis=-1, keepdims=True) / HEAD
        normed[:, start:stop] = jnp.where(mine, mixed * lax.rsqrt(power + 1e-06), mixed)
    attn = normed[...].astype(BF16)
    attn_ref[...] = attn
    place = lax.broadcasted_iota(jnp.int32, (40, length), 1)
    chosen = jnp.where(place == sel_ref[...], 1.0, 0.0).astype(BF16)
    picked = jnp.dot(chosen, attn, preferred_element_type=F32)
    picks[...] = jnp.zeros_like(picks)
    for i in range(5):
        for tile in range(6):
            picks[pl.ds(i * 6 + tile, 8, stride=SLOTS), :] = picked[
                i * 8 : i * 8 + 8, tile * LANES : (tile + 1) * LANES
            ]
    pay_ref[...] = picks[...].reshape(8, SLOTS, LANES).astype(BF16)


def cut_up_kernel(w_ref, out_ref, sems):
    parts, width = out_ref.shape[0], out_ref.shape[2]
    copies = []
    for part in range(parts):
        source = w_ref.at[:, part * width : (part + 1) * width]
        copies.append(pltpu.make_async_copy(source, out_ref.at[part], sems.at[part]))
        copies[-1].start()
    for copy in copies:
        copy.wait()


def cut_down_kernel(w_ref, out_ref):
    run = w_ref.shape[1] // 64
    for part in range(8):
        for group in range(8):
            low = (group * 8 + part) * run
            out_ref[part, :, group * run : (group + 1) * run] = w_ref[:, low : low + run]


def near_kernel(place_ref, row_ref, out_ref, rows):
    for block in range(4):
        for part in range(2):
            low = (block * 2 + part) * 30
            piece = row_ref[block * 8 + 2 * place_ref[0] + part].astype(F32)
            rows[low : low + 30] = piece[:30]
    out_ref[...] = rows[...].astype(BF16)


def up_kernel(x_ref, w_ref, out_ref, rows, picked):
    rows[...] = x_ref[...].astype(F32)
    picked[320:] = jnp.zeros((64, picked.shape[1]), BF16)
    for i in range(5):
        for part in range(2):
            for tile in range(6):
                piece = rows[pl.ds(part * 30 + i * 6 + tile, 64, stride=60), :]
                low = (part * 6 + tile) * LANES
                picked[i * 64 : i * 64 + 64, low : low + LANES] = piece.astype(BF16)
    out_ref[...] = lax.dot_general(
        w_ref[...], picked[...], (((1,), (1,)), ((), ())), preferred_element_type=F32
    ).astype(BF16)


def act_kernel(in_ref, out_ref):
    up = in_ref[0].astype(F32)
    for part in range(1, in_ref.shape[0]):
        up = up + in_ref[part].astype(F32)
    out_ref[...] = (up / (1.0 + jnp.exp(-up))).astype(BF16)


def down_kernel(h_ref, w_ref, out_ref, rows):
    for slot in (30, 31):
        rows[pl.ds(slot, 64, stride=SLOTS), :] = jnp.zeros((64, LANES), F32)
    y = lax.dot_general(
        h_ref[...], w_ref[...], (((0,), (1,)), ((), ())), preferred_element_type=F32
    )
    for i in range(5):
        for tile in range(6):
            rows[pl.ds(i * 6 + tile, 64, stride=SLOTS), :] = y[
                i * 64 : i * 64 + 64, tile * LANES : (tile + 1) * LANES
            ]
    out_ref[...] = rows[...].reshape(64, SLOTS, LANES).astype(BF16)


def weigh_kernel(place_ref, y_ref, row_ref, router_ref, out_ref):
    products = jnp.zeros((SLOTS, LANES), F32)
    own = place_ref[0] * 8
    for part in range(8):
        products = products + row_ref[own + part].astype(F32) * router_ref[part].astype(F32)
    one = lax.broadcasted_iota(jnp.int32, (SLOTS, SLOTS), 0) // 6
    two = lax.broadcasted_iota(jnp.int32, (SLOTS, SLOTS), 1) // 6
    alike = jnp.where(one == two, 1.0, 0.0)
    sums = jnp.dot(
        alike, products, preferred_element_type=F32, precision=lax.Precision.HIGHEST
    )
    gate = jax.nn.sigmoid(jnp.sum(sums, axis=-1, keepdims=True))
    for group in range(8):
        total = y_ref[group * 8].astype(F32)
        for part in range(1, 8):
            total = total + y_ref[group * 8 + part].astype(F32)
        out_ref[group] = (total * gate).astype(BF16)


def add_kernel(attn_ref, y_ref, sel_ref, out_ref, rows, weighted):
    length = attn_ref.shape[0]
    rows[...] = y_ref[...].astype(F32).reshape(8 * SLOTS, LANES)
    weighted[...] = jnp.zeros_like(weighted)
    for i in range(5):
        for tile in range(6):
            weighted[i * 8 : i * 8 + 8, tile * LANES : (tile + 1) * LANES] = rows[
                pl.ds(i * 6 + tile, 8, stride=SLOTS), :
            ]
    place = lax.broadcasted_iota(jnp.int32, (length, LANES), 0)
    chosen = jnp.where(place == sel_ref[...], 1.0, 0.0).astype(BF16)
    added = jnp.dot(chosen, weighted[...].astype(BF16), preferred_element_type=F32)
    out_ref[...] = (attn_ref[...].astype(F32) + added).astype(BF16)


def shape(dims, dtype=BF16):
    return jax.ShapeDtypeStruct(dims, dtype)


def body(queries, keys, values, selections, router, w_up, w_down):
    length, width = queries.shape
    parts = lax.axis_size("p")
    seq = ("r", "l", "y")
    patch = ("l", "y")
    units = w_up.shape[1]
    quarter = w_up.shape[2] // 4
    place = lax.axis_index("y").astype(jnp.int32)
    columns = w_down.shape[1]
    group = w_down.shape[2] // parts
    sel = selections[0].T.reshape(-1)
    sel_column = sel[:, None]
    sel_row = jnp.pad(sel, (0, LANES - sel.shape[0]), constant_values=-1)[None]
    router_rows = jnp.tile(router.reshape(parts, 6, LANES), (1, 5, 1))
    router_rows = jnp.pad(router_rows, ((0, 0), (0, SLOTS - 30), (0, 0)))

    state = call(
        state_kernel,
        shape((64, 16, LANES)),
        keys,
        values,
        scratch=[pltpu.VMEM((width, width), F32), pltpu.VMEM((64 * 16, LANES), F32)],
        name="state",
    )
    w_up, w_down, state = lax.optimization_barrier((w_up, w_down, state))
    chunks = lax.all_to_all(state, seq, 0, 0, tiled=True)
    inner = call(inner_kernel, shape((length, width), F32), queries, keys, values, name="inner")
    up_cut = call(
        cut_up_kernel,
        shape((4, units, quarter)),
        w_up[0],
        scratch=[pltpu.SemaphoreType.DMA((4,))],
        spaces=([HBM], HBM),
        name="cut_up",
    )
    chunks, inner, up_cut = lax.optimization_barrier((chunks, inner, up_cut))
    before = call(prefix_kernel, shape((64, 16, LANES)), chunks, name="prefix")
    before, w_down = lax.optimization_barrier((before, w_down))
    before = lax.all_to_all(before, seq, 0, 0, tiled=True)
    down_cut = call(cut_down_kernel, shape((8, columns, group)), w_down[0], name="cut_down")
    before, down_cut = lax.optimization_barrier((before, down_cut))
    attn, pay = call(
        attn_kernel,
        (shape((length, width)), shape((8, SLOTS, LANES))),
        queries,
        inner,
        before,
        sel_column,
        scratch=[
            pltpu.VMEM((64 * 16, LANES), F32),
            pltpu.VMEM((width, width), BF16),
            pltpu.VMEM((length, width), F32),
            pltpu.VMEM((8 * SLOTS, LANES), F32),
        ],
        name="attn",
    )
    whole_rows = lax.all_to_all(jnp.tile(pay, (4, 1, 1)), ("y", "p"), 0, 0, tiled=True)
    near_rows = call(
        near_kernel,
        shape((240, LANES)),
        place.reshape(1),
        whole_rows,
        scratch=[pltpu.VMEM((240, LANES), F32)],
        spaces=([pltpu.SMEM, pltpu.VMEM], pltpu.VMEM),
        name="near",
    )
    near_rows, up_cut = lax.optimization_barrier((near_rows, up_cut))
    up_mine = lax.all_to_all(up_cut, "y", 0, 0, tiled=True).reshape(4 * units, quarter)
    arrived = lax.all_gather(near_rows, ("r", "l"), axis=0, tiled=True)
    partial = call(
        up_kernel,
        shape((4 * units, 384)),
        arrived,
        up_mine,
        scratch=[pltpu.VMEM((64 * 60, LANES), F32), pltpu.VMEM((384, quarter), BF16)],
        name="up",
    )
    sums = lax.all_to_all(partial.reshape(4, units, 384), "y", 0, 0, tiled=True)
    act = call(act_kernel, shape((units, 384)), sums, name="act")
    act, down_cut = lax.optimization_barrier((act, down_cut))
    down_mine = lax.all_to_all(down_cut, patch, 0, 0, tiled=True).reshape(8 * columns, group)
    act = lax.all_gather(act, "r", axis=0, tiled=True)
    out = call(
        down_kernel,
        shape((64, SLOTS, LANES)),
        act,
        down_mine,
        scratch=[pltpu.VMEM((64 * SLOTS, LANES), F32)],
        name="down",
    )
    back = lax.all_to_all(out, seq, 0, 0, tiled=True)
    weighted = call(
        weigh_kernel,
        shape((8, SLOTS, LANES)),
        place.reshape(1),
        back,
        whole_rows,
        router_rows,
        spaces=([pltpu.SMEM] + [pltpu.VMEM] * 3, pltpu.VMEM),
        name="weigh",
    )
    weighted = lax.all_to_all(weighted, "p", 0, 0, tiled=True)
    return call(
        add_kernel,
        shape((length, width)),
        attn,
        weighted,
        sel_row,
        scratch=[pltpu.VMEM((8 * SLOTS, LANES), F32), pltpu.VMEM((LANES, width), F32)],
        name="add",
    )


def solution(mesh):
    split = Mesh(mesh.devices.reshape(8, 2, 4, 8), ("r", "l", "y", "p"))
    seq = ("r", "l", "y")
    placed = (
        P(seq, "p"),
        P(seq, "p"),
        P(seq, "p"),
        P(seq, None, None),
        P(None, "p"),
        P("p", seq, None),
        P("p", seq, None),
    )
    return jax.shard_map(
        body, mesh=split, in_specs=placed, out_specs=P(seq, "p"), check_vma=False
    )
```

```python
import jax
import jax.numpy as jnp
from jax import lax
from jax.experimental import pallas as pl
from jax.experimental.pallas import tpu as pltpu
from jax.sharding import Mesh, PartitionSpec as P

HEAD = 96
LANES = 128
SLOTS = 32
INTERPRET = False
BF16 = jnp.bfloat16
F32 = jnp.float32


HBM = pltpu.HBM


def call(kernel, out, *args, scratch=(), spaces=None, name=None):
    specs = {}
    if spaces:
        ins, outs = spaces
        specs["in_specs"] = [pl.BlockSpec(memory_space=space) for space in ins]
        specs["out_specs"] = (
            [pl.BlockSpec(memory_space=space) for space in outs]
            if isinstance(outs, list)
            else pl.BlockSpec(memory_space=outs)
        )
    return pl.pallas_call(
        kernel,
        out_shape=out,
        scratch_shapes=list(scratch),
        compiler_params=pltpu.CompilerParams(vmem_limit_bytes=16 * 2**20),
        interpret=INTERPRET,
        name=name,
        **specs,
    )(*args)


def tile_heads(tile):
    first = tile * LANES // HEAD
    return first, (first + 1) * HEAD - tile * LANES


def head_window(head):
    first, last = head * HEAD // LANES, (head * HEAD + HEAD - 1) // LANES
    return first * LANES, (last + 1) * LANES, head * HEAD - first * LANES


def chunk_rows(tile, third):
    upper, kind = divmod(tile, 3)
    return upper * 32 * 16 + kind * 3 + third


def state_kernel(k_ref, v_ref, out_ref, grand, rows):
    grand[...] = lax.dot_general(
        k_ref[...], v_ref[...], (((0,), (0,)), ((), ())), preferred_element_type=F32
    )
    rows[...] = jnp.zeros_like(rows)
    lane = lax.broadcasted_iota(jnp.int32, (HEAD, LANES), 1)
    for tile in range(6):
        head, split = tile_heads(tile)
        at = slice(tile * LANES, (tile + 1) * LANES)
        one = grand[head * HEAD : (head + 1) * HEAD, at]
        two = grand[(head + 1) * HEAD : (head + 2) * HEAD, at]
        block = jnp.where(lane < split, one, two)
        for third in range(3):
            rows[pl.ds(chunk_rows(tile, third), 32, stride=16), :] = block[third * 32 : third * 32 + 32]
    out_ref[...] = rows[...].reshape(64, 16, LANES).astype(BF16)


def prefix_kernel(in_ref, out_ref):
    total = jnp.zeros((16, LANES), F32)
    for block in range(in_ref.shape[0]):
        out_ref[block] = total.astype(BF16)
        total = total + in_ref[block].astype(F32)


def inner_kernel(q_ref, k_ref, v_ref, out_ref):
    length = q_ref.shape[0]
    out_ref[...] = jnp.zeros_like(out_ref)
    below = lax.broadcasted_iota(jnp.int32, (length, length), 0) >= lax.broadcasted_iota(
        jnp.int32, (length, length), 1
    )
    for head in range(8):
        start, stop, low = head_window(head)
        lane = lax.broadcasted_iota(jnp.int32, (1, stop - start), 1)
        mine = (lane >= low) & (lane < low + HEAD)
        q = q_ref[:, start:stop] * mine.astype(F32).astype(BF16)
        scores = lax.dot_general(
            q, k_ref[:, start:stop], (((1,), (1,)), ((), ())), preferred_element_type=F32
        )
        scores = jnp.where(below, scores, 0.0).astype(BF16)
        mixed = jnp.dot(scores, v_ref[:, start:stop], preferred_element_type=F32)
        out_ref[:, start:stop] = jnp.where(mine, mixed, out_ref[:, start:stop])


def attn_kernel(q_ref, inner_ref, p_ref, sel_ref, attn_ref, pay_ref, rows, wide, normed, picks):
    length = q_ref.shape[0]
    rows[...] = p_ref[...].astype(F32).reshape(64 * 16, LANES)
    wide[...] = jnp.zeros_like(wide)
    lane = lax.broadcasted_iota(jnp.int32, (32, LANES), 1)
    for tile in range(6):
        head, split = tile_heads(tile)
        at = slice(tile * LANES, (tile + 1) * LANES)
        for third in range(3):
            block = rows[pl.ds(chunk_rows(tile, third), 32, stride=16), :]
            low = head * HEAD + third * 32
            wide[low : low + 32, at] = jnp.where(lane < split, block, 0.0).astype(BF16)
            low = low + HEAD
            wide[low : low + 32, at] = jnp.where(lane < split, 0.0, block).astype(BF16)
    normed[...] = inner_ref[...] + jnp.dot(q_ref[...], wide[...], preferred_element_type=F32)
    for head in range(8):
        start, stop, low = head_window(head)
        lane = lax.broadcasted_iota(jnp.int32, (1, stop - start), 1)
        mine = (lane >= low) & (lane < low + HEAD)
        mixed = normed[:, start:stop]
        power = jnp.sum(jnp.where(mine, mixed * mixed, 0.0), axis=-1, keepdims=True) / HEAD
        normed[:, start:stop] = jnp.where(mine, mixed * lax.rsqrt(power + 1e-06), mixed)
    attn = normed[...].astype(BF16)
    attn_ref[...] = attn
    place = lax.broadcasted_iota(jnp.int32, (40, length), 1)
    chosen = jnp.where(place == sel_ref[...], 1.0, 0.0).astype(BF16)
    picked = jnp.dot(chosen, attn, preferred_element_type=F32)
    picks[...] = jnp.zeros_like(picks)
    for i in range(5):
        for tile in range(6):
            picks[pl.ds(i * 6 + tile, 8, stride=SLOTS), :] = picked[
                i * 8 : i * 8 + 8, tile * LANES : (tile + 1) * LANES
            ]
    pay_ref[...] = picks[...].reshape(8, SLOTS, LANES).astype(BF16)


def cut_up_kernel(w_ref, out_ref, sems):
    parts, width = out_ref.shape[0], out_ref.shape[2]
    copies = []
    for part in range(parts):
        source = w_ref.at[:, part * width : (part + 1) * width]
        copies.append(pltpu.make_async_copy(source, out_ref.at[part], sems.at[part]))
        copies[-1].start()
    for copy in copies:
        copy.wait()


def cut_down_kernel(place_ref, w_ref, keep_ref, one_ref, two_ref, cut, sems):
    run = w_ref.shape[1] // 64
    for part in range(8):
        for group in range(8):
            low = (group * 8 + part) * run
            cut[part, :, group * run : (group + 1) * run] = w_ref[:, low : low + run]
    own = place_ref[0] * 4
    other = 4 - own
    copies = []
    for n in range(4):
        away = (one_ref, two_ref)[n // 2].at[n % 2]
        copies.append(pltpu.make_async_copy(cut.at[own + n], keep_ref.at[n], sems.at[n]))
        copies.append(pltpu.make_async_copy(cut.at[other + n], away, sems.at[4 + n]))
    for copy in copies:
        copy.start()
    for copy in copies:
        copy.wait()


def join_kernel(place_ref, keep_ref, one_ref, two_ref, out_ref, sems):
    own = place_ref[0]
    copies = []
    for n in range(4):
        away = (one_ref, two_ref)[n // 2].at[n % 2]
        copies.append(pltpu.make_async_copy(keep_ref.at[n], out_ref.at[n, own], sems.at[n]))
        copies.append(pltpu.make_async_copy(away, out_ref.at[n, 1 - own], sems.at[4 + n]))
    for copy in copies:
        copy.start()
    for copy in copies:
        copy.wait()


def near_kernel(place_ref, row_ref, out_ref, rows):
    for block in range(4):
        for part in range(2):
            low = (block * 2 + part) * 30
            piece = row_ref[block * 8 + 2 * place_ref[0] + part].astype(F32)
            rows[low : low + 30] = piece[:30]
    out_ref[...] = rows[...].astype(BF16)


def up_kernel(x_ref, w_ref, out_ref, rows, picked):
    rows[...] = x_ref[...].astype(F32)
    picked[320:] = jnp.zeros((64, picked.shape[1]), BF16)
    for i in range(5):
        for part in range(2):
            for tile in range(6):
                piece = rows[pl.ds(part * 30 + i * 6 + tile, 64, stride=60), :]
                low = (part * 6 + tile) * LANES
                picked[i * 64 : i * 64 + 64, low : low + LANES] = piece.astype(BF16)
    out_ref[...] = lax.dot_general(
        w_ref[...], picked[...], (((1,), (1,)), ((), ())), preferred_element_type=F32
    ).astype(BF16)


def act_kernel(in_ref, out_ref):
    up = in_ref[0].astype(F32)
    for part in range(1, in_ref.shape[0]):
        up = up + in_ref[part].astype(F32)
    out_ref[...] = (up / (1.0 + jnp.exp(-up))).astype(BF16)


def down_kernel(h_ref, w_ref, out_ref, rows, whole):
    columns = w_ref.shape[2]
    for y in range(4):
        for pair in range(2):
            low = (pair * 4 + y) * columns
            whole[low : low + columns] = w_ref[y, pair]
    for slot in (30, 31):
        rows[pl.ds(slot, 64, stride=SLOTS), :] = jnp.zeros((64, LANES), F32)
    out = lax.dot_general(
        h_ref[...], whole[...], (((0,), (1,)), ((), ())), preferred_element_type=F32
    )
    for i in range(5):
        for tile in range(6):
            rows[pl.ds(i * 6 + tile, 64, stride=SLOTS), :] = out[
                i * 64 : i * 64 + 64, tile * LANES : (tile + 1) * LANES
            ]
    for block in range(64):
        z, y = divmod(block, 4)
        out_ref[y * 16 + z] = rows[block * SLOTS : (block + 1) * SLOTS].astype(BF16)


def sum_kernel(in_ref, out_ref):
    total = in_ref[0:16].astype(F32)
    for part in range(1, 4):
        total = total + in_ref[part * 16 : part * 16 + 16].astype(F32)
    out_ref[...] = total.astype(BF16)


def weigh_kernel(place_ref, y_ref, row_ref, router_ref, out_ref):
    products = jnp.zeros((SLOTS, LANES), F32)
    own = place_ref[0] * 8
    for part in range(8):
        products = products + row_ref[own + part].astype(F32) * router_ref[part].astype(F32)
    one = lax.broadcasted_iota(jnp.int32, (SLOTS, SLOTS), 0) // 6
    two = lax.broadcasted_iota(jnp.int32, (SLOTS, SLOTS), 1) // 6
    alike = jnp.where(one == two, 1.0, 0.0)
    sums = jnp.dot(
        alike, products, preferred_element_type=F32, precision=lax.Precision.HIGHEST
    )
    gate = jax.nn.sigmoid(jnp.sum(sums, axis=-1, keepdims=True))
    for group in range(8):
        total = y_ref[group * 2].astype(F32) + y_ref[group * 2 + 1].astype(F32)
        out_ref[group] = (total * gate).astype(BF16)


def add_kernel(attn_ref, y_ref, sel_ref, out_ref, rows, weighted):
    length = attn_ref.shape[0]
    rows[...] = y_ref[...].astype(F32).reshape(8 * SLOTS, LANES)
    weighted[...] = jnp.zeros_like(weighted)
    for i in range(5):
        for tile in range(6):
            weighted[i * 8 : i * 8 + 8, tile * LANES : (tile + 1) * LANES] = rows[
                pl.ds(i * 6 + tile, 8, stride=SLOTS), :
            ]
    place = lax.broadcasted_iota(jnp.int32, (length, LANES), 0)
    chosen = jnp.where(place == sel_ref[...], 1.0, 0.0).astype(BF16)
    added = jnp.dot(chosen, weighted[...].astype(BF16), preferred_element_type=F32)
    out_ref[...] = (attn_ref[...].astype(F32) + added).astype(BF16)


def shape(dims, dtype=BF16):
    return jax.ShapeDtypeStruct(dims, dtype)


def body(queries, keys, values, selections, router, w_up, w_down):
    length, width = queries.shape
    parts = lax.axis_size("p")
    seq = ("r", "l", "y")
    units = w_up.shape[1]
    quarter = w_up.shape[2] // 4
    place = lax.axis_index("y").astype(jnp.int32)
    columns = w_down.shape[1]
    group = w_down.shape[2] // parts
    sel = selections[0].T.reshape(-1)
    sel_column = sel[:, None]
    sel_row = jnp.pad(sel, (0, LANES - sel.shape[0]), constant_values=-1)[None]
    router_rows = jnp.tile(router.reshape(parts, 6, LANES), (1, 5, 1))
    router_rows = jnp.pad(router_rows, ((0, 0), (0, SLOTS - 30), (0, 0)))

    state = call(
        state_kernel,
        shape((64, 16, LANES)),
        keys,
        values,
        scratch=[pltpu.VMEM((width, width), F32), pltpu.VMEM((64 * 16, LANES), F32)],
        name="state",
    )
    w_up, w_down, state = lax.optimization_barrier((w_up, w_down, state))
    chunks = lax.all_to_all(state, seq, 0, 0, tiled=True)
    inner = call(inner_kernel, shape((length, width), F32), queries, keys, values, name="inner")
    up_cut = call(
        cut_up_kernel,
        shape((4, units, quarter)),
        w_up[0],
        scratch=[pltpu.SemaphoreType.DMA((4,))],
        spaces=([HBM], HBM),
        name="cut_up",
    )
    pair = lax.axis_index("l").astype(jnp.int32).reshape(1)
    down_keep, down_one, down_two = call(
        cut_down_kernel,
        [shape((n, columns, group)) for n in (4, 2, 2)],
        pair,
        w_down[0],
        scratch=[pltpu.VMEM((8, columns, group), BF16), pltpu.SemaphoreType.DMA((8,))],
        spaces=([pltpu.SMEM, pltpu.VMEM], [HBM] * 3),
        name="cut_down",
    )
    down_one = lax.ppermute(down_one, "l", [(0, 1), (1, 0)])
    chunks, inner, up_cut, down_keep, down_one, down_two = lax.optimization_barrier(
        (chunks, inner, up_cut, down_keep, down_one, down_two)
    )
    before = call(prefix_kernel, shape((64, 16, LANES)), chunks, name="prefix")
    before = lax.all_to_all(before, seq, 0, 0, tiled=True)
    attn, pay = call(
        attn_kernel,
        (shape((length, width)), shape((8, SLOTS, LANES))),
        queries,
        inner,
        before,
        sel_column,
        scratch=[
            pltpu.VMEM((64 * 16, LANES), F32),
            pltpu.VMEM((width, width), BF16),
            pltpu.VMEM((length, width), F32),
            pltpu.VMEM((8 * SLOTS, LANES), F32),
        ],
        name="attn",
    )
    pay, down_two = lax.optimization_barrier((pay, down_two))
    down_two = lax.ppermute(down_two, "l", [(0, 1), (1, 0)])
    whole_rows = lax.all_to_all(jnp.tile(pay, (4, 1, 1)), ("y", "p"), 0, 0, tiled=True)
    whole_rows, down_two = lax.optimization_barrier((whole_rows, down_two))
    near_rows = call(
        near_kernel,
        shape((240, LANES)),
        place.reshape(1),
        whole_rows,
        scratch=[pltpu.VMEM((240, LANES), F32)],
        spaces=([pltpu.SMEM, pltpu.VMEM], pltpu.VMEM),
        name="near",
    )
    near_rows, up_cut = lax.optimization_barrier((near_rows, up_cut))
    up_mine = lax.all_to_all(up_cut, "y", 0, 0, tiled=True).reshape(4 * units, quarter)
    arrived = lax.all_gather(near_rows, ("r", "l"), axis=0, tiled=True)
    partial = call(
        up_kernel,
        shape((4 * units, 384)),
        arrived,
        up_mine,
        scratch=[pltpu.VMEM((64 * 60, LANES), F32), pltpu.VMEM((384, quarter), BF16)],
        name="up",
    )
    partial, down_keep = lax.optimization_barrier((partial, down_keep))
    sums = lax.all_to_all(partial.reshape(4, units, 384), "y", 0, 0, tiled=True)
    down_cut = call(
        join_kernel,
        shape((4, 2, columns, group)),
        pair,
        down_keep,
        down_one,
        down_two,
        scratch=[pltpu.SemaphoreType.DMA((8,))],
        spaces=([pltpu.SMEM] + [HBM] * 3, HBM),
        name="join",
    )
    sums, down_cut = lax.optimization_barrier((sums, down_cut))
    act = call(act_kernel, shape((units, 384)), sums, name="act")
    act, down_cut = lax.optimization_barrier((act, down_cut))
    down_mine = lax.all_to_all(down_cut, "y", 0, 0, tiled=True)
    act = lax.all_gather(act, "r", axis=0, tiled=True)
    out = call(
        down_kernel,
        shape((64, SLOTS, LANES)),
        act,
        down_mine,
        scratch=[
            pltpu.VMEM((64 * SLOTS, LANES), F32),
            pltpu.VMEM((8 * columns, group), BF16),
        ],
        name="down",
    )
    back = lax.all_to_all(out, "y", 0, 0, tiled=True)
    back = call(sum_kernel, shape((16, SLOTS, LANES)), back, name="sum")
    back = lax.all_to_all(back, ("r", "l"), 0, 0, tiled=True)
    weighted = call(
        weigh_kernel,
        shape((8, SLOTS, LANES)),
        place.reshape(1),
        back,
        whole_rows,
        router_rows,
        spaces=([pltpu.SMEM] + [pltpu.VMEM] * 3, pltpu.VMEM),
        name="weigh",
    )
    weighted = lax.all_to_all(weighted, "p", 0, 0, tiled=True)
    return call(
        add_kernel,
        shape((length, width)),
        attn,
        weighted,
        sel_row,
        scratch=[pltpu.VMEM((8 * SLOTS, LANES), F32), pltpu.VMEM((LANES, width), F32)],
        name="add",
    )


def solution(mesh):
    split = Mesh(mesh.devices.reshape(8, 2, 4, 8), ("r", "l", "y", "p"))
    seq = ("r", "l", "y")
    placed = (
        P(seq, "p"),
        P(seq, "p"),
        P(seq, "p"),
        P(seq, None, None),
        P(None, "p"),
        P("p", seq, None),
        P("p", seq, None),
    )
    return jax.shard_map(
        body, mesh=split, in_specs=placed, out_specs=P(seq, "p"), check_vma=False
    )
```

```python
import jax
import jax.numpy as jnp
from jax import lax
from jax.experimental import pallas as pl
from jax.experimental.pallas import tpu as pltpu
from jax.sharding import Mesh, PartitionSpec as P

HEAD = 96
LANES = 128
SLOTS = 32
INTERPRET = False
BF16 = jnp.bfloat16
F32 = jnp.float32


HBM = pltpu.HBM


def call(kernel, out, *args, scratch=(), spaces=None, name=None):
    specs = {}
    if spaces:
        ins, outs = spaces
        specs["in_specs"] = [pl.BlockSpec(memory_space=space) for space in ins]
        specs["out_specs"] = (
            [pl.BlockSpec(memory_space=space) for space in outs]
            if isinstance(outs, list)
            else pl.BlockSpec(memory_space=outs)
        )
    return pl.pallas_call(
        kernel,
        out_shape=out,
        scratch_shapes=list(scratch),
        compiler_params=pltpu.CompilerParams(vmem_limit_bytes=16 * 2**20),
        interpret=INTERPRET,
        name=name,
        **specs,
    )(*args)


def tile_heads(tile):
    first = tile * LANES // HEAD
    return first, (first + 1) * HEAD - tile * LANES


def head_window(head):
    first, last = head * HEAD // LANES, (head * HEAD + HEAD - 1) // LANES
    return first * LANES, (last + 1) * LANES, head * HEAD - first * LANES


def state_kernel(k_ref, v_ref, out_ref, grand, rows):
    grand[...] = lax.dot_general(
        k_ref[...], v_ref[...], (((0,), (0,)), ((), ())), preferred_element_type=F32
    )
    lane = lax.broadcasted_iota(jnp.int32, (HEAD, LANES), 1)
    for tile in range(6):
        head, split = tile_heads(tile)
        at = slice(tile * LANES, (tile + 1) * LANES)
        one = grand[head * HEAD : (head + 1) * HEAD, at]
        two = grand[(head + 1) * HEAD : (head + 2) * HEAD, at]
        block = jnp.where(lane < split, one, two)
        for quarter in range(4):
            rows[quarter, tile * 24 : tile * 24 + 24] = block[quarter * 24 : quarter * 24 + 24]
    out_ref[...] = rows[...].astype(BF16)


def total_kernel(in_ref, out_ref, rows):
    total = in_ref[0].astype(F32)
    for y in range(1, 4):
        total = total + in_ref[y].astype(F32)
    rows[0:144] = total
    rows[144:152] = jnp.zeros((8, LANES), F32)
    for z in range(16):
        out_ref[z] = rows[z * 9 : z * 9 + 16].astype(BF16)


def prefix_kernel(in_ref, out_ref):
    total = jnp.zeros((16, LANES), F32)
    for z in range(16):
        out_ref[z] = total.astype(BF16)
        total = total + in_ref[z].astype(F32)


def spread_kernel(base_ref, in_ref, out_ref, rows):
    for z in range(16):
        rows[z * 9 : z * 9 + 9] = base_ref[z].astype(F32)[0:9]
    total = rows[...]
    for y in range(4):
        out_ref[y] = total.astype(BF16)
        total = total + in_ref[y].astype(F32)


def inner_kernel(q_ref, k_ref, v_ref, out_ref):
    length = q_ref.shape[0]
    out_ref[...] = jnp.zeros_like(out_ref)
    below = lax.broadcasted_iota(jnp.int32, (length, length), 0) >= lax.broadcasted_iota(
        jnp.int32, (length, length), 1
    )
    for head in range(8):
        start, stop, low = head_window(head)
        lane = lax.broadcasted_iota(jnp.int32, (1, stop - start), 1)
        mine = (lane >= low) & (lane < low + HEAD)
        q = q_ref[:, start:stop] * mine.astype(F32).astype(BF16)
        scores = lax.dot_general(
            q, k_ref[:, start:stop], (((1,), (1,)), ((), ())), preferred_element_type=F32
        )
        scores = jnp.where(below, scores, 0.0).astype(BF16)
        mixed = jnp.dot(scores, v_ref[:, start:stop], preferred_element_type=F32)
        out_ref[:, start:stop] = jnp.where(mine, mixed, out_ref[:, start:stop])


def attn_kernel(q_ref, inner_ref, p_ref, sel_ref, attn_ref, pay_ref, rows, wide, normed, picks):
    length = q_ref.shape[0]
    for quarter in range(4):
        part = p_ref[quarter].astype(F32)
        for tile in range(6):
            low = tile * HEAD + quarter * 24
            rows[low : low + 24] = part[tile * 24 : tile * 24 + 24]
    wide[...] = jnp.zeros_like(wide)
    lane = lax.broadcasted_iota(jnp.int32, (HEAD, LANES), 1)
    for tile in range(6):
        head, split = tile_heads(tile)
        at = slice(tile * LANES, (tile + 1) * LANES)
        block = rows[tile * HEAD : (tile + 1) * HEAD]
        low = head * HEAD
        wide[low : low + HEAD, at] = jnp.where(lane < split, block, 0.0).astype(BF16)
        low = low + HEAD
        wide[low : low + HEAD, at] = jnp.where(lane < split, 0.0, block).astype(BF16)
    normed[...] = inner_ref[...] + jnp.dot(q_ref[...], wide[...], preferred_element_type=F32)
    for head in range(8):
        start, stop, low = head_window(head)
        lane = lax.broadcasted_iota(jnp.int32, (1, stop - start), 1)
        mine = (lane >= low) & (lane < low + HEAD)
        mixed = normed[:, start:stop]
        power = jnp.sum(jnp.where(mine, mixed * mixed, 0.0), axis=-1, keepdims=True) / HEAD
        normed[:, start:stop] = jnp.where(mine, mixed * lax.rsqrt(power + 1e-06), mixed)
    attn = normed[...].astype(BF16)
    attn_ref[...] = attn
    place = lax.broadcasted_iota(jnp.int32, (40, length), 1)
    chosen = jnp.where(place == sel_ref[...], 1.0, 0.0).astype(BF16)
    picked = jnp.dot(chosen, attn, preferred_element_type=F32)
    picks[...] = jnp.zeros_like(picks)
    for i in range(5):
        for tile in range(6):
            picks[pl.ds(i * 6 + tile, 8, stride=SLOTS), :] = picked[
                i * 8 : i * 8 + 8, tile * LANES : (tile + 1) * LANES
            ]
    pay_ref[...] = picks[...].reshape(8, SLOTS, LANES).astype(BF16)


def cut_up_kernel(w_ref, out_ref, sems):
    parts, width = out_ref.shape[0], out_ref.shape[2]
    copies = []
    for part in range(parts):
        source = w_ref.at[:, part * width : (part + 1) * width]
        copies.append(pltpu.make_async_copy(source, out_ref.at[part], sems.at[part]))
        copies[-1].start()
    for copy in copies:
        copy.wait()


def cut_down_kernel(place_ref, w_ref, keep_ref, one_ref, two_ref, cut, sems):
    run = w_ref.shape[1] // 64
    for part in range(8):
        for group in range(8):
            low = (group * 8 + part) * run
            cut[part, :, group * run : (group + 1) * run] = w_ref[:, low : low + run]
    own = place_ref[0] * 4
    other = 4 - own
    copies = []
    for n in range(4):
        away = (one_ref, two_ref)[n // 2].at[n % 2]
        copies.append(pltpu.make_async_copy(cut.at[own + n], keep_ref.at[n], sems.at[n]))
        copies.append(pltpu.make_async_copy(cut.at[other + n], away, sems.at[4 + n]))
    for copy in copies:
        copy.start()
    for copy in copies:
        copy.wait()


def join_kernel(place_ref, keep_ref, one_ref, two_ref, out_ref, sems):
    own = place_ref[0]
    copies = []
    for n in range(4):
        away = (one_ref, two_ref)[n // 2].at[n % 2]
        copies.append(pltpu.make_async_copy(keep_ref.at[n], out_ref.at[n, own], sems.at[n]))
        copies.append(pltpu.make_async_copy(away, out_ref.at[n, 1 - own], sems.at[4 + n]))
    for copy in copies:
        copy.start()
    for copy in copies:
        copy.wait()


def near_kernel(place_ref, row_ref, out_ref, rows):
    for block in range(4):
        for part in range(2):
            low = (block * 2 + part) * 30
            piece = row_ref[block * 8 + 2 * place_ref[0] + part].astype(F32)
            rows[low : low + 30] = piece[:30]
    out_ref[...] = rows[...].astype(BF16)


def up_kernel(x_ref, w_ref, out_ref, rows, picked):
    rows[...] = x_ref[...].astype(F32)
    picked[320:] = jnp.zeros((64, picked.shape[1]), BF16)
    for i in range(5):
        for part in range(2):
            for tile in range(6):
                piece = rows[pl.ds(part * 30 + i * 6 + tile, 64, stride=60), :]
                low = (part * 6 + tile) * LANES
                picked[i * 64 : i * 64 + 64, low : low + LANES] = piece.astype(BF16)
    out_ref[...] = lax.dot_general(
        w_ref[...], picked[...], (((1,), (1,)), ((), ())), preferred_element_type=F32
    ).astype(BF16)


def act_kernel(in_ref, out_ref):
    up = in_ref[0].astype(F32)
    for part in range(1, in_ref.shape[0]):
        up = up + in_ref[part].astype(F32)
    out_ref[...] = (up / (1.0 + jnp.exp(-up))).astype(BF16)


def down_kernel(h_ref, w_ref, out_ref, rows, whole):
    columns = w_ref.shape[2]
    for y in range(4):
        for pair in range(2):
            low = (pair * 4 + y) * columns
            whole[low : low + columns] = w_ref[y, pair]
    for slot in (30, 31):
        rows[pl.ds(slot, 64, stride=SLOTS), :] = jnp.zeros((64, LANES), F32)
    out = lax.dot_general(
        h_ref[...], whole[...], (((0,), (1,)), ((), ())), preferred_element_type=F32
    )
    for i in range(5):
        for tile in range(6):
            rows[pl.ds(i * 6 + tile, 64, stride=SLOTS), :] = out[
                i * 64 : i * 64 + 64, tile * LANES : (tile + 1) * LANES
            ]
    for block in range(64):
        z, y = divmod(block, 4)
        out_ref[y * 16 + z] = rows[block * SLOTS : (block + 1) * SLOTS].astype(BF16)


def sum_kernel(in_ref, out_ref):
    total = in_ref[0:16].astype(F32)
    for part in range(1, 4):
        total = total + in_ref[part * 16 : part * 16 + 16].astype(F32)
    out_ref[...] = total.astype(BF16)


def weigh_kernel(place_ref, y_ref, row_ref, router_ref, out_ref):
    products = jnp.zeros((SLOTS, LANES), F32)
    own = place_ref[0] * 8
    for part in range(8):
        products = products + row_ref[own + part].astype(F32) * router_ref[part].astype(F32)
    one = lax.broadcasted_iota(jnp.int32, (SLOTS, SLOTS), 0) // 6
    two = lax.broadcasted_iota(jnp.int32, (SLOTS, SLOTS), 1) // 6
    alike = jnp.where(one == two, 1.0, 0.0)
    sums = jnp.dot(
        alike, products, preferred_element_type=F32, precision=lax.Precision.HIGHEST
    )
    gate = jax.nn.sigmoid(jnp.sum(sums, axis=-1, keepdims=True))
    for group in range(8):
        total = y_ref[group * 2].astype(F32) + y_ref[group * 2 + 1].astype(F32)
        out_ref[group] = (total * gate).astype(BF16)


def add_kernel(attn_ref, y_ref, sel_ref, out_ref, rows, weighted):
    length = attn_ref.shape[0]
    rows[...] = y_ref[...].astype(F32).reshape(8 * SLOTS, LANES)
    weighted[...] = jnp.zeros_like(weighted)
    for i in range(5):
        for tile in range(6):
            weighted[i * 8 : i * 8 + 8, tile * LANES : (tile + 1) * LANES] = rows[
                pl.ds(i * 6 + tile, 8, stride=SLOTS), :
            ]
    place = lax.broadcasted_iota(jnp.int32, (length, LANES), 0)
    chosen = jnp.where(place == sel_ref[...], 1.0, 0.0).astype(BF16)
    added = jnp.dot(chosen, weighted[...].astype(BF16), preferred_element_type=F32)
    out_ref[...] = (attn_ref[...].astype(F32) + added).astype(BF16)


def shape(dims, dtype=BF16):
    return jax.ShapeDtypeStruct(dims, dtype)


def body(queries, keys, values, selections, router, w_up, w_down):
    length, width = queries.shape
    parts = lax.axis_size("p")
    seq = ("r", "l", "y")
    units = w_up.shape[1]
    quarter = w_up.shape[2] // 4
    place = lax.axis_index("y").astype(jnp.int32)
    columns = w_down.shape[1]
    group = w_down.shape[2] // parts
    sel = selections[0].T.reshape(-1)
    sel_column = sel[:, None]
    sel_row = jnp.pad(sel, (0, LANES - sel.shape[0]), constant_values=-1)[None]
    router_rows = jnp.tile(router.reshape(parts, 6, LANES), (1, 5, 1))
    router_rows = jnp.pad(router_rows, ((0, 0), (0, SLOTS - 30), (0, 0)))

    state = call(
        state_kernel,
        shape((4, 144, LANES)),
        keys,
        values,
        scratch=[pltpu.VMEM((width, width), F32), pltpu.VMEM((4, 144, LANES), F32)],
        name="state",
    )
    quarters = lax.all_to_all(state, "y", 0, 0, tiled=True)
    quarters, queries, w_up, w_down = lax.optimization_barrier((quarters, queries, w_up, w_down))
    totals = call(
        total_kernel,
        shape((16, 16, LANES)),
        quarters,
        scratch=[pltpu.VMEM((152, LANES), F32)],
        name="total",
    )
    totals = lax.all_to_all(totals, ("r", "l"), 0, 0, tiled=True)
    inner = call(inner_kernel, shape((length, width), F32), queries, keys, values, name="inner")
    up_cut = call(
        cut_up_kernel,
        shape((4, units, quarter)),
        w_up[0],
        scratch=[pltpu.SemaphoreType.DMA((4,))],
        spaces=([HBM], HBM),
        name="cut_up",
    )
    totals, inner, up_cut, w_down = lax.optimization_barrier((totals, inner, up_cut, w_down))
    bases = call(prefix_kernel, shape((16, 16, LANES)), totals, name="prefix")
    bases = lax.all_to_all(bases, ("r", "l"), 0, 0, tiled=True)
    pair = lax.axis_index("l").astype(jnp.int32).reshape(1)
    down_keep, down_one, down_two = call(
        cut_down_kernel,
        [shape((n, columns, group)) for n in (4, 2, 2)],
        pair,
        w_down[0],
        scratch=[pltpu.VMEM((8, columns, group), BF16), pltpu.SemaphoreType.DMA((8,))],
        spaces=([pltpu.SMEM, pltpu.VMEM], [HBM] * 3),
        name="cut_down",
    )
    bases, down_keep, down_one, down_two = lax.optimization_barrier(
        (bases, down_keep, down_one, down_two)
    )
    before = call(
        spread_kernel,
        shape((4, 144, LANES)),
        bases,
        quarters,
        scratch=[pltpu.VMEM((144, LANES), F32)],
        name="spread",
    )
    before, down_one = lax.optimization_barrier((before, down_one))
    before = lax.all_to_all(before, "y", 0, 0, tiled=True)
    down_one = lax.ppermute(down_one, "l", [(0, 1), (1, 0)])
    before, down_one, down_two = lax.optimization_barrier((before, down_one, down_two))
    attn, pay = call(
        attn_kernel,
        (shape((length, width)), shape((8, SLOTS, LANES))),
        queries,
        inner,
        before,
        sel_column,
        scratch=[
            pltpu.VMEM((6 * HEAD, LANES), F32),
            pltpu.VMEM((width, width), BF16),
            pltpu.VMEM((length, width), F32),
            pltpu.VMEM((8 * SLOTS, LANES), F32),
        ],
        name="attn",
    )
    pay, down_two = lax.optimization_barrier((pay, down_two))
    down_two = lax.ppermute(down_two, "l", [(0, 1), (1, 0)])
    whole_rows = lax.all_to_all(jnp.tile(pay, (4, 1, 1)), ("y", "p"), 0, 0, tiled=True)
    whole_rows, down_two = lax.optimization_barrier((whole_rows, down_two))
    near_rows = call(
        near_kernel,
        shape((240, LANES)),
        place.reshape(1),
        whole_rows,
        scratch=[pltpu.VMEM((240, LANES), F32)],
        spaces=([pltpu.SMEM, pltpu.VMEM], pltpu.VMEM),
        name="near",
    )
    near_rows, up_cut = lax.optimization_barrier((near_rows, up_cut))
    up_mine = lax.all_to_all(up_cut, "y", 0, 0, tiled=True).reshape(4 * units, quarter)
    arrived = lax.all_gather(near_rows, ("r", "l"), axis=0, tiled=True)
    partial = call(
        up_kernel,
        shape((4 * units, 384)),
        arrived,
        up_mine,
        scratch=[pltpu.VMEM((64 * 60, LANES), F32), pltpu.VMEM((384, quarter), BF16)],
        name="up",
    )
    partial, down_keep = lax.optimization_barrier((partial, down_keep))
    sums = lax.all_to_all(partial.reshape(4, units, 384), "y", 0, 0, tiled=True)
    down_cut = call(
        join_kernel,
        shape((4, 2, columns, group)),
        pair,
        down_keep,
        down_one,
        down_two,
        scratch=[pltpu.SemaphoreType.DMA((8,))],
        spaces=([pltpu.SMEM] + [HBM] * 3, HBM),
        name="join",
    )
    sums, down_cut = lax.optimization_barrier((sums, down_cut))
    act = call(act_kernel, shape((units, 384)), sums, name="act")
    act, down_cut = lax.optimization_barrier((act, down_cut))
    down_mine = lax.all_to_all(down_cut, "y", 0, 0, tiled=True)
    act = lax.all_gather(act, "r", axis=0, tiled=True)
    out = call(
        down_kernel,
        shape((64, SLOTS, LANES)),
        act,
        down_mine,
        scratch=[
            pltpu.VMEM((64 * SLOTS, LANES), F32),
            pltpu.VMEM((8 * columns, group), BF16),
        ],
        name="down",
    )
    back = lax.all_to_all(out, "y", 0, 0, tiled=True)
    back = call(sum_kernel, shape((16, SLOTS, LANES)), back, name="sum")
    back = lax.all_to_all(back, ("r", "l"), 0, 0, tiled=True)
    weighted = call(
        weigh_kernel,
        shape((8, SLOTS, LANES)),
        place.reshape(1),
        back,
        whole_rows,
        router_rows,
        spaces=([pltpu.SMEM] + [pltpu.VMEM] * 3, pltpu.VMEM),
        name="weigh",
    )
    weighted = lax.all_to_all(weighted, "p", 0, 0, tiled=True)
    return call(
        add_kernel,
        shape((length, width)),
        attn,
        weighted,
        sel_row,
        scratch=[pltpu.VMEM((8 * SLOTS, LANES), F32), pltpu.VMEM((LANES, width), F32)],
        name="add",
    )


def solution(mesh):
    split = Mesh(mesh.devices.reshape(8, 2, 4, 8), ("r", "l", "y", "p"))
    seq = ("r", "l", "y")
    placed = (
        P(seq, "p"),
        P(seq, "p"),
        P(seq, "p"),
        P(seq, None, None),
        P(None, "p"),
        P("p", seq, None),
        P("p", seq, None),
    )
    return jax.shard_map(
        body, mesh=split, in_specs=placed, out_specs=P(seq, "p"), check_vma=False
    )
```

```python
import jax
import jax.numpy as jnp
from jax import lax
from jax.experimental import pallas as pl
from jax.experimental.pallas import tpu as pltpu
from jax.sharding import Mesh, PartitionSpec as P

HEAD = 96
LANES = 128
SLOTS = 32
INTERPRET = False
BF16 = jnp.bfloat16
F32 = jnp.float32


HBM = pltpu.HBM


def call(kernel, out, *args, scratch=(), spaces=None, name=None):
    specs = {}
    if spaces:
        ins, outs = spaces
        specs["in_specs"] = [pl.BlockSpec(memory_space=space) for space in ins]
        specs["out_specs"] = (
            [pl.BlockSpec(memory_space=space) for space in outs]
            if isinstance(outs, list)
            else pl.BlockSpec(memory_space=outs)
        )
    return pl.pallas_call(
        kernel,
        out_shape=out,
        scratch_shapes=list(scratch),
        compiler_params=pltpu.CompilerParams(vmem_limit_bytes=16 * 2**20),
        interpret=INTERPRET,
        name=name,
        **specs,
    )(*args)


def tile_heads(tile):
    first = tile * LANES // HEAD
    return first, (first + 1) * HEAD - tile * LANES


def head_window(head):
    first, last = head * HEAD // LANES, (head * HEAD + HEAD - 1) // LANES
    return first * LANES, (last + 1) * LANES, head * HEAD - first * LANES


def eighth(tile, rows8):
    group = tile * 12 + rows8
    return group % 8, group // 8 * 8


def state_kernel(k_ref, v_ref, out_ref, grand, rows):
    grand[...] = lax.dot_general(
        k_ref[...], v_ref[...], (((0,), (0,)), ((), ())), preferred_element_type=F32
    )
    lane = lax.broadcasted_iota(jnp.int32, (HEAD, LANES), 1)
    for tile in range(6):
        head, split = tile_heads(tile)
        at = slice(tile * LANES, (tile + 1) * LANES)
        one = grand[head * HEAD : (head + 1) * HEAD, at]
        two = grand[(head + 1) * HEAD : (head + 2) * HEAD, at]
        block = jnp.where(lane < split, one, two)
        for rows8 in range(12):
            part, low = eighth(tile, rows8)
            rows[part, low : low + 8] = block[rows8 * 8 : rows8 * 8 + 8]
    out_ref[...] = rows[...].astype(BF16)


def total_kernel(in_ref, out_ref, rows):
    total = in_ref[0].astype(F32)
    for part in range(1, 8):
        total = total + in_ref[part].astype(F32)
    rows[0:72] = total
    rows[72:128] = jnp.zeros((56, LANES), F32)
    for part in range(8):
        out_ref[part] = rows[pl.ds(part, 16, stride=8), :].astype(BF16)


def prefix_kernel(in_ref, out_ref):
    total = jnp.zeros((16, LANES), F32)
    for part in range(8):
        out_ref[part] = total.astype(BF16)
        total = total + in_ref[part].astype(F32)


def spread_kernel(base_ref, in_ref, out_ref, rows):
    for part in range(8):
        rows[pl.ds(part, 16, stride=8), :] = base_ref[part].astype(F32)
    total = rows[0:72]
    for part in range(8):
        out_ref[part] = total.astype(BF16)
        total = total + in_ref[part].astype(F32)


def inner_kernel(q_ref, k_ref, v_ref, out_ref):
    length = q_ref.shape[0]
    out_ref[...] = jnp.zeros_like(out_ref)
    below = lax.broadcasted_iota(jnp.int32, (length, length), 0) >= lax.broadcasted_iota(
        jnp.int32, (length, length), 1
    )
    for head in range(8):
        start, stop, low = head_window(head)
        lane = lax.broadcasted_iota(jnp.int32, (1, stop - start), 1)
        mine = (lane >= low) & (lane < low + HEAD)
        q = q_ref[:, start:stop] * mine.astype(F32).astype(BF16)
        scores = lax.dot_general(
            q, k_ref[:, start:stop], (((1,), (1,)), ((), ())), preferred_element_type=F32
        )
        scores = jnp.where(below, scores, 0.0).astype(BF16)
        mixed = jnp.dot(scores, v_ref[:, start:stop], preferred_element_type=F32)
        out_ref[:, start:stop] = jnp.where(mine, mixed, out_ref[:, start:stop])


def attn_kernel(q_ref, inner_ref, p_ref, sel_ref, attn_ref, pay_ref, rows, wide, normed, picks):
    length = q_ref.shape[0]
    parts = [p_ref[part].astype(F32) for part in range(8)]
    for tile in range(6):
        for rows8 in range(12):
            part, low = eighth(tile, rows8)
            at = tile * HEAD + rows8 * 8
            rows[at : at + 8] = parts[part][low : low + 8]
    wide[...] = jnp.zeros_like(wide)
    lane = lax.broadcasted_iota(jnp.int32, (HEAD, LANES), 1)
    for tile in range(6):
        head, split = tile_heads(tile)
        at = slice(tile * LANES, (tile + 1) * LANES)
        block = rows[tile * HEAD : (tile + 1) * HEAD]
        low = head * HEAD
        wide[low : low + HEAD, at] = jnp.where(lane < split, block, 0.0).astype(BF16)
        low = low + HEAD
        wide[low : low + HEAD, at] = jnp.where(lane < split, 0.0, block).astype(BF16)
    normed[...] = inner_ref[...] + jnp.dot(q_ref[...], wide[...], preferred_element_type=F32)
    for head in range(8):
        start, stop, low = head_window(head)
        lane = lax.broadcasted_iota(jnp.int32, (1, stop - start), 1)
        mine = (lane >= low) & (lane < low + HEAD)
        mixed = normed[:, start:stop]
        power = jnp.sum(jnp.where(mine, mixed * mixed, 0.0), axis=-1, keepdims=True) / HEAD
        normed[:, start:stop] = jnp.where(mine, mixed * lax.rsqrt(power + 1e-06), mixed)
    attn = normed[...].astype(BF16)
    attn_ref[...] = attn
    place = lax.broadcasted_iota(jnp.int32, (40, length), 1)
    chosen = jnp.where(place == sel_ref[...], 1.0, 0.0).astype(BF16)
    picked = jnp.dot(chosen, attn, preferred_element_type=F32)
    picks[...] = jnp.zeros_like(picks)
    for i in range(5):
        for tile in range(6):
            picks[pl.ds(i * 6 + tile, 8, stride=SLOTS), :] = picked[
                i * 8 : i * 8 + 8, tile * LANES : (tile + 1) * LANES
            ]
    pay_ref[...] = picks[...].reshape(8, SLOTS, LANES).astype(BF16)


def cut_up_kernel(w_ref, out_ref, sems):
    parts, width = out_ref.shape[0], out_ref.shape[2]
    copies = []
    for part in range(parts):
        source = w_ref.at[:, part * width : (part + 1) * width]
        copies.append(pltpu.make_async_copy(source, out_ref.at[part], sems.at[part]))
        copies[-1].start()
    for copy in copies:
        copy.wait()


def cut_down_kernel(place_ref, w_ref, keep_ref, one_ref, two_ref, cut, sems):
    run = w_ref.shape[1] // 64
    for part in range(8):
        for group in range(8):
            low = (group * 8 + part) * run
            cut[part, :, group * run : (group + 1) * run] = w_ref[:, low : low + run]
    own = place_ref[0] * 4
    other = 4 - own
    copies = []
    for n in range(4):
        away = (one_ref, two_ref)[n // 2].at[n % 2]
        copies.append(pltpu.make_async_copy(cut.at[own + n], keep_ref.at[n], sems.at[n]))
        copies.append(pltpu.make_async_copy(cut.at[other + n], away, sems.at[4 + n]))
    for copy in copies:
        copy.start()
    for copy in copies:
        copy.wait()


def join_kernel(place_ref, keep_ref, one_ref, two_ref, out_ref, sems):
    own = place_ref[0]
    copies = []
    for n in range(4):
        away = (one_ref, two_ref)[n // 2].at[n % 2]
        copies.append(pltpu.make_async_copy(keep_ref.at[n], out_ref.at[n, own], sems.at[n]))
        copies.append(pltpu.make_async_copy(away, out_ref.at[n, 1 - own], sems.at[4 + n]))
    for copy in copies:
        copy.start()
    for copy in copies:
        copy.wait()


def near_kernel(place_ref, row_ref, out_ref, rows):
    for block in range(4):
        for part in range(2):
            low = (block * 2 + part) * 30
            piece = row_ref[block * 8 + 2 * place_ref[0] + part].astype(F32)
            rows[low : low + 30] = piece[:30]
    out_ref[...] = rows[...].astype(BF16)


def up_kernel(x_ref, w_ref, out_ref, rows, picked):
    rows[...] = x_ref[...].astype(F32)
    picked[320:] = jnp.zeros((64, picked.shape[1]), BF16)
    for i in range(5):
        for part in range(2):
            for tile in range(6):
                piece = rows[pl.ds(part * 30 + i * 6 + tile, 64, stride=60), :]
                low = (part * 6 + tile) * LANES
                picked[i * 64 : i * 64 + 64, low : low + LANES] = piece.astype(BF16)
    out_ref[...] = lax.dot_general(
        w_ref[...], picked[...], (((1,), (1,)), ((), ())), preferred_element_type=F32
    ).astype(BF16)


def act_kernel(in_ref, out_ref):
    up = in_ref[0].astype(F32)
    for part in range(1, in_ref.shape[0]):
        up = up + in_ref[part].astype(F32)
    out_ref[...] = (up / (1.0 + jnp.exp(-up))).astype(BF16)


def down_kernel(h_ref, w_ref, out_ref, rows, whole):
    columns = w_ref.shape[2]
    for y in range(4):
        for pair in range(2):
            low = (pair * 4 + y) * columns
            whole[low : low + columns] = w_ref[y, pair]
    for slot in (30, 31):
        rows[pl.ds(slot, 64, stride=SLOTS), :] = jnp.zeros((64, LANES), F32)
    out = lax.dot_general(
        h_ref[...], whole[...], (((0,), (1,)), ((), ())), preferred_element_type=F32
    )
    for i in range(5):
        for tile in range(6):
            rows[pl.ds(i * 6 + tile, 64, stride=SLOTS), :] = out[
                i * 64 : i * 64 + 64, tile * LANES : (tile + 1) * LANES
            ]
    for block in range(64):
        r, place = divmod(block, 8)
        out_ref[place * 8 + r] = rows[block * SLOTS : (block + 1) * SLOTS].astype(BF16)


def sum_kernel(in_ref, out_ref):
    total = in_ref[0:8].astype(F32)
    for part in range(1, 8):
        total = total + in_ref[part * 8 : part * 8 + 8].astype(F32)
    out_ref[...] = total.astype(BF16)


def weigh_kernel(place_ref, y_ref, row_ref, router_ref, out_ref):
    products = jnp.zeros((SLOTS, LANES), F32)
    own = place_ref[0] * 8
    for part in range(8):
        products = products + row_ref[own + part].astype(F32) * router_ref[part].astype(F32)
    one = lax.broadcasted_iota(jnp.int32, (SLOTS, SLOTS), 0) // 6
    two = lax.broadcasted_iota(jnp.int32, (SLOTS, SLOTS), 1) // 6
    alike = jnp.where(one == two, 1.0, 0.0)
    sums = jnp.dot(
        alike, products, preferred_element_type=F32, precision=lax.Precision.HIGHEST
    )
    gate = jax.nn.sigmoid(jnp.sum(sums, axis=-1, keepdims=True))
    for group in range(8):
        out_ref[group] = (y_ref[group].astype(F32) * gate).astype(BF16)


def add_kernel(attn_ref, y_ref, sel_ref, out_ref, rows, weighted):
    length = attn_ref.shape[0]
    rows[...] = y_ref[...].astype(F32).reshape(8 * SLOTS, LANES)
    weighted[...] = jnp.zeros_like(weighted)
    for i in range(5):
        for tile in range(6):
            weighted[i * 8 : i * 8 + 8, tile * LANES : (tile + 1) * LANES] = rows[
                pl.ds(i * 6 + tile, 8, stride=SLOTS), :
            ]
    place = lax.broadcasted_iota(jnp.int32, (length, LANES), 0)
    chosen = jnp.where(place == sel_ref[...], 1.0, 0.0).astype(BF16)
    added = jnp.dot(chosen, weighted[...].astype(BF16), preferred_element_type=F32)
    out_ref[...] = (attn_ref[...].astype(F32) + added).astype(BF16)


def shape(dims, dtype=BF16):
    return jax.ShapeDtypeStruct(dims, dtype)


def body(queries, keys, values, selections, router, w_up, w_down):
    length, width = queries.shape
    parts = lax.axis_size("p")
    patch = ("l", "y")
    units = w_up.shape[1]
    quarter = w_up.shape[2] // 4
    place = lax.axis_index("y").astype(jnp.int32)
    columns = w_down.shape[1]
    group = w_down.shape[2] // parts
    sel = selections[0].T.reshape(-1)
    sel_column = sel[:, None]
    sel_row = jnp.pad(sel, (0, LANES - sel.shape[0]), constant_values=-1)[None]
    router_rows = jnp.tile(router.reshape(parts, 6, LANES), (1, 5, 1))
    router_rows = jnp.pad(router_rows, ((0, 0), (0, SLOTS - 30), (0, 0)))

    state = call(
        state_kernel,
        shape((8, 72, LANES)),
        keys,
        values,
        scratch=[pltpu.VMEM((width, width), F32), pltpu.VMEM((8, 72, LANES), F32)],
        name="state",
    )
    parts_here = lax.all_to_all(state, patch, 0, 0, tiled=True)
    parts_here, queries, w_up, w_down = lax.optimization_barrier(
        (parts_here, queries, w_up, w_down)
    )
    totals = call(
        total_kernel,
        shape((8, 16, LANES)),
        parts_here,
        scratch=[pltpu.VMEM((128, LANES), F32)],
        name="total",
    )
    totals = lax.all_to_all(totals, "r", 0, 0, tiled=True)
    inner = call(inner_kernel, shape((length, width), F32), queries, keys, values, name="inner")
    up_cut = call(
        cut_up_kernel,
        shape((4, units, quarter)),
        w_up[0],
        scratch=[pltpu.SemaphoreType.DMA((4,))],
        spaces=([HBM], HBM),
        name="cut_up",
    )
    totals, inner, up_cut, w_down = lax.optimization_barrier((totals, inner, up_cut, w_down))
    bases = call(prefix_kernel, shape((8, 16, LANES)), totals, name="prefix")
    bases = lax.all_to_all(bases, "r", 0, 0, tiled=True)
    pair = lax.axis_index("l").astype(jnp.int32).reshape(1)
    down_keep, down_one, down_two = call(
        cut_down_kernel,
        [shape((n, columns, group)) for n in (4, 2, 2)],
        pair,
        w_down[0],
        scratch=[pltpu.VMEM((8, columns, group), BF16), pltpu.SemaphoreType.DMA((8,))],
        spaces=([pltpu.SMEM, pltpu.VMEM], [HBM] * 3),
        name="cut_down",
    )
    bases, down_keep, down_one, down_two = lax.optimization_barrier(
        (bases, down_keep, down_one, down_two)
    )
    before = call(
        spread_kernel,
        shape((8, 72, LANES)),
        bases,
        parts_here,
        scratch=[pltpu.VMEM((128, LANES), F32)],
        name="spread",
    )
    before, down_one = lax.optimization_barrier((before, down_one))
    before = lax.all_to_all(before, patch, 0, 0, tiled=True)
    down_one = lax.ppermute(down_one, "l", [(0, 1), (1, 0)])
    before, down_one, down_two = lax.optimization_barrier((before, down_one, down_two))
    attn, pay = call(
        attn_kernel,
        (shape((length, width)), shape((8, SLOTS, LANES))),
        queries,
        inner,
        before,
        sel_column,
        scratch=[
            pltpu.VMEM((6 * HEAD, LANES), F32),
            pltpu.VMEM((width, width), BF16),
            pltpu.VMEM((length, width), F32),
            pltpu.VMEM((8 * SLOTS, LANES), F32),
        ],
        name="attn",
    )
    pay, down_two = lax.optimization_barrier((pay, down_two))
    down_two = lax.ppermute(down_two, "l", [(0, 1), (1, 0)])
    whole_rows = lax.all_to_all(jnp.tile(pay, (4, 1, 1)), ("y", "p"), 0, 0, tiled=True)
    whole_rows, down_two = lax.optimization_barrier((whole_rows, down_two))
    near_rows = call(
        near_kernel,
        shape((240, LANES)),
        place.reshape(1),
        whole_rows,
        scratch=[pltpu.VMEM((240, LANES), F32)],
        spaces=([pltpu.SMEM, pltpu.VMEM], pltpu.VMEM),
        name="near",
    )
    near_rows, up_cut = lax.optimization_barrier((near_rows, up_cut))
    up_mine = lax.all_to_all(up_cut, "y", 0, 0, tiled=True).reshape(4 * units, quarter)
    arrived = lax.all_gather(near_rows, ("r", "l"), axis=0, tiled=True)
    partial = call(
        up_kernel,
        shape((4 * units, 384)),
        arrived,
        up_mine,
        scratch=[pltpu.VMEM((64 * 60, LANES), F32), pltpu.VMEM((384, quarter), BF16)],
        name="up",
    )
    partial, down_keep = lax.optimization_barrier((partial, down_keep))
    sums = lax.all_to_all(partial.reshape(4, units, 384), "y", 0, 0, tiled=True)
    down_cut = call(
        join_kernel,
        shape((4, 2, columns, group)),
        pair,
        down_keep,
        down_one,
        down_two,
        scratch=[pltpu.SemaphoreType.DMA((8,))],
        spaces=([pltpu.SMEM] + [HBM] * 3, HBM),
        name="join",
    )
    sums, down_cut = lax.optimization_barrier((sums, down_cut))
    act = call(act_kernel, shape((units, 384)), sums, name="act")
    act, down_cut = lax.optimization_barrier((act, down_cut))
    down_mine = lax.all_to_all(down_cut, "y", 0, 0, tiled=True)
    act = lax.all_gather(act, "r", axis=0, tiled=True)
    out = call(
        down_kernel,
        shape((64, SLOTS, LANES)),
        act,
        down_mine,
        scratch=[
            pltpu.VMEM((64 * SLOTS, LANES), F32),
            pltpu.VMEM((8 * columns, group), BF16),
        ],
        name="down",
    )
    back = lax.all_to_all(out, patch, 0, 0, tiled=True)
    back = call(sum_kernel, shape((8, SLOTS, LANES)), back, name="sum")
    back = lax.all_to_all(back, "r", 0, 0, tiled=True)
    weighted = call(
        weigh_kernel,
        shape((8, SLOTS, LANES)),
        place.reshape(1),
        back,
        whole_rows,
        router_rows,
        spaces=([pltpu.SMEM] + [pltpu.VMEM] * 3, pltpu.VMEM),
        name="weigh",
    )
    weighted = lax.all_to_all(weighted, "p", 0, 0, tiled=True)
    return call(
        add_kernel,
        shape((length, width)),
        attn,
        weighted,
        sel_row,
        scratch=[pltpu.VMEM((8 * SLOTS, LANES), F32), pltpu.VMEM((LANES, width), F32)],
        name="add",
    )


def solution(mesh):
    split = Mesh(mesh.devices.reshape(8, 2, 4, 8), ("r", "l", "y", "p"))
    seq = ("r", "l", "y")
    placed = (
        P(seq, "p"),
        P(seq, "p"),
        P(seq, "p"),
        P(seq, None, None),
        P(None, "p"),
        P("p", seq, None),
        P("p", seq, None),
    )
    return jax.shard_map(
        body, mesh=split, in_specs=placed, out_specs=P(seq, "p"), check_vma=False
    )
```

```python
import jax
import jax.numpy as jnp
from jax import lax
from jax.experimental import pallas as pl
from jax.experimental.pallas import tpu as pltpu
from jax.sharding import Mesh, PartitionSpec as P

HEAD = 96
LANES = 128
SLOTS = 32
INTERPRET = False
BF16 = jnp.bfloat16
F32 = jnp.float32


HBM = pltpu.HBM


def call(kernel, out, *args, scratch=(), spaces=None, name=None):
    specs = {}
    if spaces:
        ins, outs = spaces
        specs["in_specs"] = [pl.BlockSpec(memory_space=space) for space in ins]
        specs["out_specs"] = (
            [pl.BlockSpec(memory_space=space) for space in outs]
            if isinstance(outs, list)
            else pl.BlockSpec(memory_space=outs)
        )
    return pl.pallas_call(
        kernel,
        out_shape=out,
        scratch_shapes=list(scratch),
        compiler_params=pltpu.CompilerParams(vmem_limit_bytes=16 * 2**20),
        interpret=INTERPRET,
        name=name,
        **specs,
    )(*args)


def tile_heads(tile):
    first = tile * LANES // HEAD
    return first, (first + 1) * HEAD - tile * LANES


def head_window(head):
    first, last = head * HEAD // LANES, (head * HEAD + HEAD - 1) // LANES
    return first * LANES, (last + 1) * LANES, head * HEAD - first * LANES


def state_kernel(k_ref, v_ref, out_ref, grand, rows):
    grand[...] = lax.dot_general(
        k_ref[...], v_ref[...], (((0,), (0,)), ((), ())), preferred_element_type=F32
    )
    lane = lax.broadcasted_iota(jnp.int32, (HEAD, LANES), 1)
    for tile in range(6):
        head, split = tile_heads(tile)
        at = slice(tile * LANES, (tile + 1) * LANES)
        one = grand[head * HEAD : (head + 1) * HEAD, at]
        two = grand[(head + 1) * HEAD : (head + 2) * HEAD, at]
        block = jnp.where(lane < split, one, two)
        for quarter in range(4):
            rows[quarter, tile * 24 : tile * 24 + 24] = block[quarter * 24 : quarter * 24 + 24]
    out_ref[...] = rows[...].astype(BF16)


def total_kernel(in_ref, out_ref, rows):
    total = in_ref[0].astype(F32)
    for y in range(1, 4):
        total = total + in_ref[y].astype(F32)
    rows[0:144] = total
    rows[144:152] = jnp.zeros((8, LANES), F32)
    for z in range(16):
        out_ref[z] = rows[z * 9 : z * 9 + 16].astype(BF16)


def prefix_kernel(in_ref, out_ref):
    total = jnp.zeros((16, LANES), F32)
    for z in range(16):
        out_ref[z] = total.astype(BF16)
        total = total + in_ref[z].astype(F32)


def spread_kernel(base_ref, in_ref, out_ref, rows):
    for z in range(16):
        rows[z * 9 : z * 9 + 9] = base_ref[z].astype(F32)[0:9]
    total = rows[...]
    for y in range(4):
        out_ref[y] = total.astype(BF16)
        total = total + in_ref[y].astype(F32)


def inner_kernel(q_ref, k_ref, v_ref, out_ref):
    length = q_ref.shape[0]
    out_ref[...] = jnp.zeros_like(out_ref)
    below = lax.broadcasted_iota(jnp.int32, (length, length), 0) >= lax.broadcasted_iota(
        jnp.int32, (length, length), 1
    )
    for head in range(8):
        start, stop, low = head_window(head)
        lane = lax.broadcasted_iota(jnp.int32, (1, stop - start), 1)
        mine = (lane >= low) & (lane < low + HEAD)
        q = q_ref[:, start:stop] * mine.astype(F32).astype(BF16)
        scores = lax.dot_general(
            q, k_ref[:, start:stop], (((1,), (1,)), ((), ())), preferred_element_type=F32
        )
        scores = jnp.where(below, scores, 0.0).astype(BF16)
        mixed = jnp.dot(scores, v_ref[:, start:stop], preferred_element_type=F32)
        out_ref[:, start:stop] = jnp.where(mine, mixed, out_ref[:, start:stop])


def attn_kernel(q_ref, inner_ref, p_ref, sel_ref, attn_ref, pay_ref, rows, wide, normed, picks):
    length = q_ref.shape[0]
    for quarter in range(4):
        part = p_ref[quarter].astype(F32)
        for tile in range(6):
            low = tile * HEAD + quarter * 24
            rows[low : low + 24] = part[tile * 24 : tile * 24 + 24]
    wide[...] = jnp.zeros_like(wide)
    lane = lax.broadcasted_iota(jnp.int32, (HEAD, LANES), 1)
    for tile in range(6):
        head, split = tile_heads(tile)
        at = slice(tile * LANES, (tile + 1) * LANES)
        block = rows[tile * HEAD : (tile + 1) * HEAD]
        low = head * HEAD
        wide[low : low + HEAD, at] = jnp.where(lane < split, block, 0.0).astype(BF16)
        low = low + HEAD
        wide[low : low + HEAD, at] = jnp.where(lane < split, 0.0, block).astype(BF16)
    normed[...] = inner_ref[...] + jnp.dot(q_ref[...], wide[...], preferred_element_type=F32)
    for head in range(8):
        start, stop, low = head_window(head)
        lane = lax.broadcasted_iota(jnp.int32, (1, stop - start), 1)
        mine = (lane >= low) & (lane < low + HEAD)
        mixed = normed[:, start:stop]
        power = jnp.sum(jnp.where(mine, mixed * mixed, 0.0), axis=-1, keepdims=True) / HEAD
        normed[:, start:stop] = jnp.where(mine, mixed * lax.rsqrt(power + 1e-06), mixed)
    attn = normed[...].astype(BF16)
    attn_ref[...] = attn
    place = lax.broadcasted_iota(jnp.int32, (40, length), 1)
    chosen = jnp.where(place == sel_ref[...], 1.0, 0.0).astype(BF16)
    picked = jnp.dot(chosen, attn, preferred_element_type=F32)
    picks[...] = jnp.zeros_like(picks)
    for i in range(5):
        for tile in range(6):
            picks[pl.ds(i * 6 + tile, 8, stride=SLOTS), :] = picked[
                i * 8 : i * 8 + 8, tile * LANES : (tile + 1) * LANES
            ]
    pay = picks[...].reshape(8, SLOTS, LANES).astype(BF16)
    for y in range(4):
        pay_ref[y * 8 : y * 8 + 8] = pay


def cut_up_kernel(w_ref, out_ref, sems):
    parts, width = out_ref.shape[0], out_ref.shape[2]
    copies = []
    for part in range(parts):
        source = w_ref.at[:, part * width : (part + 1) * width]
        copies.append(pltpu.make_async_copy(source, out_ref.at[part], sems.at[part]))
        copies[-1].start()
    for copy in copies:
        copy.wait()


def cut_down_kernel(place_ref, w_ref, keep_ref, one_ref, two_ref, cut, sems):
    run = w_ref.shape[1] // 64
    for part in range(8):
        for group in range(8):
            low = (group * 8 + part) * run
            cut[part, :, group * run : (group + 1) * run] = w_ref[:, low : low + run]
    own = place_ref[0] * 4
    other = 4 - own
    copies = []
    for n in range(4):
        away = (one_ref, two_ref)[n // 2].at[n % 2]
        copies.append(pltpu.make_async_copy(cut.at[own + n], keep_ref.at[n], sems.at[n]))
        copies.append(pltpu.make_async_copy(cut.at[other + n], away, sems.at[4 + n]))
    for copy in copies:
        copy.start()
    for copy in copies:
        copy.wait()


def join_kernel(place_ref, keep_ref, one_ref, two_ref, out_ref, sems):
    own = place_ref[0]
    copies = []
    for n in range(4):
        away = (one_ref, two_ref)[n // 2].at[n % 2]
        copies.append(pltpu.make_async_copy(keep_ref.at[n], out_ref.at[n, own], sems.at[n]))
        copies.append(pltpu.make_async_copy(away, out_ref.at[n, 1 - own], sems.at[4 + n]))
    for copy in copies:
        copy.start()
    for copy in copies:
        copy.wait()


def near_kernel(place_ref, row_ref, out_ref, rows):
    for block in range(4):
        for part in range(2):
            low = (block * 2 + part) * 30
            piece = row_ref[block * 8 + 2 * place_ref[0] + part].astype(F32)
            rows[low : low + 30] = piece[:30]
    out_ref[...] = rows[...].astype(BF16)


def up_kernel(x_ref, w_ref, out_ref, rows, picked):
    rows[...] = x_ref[...].astype(F32)
    picked[320:] = jnp.zeros((64, picked.shape[1]), BF16)
    for i in range(5):
        for part in range(2):
            for tile in range(6):
                piece = rows[pl.ds(part * 30 + i * 6 + tile, 64, stride=60), :]
                low = (part * 6 + tile) * LANES
                picked[i * 64 : i * 64 + 64, low : low + LANES] = piece.astype(BF16)
    out_ref[...] = lax.dot_general(
        w_ref[...], picked[...], (((1,), (1,)), ((), ())), preferred_element_type=F32
    ).astype(BF16)


def act_kernel(in_ref, out_ref):
    up = in_ref[0].astype(F32)
    for part in range(1, in_ref.shape[0]):
        up = up + in_ref[part].astype(F32)
    out_ref[...] = (up / (1.0 + jnp.exp(-up))).astype(BF16)


def down_kernel(h_ref, w_ref, out_ref, rows, whole):
    columns = w_ref.shape[2]
    for y in range(4):
        for pair in range(2):
            low = (pair * 4 + y) * columns
            whole[low : low + columns] = w_ref[y, pair]
    for slot in (30, 31):
        rows[pl.ds(slot, 64, stride=SLOTS), :] = jnp.zeros((64, LANES), F32)
    out = lax.dot_general(
        h_ref[...], whole[...], (((0,), (1,)), ((), ())), preferred_element_type=F32
    )
    for i in range(5):
        for tile in range(6):
            rows[pl.ds(i * 6 + tile, 64, stride=SLOTS), :] = out[
                i * 64 : i * 64 + 64, tile * LANES : (tile + 1) * LANES
            ]
    for block in range(64):
        z, y = divmod(block, 4)
        out_ref[y * 16 + z] = rows[block * SLOTS : (block + 1) * SLOTS].astype(BF16)


def sum_kernel(in_ref, out_ref):
    total = in_ref[0:16].astype(F32)
    for part in range(1, 4):
        total = total + in_ref[part * 16 : part * 16 + 16].astype(F32)
    out_ref[...] = total.astype(BF16)


def weigh_kernel(place_ref, y_ref, row_ref, router_ref, out_ref):
    products = jnp.zeros((SLOTS, LANES), F32)
    own = place_ref[0] * 8
    for part in range(8):
        products = products + row_ref[own + part].astype(F32) * router_ref[part].astype(F32)
    one = lax.broadcasted_iota(jnp.int32, (SLOTS, SLOTS), 0) // 6
    two = lax.broadcasted_iota(jnp.int32, (SLOTS, SLOTS), 1) // 6
    alike = jnp.where(one == two, 1.0, 0.0)
    sums = jnp.dot(
        alike, products, preferred_element_type=F32, precision=lax.Precision.HIGHEST
    )
    gate = jax.nn.sigmoid(jnp.sum(sums, axis=-1, keepdims=True))
    for group in range(8):
        total = y_ref[group * 2].astype(F32) + y_ref[group * 2 + 1].astype(F32)
        out_ref[group] = (total * gate).astype(BF16)


def add_kernel(attn_ref, y_ref, sel_ref, out_ref, rows, weighted):
    length = attn_ref.shape[0]
    rows[...] = y_ref[...].astype(F32).reshape(8 * SLOTS, LANES)
    weighted[...] = jnp.zeros_like(weighted)
    for i in range(5):
        for tile in range(6):
            weighted[i * 8 : i * 8 + 8, tile * LANES : (tile + 1) * LANES] = rows[
                pl.ds(i * 6 + tile, 8, stride=SLOTS), :
            ]
    place = lax.broadcasted_iota(jnp.int32, (length, LANES), 0)
    chosen = jnp.where(place == sel_ref[...], 1.0, 0.0).astype(BF16)
    added = jnp.dot(chosen, weighted[...].astype(BF16), preferred_element_type=F32)
    out_ref[...] = (attn_ref[...].astype(F32) + added).astype(BF16)


def shape(dims, dtype=BF16):
    return jax.ShapeDtypeStruct(dims, dtype)


def in_hbm(array):
    return array if INTERPRET else pltpu.with_memory_space_constraint(array, HBM)


def body(queries, keys, values, selections, router, w_up, w_down):
    length, width = queries.shape
    parts = lax.axis_size("p")
    seq = ("r", "l", "y")
    units = w_up.shape[1]
    quarter = w_up.shape[2] // 4
    place = lax.axis_index("y").astype(jnp.int32)
    columns = w_down.shape[1]
    group = w_down.shape[2] // parts
    sel = selections[0].T.reshape(-1)
    sel_column = sel[:, None]
    sel_row = jnp.pad(sel, (0, LANES - sel.shape[0]), constant_values=-1)[None]
    router_rows = jnp.tile(router.reshape(parts, 6, LANES), (1, 5, 1))
    router_rows = jnp.pad(router_rows, ((0, 0), (0, SLOTS - 30), (0, 0)))

    state = call(
        state_kernel,
        shape((4, 144, LANES)),
        in_hbm(keys),
        in_hbm(values),
        scratch=[pltpu.VMEM((width, width), F32), pltpu.VMEM((4, 144, LANES), F32)],
        name="state",
    )
    quarters = lax.all_to_all(state, "y", 0, 0, tiled=True)
    quarters, queries, w_up, w_down = lax.optimization_barrier((quarters, queries, w_up, w_down))
    totals = call(
        total_kernel,
        shape((16, 16, LANES)),
        quarters,
        scratch=[pltpu.VMEM((152, LANES), F32)],
        name="total",
    )
    totals = lax.all_to_all(totals, ("r", "l"), 0, 0, tiled=True)
    inner = call(
        inner_kernel,
        shape((length, width), F32),
        in_hbm(queries),
        in_hbm(keys),
        in_hbm(values),
        name="inner",
    )
    up_cut = call(
        cut_up_kernel,
        shape((4, units, quarter)),
        w_up[0],
        scratch=[pltpu.SemaphoreType.DMA((4,))],
        spaces=([HBM], HBM),
        name="cut_up",
    )
    totals, inner, up_cut, w_down = lax.optimization_barrier((totals, inner, up_cut, w_down))
    bases = call(prefix_kernel, shape((16, 16, LANES)), totals, name="prefix")
    bases = lax.all_to_all(bases, ("r", "l"), 0, 0, tiled=True)
    pair = lax.axis_index("l").astype(jnp.int32).reshape(1)
    down_keep, down_one, down_two = call(
        cut_down_kernel,
        [HBM((n, columns, group), BF16) for n in (4, 2, 2)],
        pair,
        w_down[0],
        scratch=[pltpu.VMEM((8, columns, group), BF16), pltpu.SemaphoreType.DMA((8,))],
        spaces=([pltpu.SMEM, pltpu.VMEM], [HBM] * 3),
        name="cut_down",
    )
    bases, down_keep, down_one, down_two = lax.optimization_barrier(
        (bases, down_keep, down_one, down_two)
    )
    before = call(
        spread_kernel,
        shape((4, 144, LANES)),
        bases,
        quarters,
        scratch=[pltpu.VMEM((144, LANES), F32)],
        name="spread",
    )
    before, down_one = lax.optimization_barrier((before, down_one))
    before = lax.all_to_all(before, "y", 0, 0, tiled=True)
    down_one = lax.ppermute(down_one, "l", [(0, 1), (1, 0)])
    before, down_one, down_two = lax.optimization_barrier((before, down_one, down_two))
    attn, pay = call(
        attn_kernel,
        (pltpu.HBM((length, width), BF16), shape((32, SLOTS, LANES))),
        queries,
        inner,
        before,
        sel_column,
        scratch=[
            pltpu.VMEM((6 * HEAD, LANES), F32),
            pltpu.VMEM((width, width), BF16),
            pltpu.VMEM((length, width), F32),
            pltpu.VMEM((8 * SLOTS, LANES), F32),
        ],
        name="attn",
    )
    pay, down_two = lax.optimization_barrier((pay, down_two))
    down_two = lax.ppermute(down_two, "l", [(0, 1), (1, 0)])
    whole_rows = lax.all_to_all(pay, ("y", "p"), 0, 0, tiled=True)
    whole_rows, down_two = lax.optimization_barrier((whole_rows, down_two))
    near_rows = call(
        near_kernel,
        shape((240, LANES)),
        place.reshape(1),
        whole_rows,
        scratch=[pltpu.VMEM((240, LANES), F32)],
        spaces=([pltpu.SMEM, pltpu.VMEM], pltpu.VMEM),
        name="near",
    )
    near_rows, up_cut = lax.optimization_barrier((near_rows, up_cut))
    up_mine = lax.all_to_all(up_cut, "y", 0, 0, tiled=True).reshape(4 * units, quarter)
    arrived = lax.all_gather(near_rows, ("r", "l"), axis=0, tiled=True)
    partial = call(
        up_kernel,
        shape((4 * units, 384)),
        arrived,
        up_mine,
        scratch=[pltpu.VMEM((64 * 60, LANES), F32), pltpu.VMEM((384, quarter), BF16)],
        name="up",
    )
    partial, down_keep = lax.optimization_barrier((partial, down_keep))
    sums = lax.all_to_all(partial.reshape(4, units, 384), "y", 0, 0, tiled=True)
    down_cut = call(
        join_kernel,
        shape((4, 2, columns, group)),
        pair,
        in_hbm(down_keep),
        in_hbm(down_one),
        in_hbm(down_two),
        scratch=[pltpu.SemaphoreType.DMA((8,))],
        spaces=([pltpu.SMEM] + [HBM] * 3, HBM),
        name="join",
    )
    sums, down_cut = lax.optimization_barrier((sums, down_cut))
    act = call(act_kernel, shape((units, 384)), sums, name="act")
    act, down_cut = lax.optimization_barrier((act, down_cut))
    down_mine = lax.all_to_all(down_cut, "y", 0, 0, tiled=True)
    act = lax.all_gather(act, "r", axis=0, tiled=True)
    out = call(
        down_kernel,
        shape((64, SLOTS, LANES)),
        act,
        down_mine,
        scratch=[
            pltpu.VMEM((64 * SLOTS, LANES), F32),
            pltpu.VMEM((8 * columns, group), BF16),
        ],
        name="down",
    )
    back = lax.all_to_all(out, "y", 0, 0, tiled=True)
    back = call(sum_kernel, shape((16, SLOTS, LANES)), back, name="sum")
    back = lax.all_to_all(back, ("r", "l"), 0, 0, tiled=True)
    weighted = call(
        weigh_kernel,
        shape((8, SLOTS, LANES)),
        place.reshape(1),
        back,
        whole_rows,
        router_rows,
        spaces=([pltpu.SMEM] + [pltpu.VMEM] * 3, pltpu.VMEM),
        name="weigh",
    )
    weighted = lax.all_to_all(weighted, "p", 0, 0, tiled=True)
    return call(
        add_kernel,
        shape((length, width)),
        attn,
        weighted,
        sel_row,
        scratch=[pltpu.VMEM((8 * SLOTS, LANES), F32), pltpu.VMEM((LANES, width), F32)],
        name="add",
    )


def solution(mesh):
    split = Mesh(mesh.devices.reshape(8, 2, 4, 8), ("r", "l", "y", "p"))
    seq = ("r", "l", "y")
    placed = (
        P(seq, "p"),
        P(seq, "p"),
        P(seq, "p"),
        P(seq, None, None),
        P(None, "p"),
        P("p", seq, None),
        P("p", seq, None),
    )
    return jax.shard_map(
        body, mesh=split, in_specs=placed, out_specs=P(seq, "p"), check_vma=False
    )
```

```python
import jax
import jax.numpy as jnp
from jax import lax
from jax.experimental import pallas as pl
from jax.experimental.pallas import tpu as pltpu
from jax.sharding import Mesh, PartitionSpec as P

HEAD = 96
LANES = 128
SLOTS = 32
INTERPRET = False
BF16 = jnp.bfloat16
F32 = jnp.float32


HBM = pltpu.HBM


def call(kernel, out, *args, scratch=(), spaces=None, name=None):
    specs = {}
    if spaces:
        ins, outs = spaces
        specs["in_specs"] = [pl.BlockSpec(memory_space=space) for space in ins]
        specs["out_specs"] = (
            [pl.BlockSpec(memory_space=space) for space in outs]
            if isinstance(outs, list)
            else pl.BlockSpec(memory_space=outs)
        )
    return pl.pallas_call(
        kernel,
        out_shape=out,
        scratch_shapes=list(scratch),
        compiler_params=pltpu.CompilerParams(vmem_limit_bytes=16 * 2**20),
        interpret=INTERPRET,
        name=name,
        **specs,
    )(*args)


def tile_heads(tile):
    first = tile * LANES // HEAD
    return first, (first + 1) * HEAD - tile * LANES


def head_window(head):
    first, last = head * HEAD // LANES, (head * HEAD + HEAD - 1) // LANES
    return first * LANES, (last + 1) * LANES, head * HEAD - first * LANES


def state_kernel(k_ref, v_ref, out_ref, grand, rows):
    grand[...] = lax.dot_general(
        k_ref[...], v_ref[...], (((0,), (0,)), ((), ())), preferred_element_type=F32
    )
    lane = lax.broadcasted_iota(jnp.int32, (HEAD, LANES), 1)
    for tile in range(6):
        head, split = tile_heads(tile)
        at = slice(tile * LANES, (tile + 1) * LANES)
        one = grand[head * HEAD : (head + 1) * HEAD, at]
        two = grand[(head + 1) * HEAD : (head + 2) * HEAD, at]
        block = jnp.where(lane < split, one, two)
        for quarter in range(4):
            rows[quarter, tile * 24 : tile * 24 + 24] = block[quarter * 24 : quarter * 24 + 24]
    out_ref[...] = rows[...].astype(BF16)


def total_kernel(in_ref, out_ref, rows):
    total = in_ref[0].astype(F32)
    for y in range(1, 4):
        total = total + in_ref[y].astype(F32)
    rows[0:144] = total
    rows[144:152] = jnp.zeros((8, LANES), F32)
    for z in range(16):
        out_ref[z] = rows[z * 9 : z * 9 + 16].astype(BF16)


def prefix_kernel(in_ref, out_ref):
    total = jnp.zeros((16, LANES), F32)
    for z in range(16):
        out_ref[z] = total.astype(BF16)
        total = total + in_ref[z].astype(F32)


def spread_kernel(base_ref, in_ref, out_ref, rows):
    for z in range(16):
        rows[z * 9 : z * 9 + 9] = base_ref[z].astype(F32)[0:9]
    total = rows[...]
    for y in range(4):
        out_ref[y] = total.astype(BF16)
        total = total + in_ref[y].astype(F32)


def inner_kernel(q_ref, k_ref, v_ref, out_ref):
    length = q_ref.shape[0]
    out_ref[...] = jnp.zeros_like(out_ref)
    below = lax.broadcasted_iota(jnp.int32, (length, length), 0) >= lax.broadcasted_iota(
        jnp.int32, (length, length), 1
    )
    for head in range(8):
        start, stop, low = head_window(head)
        lane = lax.broadcasted_iota(jnp.int32, (1, stop - start), 1)
        mine = (lane >= low) & (lane < low + HEAD)
        q = q_ref[:, start:stop] * mine.astype(F32).astype(BF16)
        scores = lax.dot_general(
            q, k_ref[:, start:stop], (((1,), (1,)), ((), ())), preferred_element_type=F32
        )
        scores = jnp.where(below, scores, 0.0).astype(BF16)
        mixed = jnp.dot(scores, v_ref[:, start:stop], preferred_element_type=F32)
        out_ref[:, start:stop] = jnp.where(mine, mixed, out_ref[:, start:stop])


def attn_kernel(q_ref, inner_ref, p_ref, sel_ref, attn_ref, pay_ref, rows, wide, normed, picks):
    length = q_ref.shape[0]
    for quarter in range(4):
        part = p_ref[quarter].astype(F32)
        for tile in range(6):
            low = tile * HEAD + quarter * 24
            rows[low : low + 24] = part[tile * 24 : tile * 24 + 24]
    wide[...] = jnp.zeros_like(wide)
    lane = lax.broadcasted_iota(jnp.int32, (HEAD, LANES), 1)
    for tile in range(6):
        head, split = tile_heads(tile)
        at = slice(tile * LANES, (tile + 1) * LANES)
        block = rows[tile * HEAD : (tile + 1) * HEAD]
        low = head * HEAD
        wide[low : low + HEAD, at] = jnp.where(lane < split, block, 0.0).astype(BF16)
        low = low + HEAD
        wide[low : low + HEAD, at] = jnp.where(lane < split, 0.0, block).astype(BF16)
    normed[...] = inner_ref[...] + jnp.dot(q_ref[...], wide[...], preferred_element_type=F32)
    for head in range(8):
        start, stop, low = head_window(head)
        lane = lax.broadcasted_iota(jnp.int32, (1, stop - start), 1)
        mine = (lane >= low) & (lane < low + HEAD)
        mixed = normed[:, start:stop]
        power = jnp.sum(jnp.where(mine, mixed * mixed, 0.0), axis=-1, keepdims=True) / HEAD
        normed[:, start:stop] = jnp.where(mine, mixed * lax.rsqrt(power + 1e-06), mixed)
    attn = normed[...].astype(BF16)
    attn_ref[...] = attn
    place = lax.broadcasted_iota(jnp.int32, (40, length), 1)
    chosen = jnp.where(place == sel_ref[...], 1.0, 0.0).astype(BF16)
    picked = jnp.dot(chosen, attn, preferred_element_type=F32)
    picks[...] = jnp.zeros_like(picks)
    for i in range(5):
        for tile in range(6):
            picks[pl.ds(i * 6 + tile, 8, stride=SLOTS), :] = picked[
                i * 8 : i * 8 + 8, tile * LANES : (tile + 1) * LANES
            ]
    pay = picks[...].reshape(8, SLOTS, LANES).astype(BF16)
    for y in range(4):
        pay_ref[y * 8 : y * 8 + 8] = pay


def cut_up_kernel(w_ref, out_ref, sems):
    parts, width = out_ref.shape[0], out_ref.shape[2]
    copies = []
    for part in range(parts):
        source = w_ref.at[:, part * width : (part + 1) * width]
        copies.append(pltpu.make_async_copy(source, out_ref.at[part], sems.at[part]))
        copies[-1].start()
    for copy in copies:
        copy.wait()


def cut_down_kernel(place_ref, w_ref, keep_ref, one_ref, two_ref, cut, sems):
    run = w_ref.shape[1] // 64
    for part in range(8):
        for group in range(8):
            low = (group * 8 + part) * run
            cut[part, :, group * run : (group + 1) * run] = w_ref[:, low : low + run]
    own = place_ref[0] * 4
    other = 4 - own
    copies = []
    for n in range(4):
        away = (one_ref, two_ref)[n // 2].at[n % 2]
        copies.append(pltpu.make_async_copy(cut.at[own + n], keep_ref.at[n], sems.at[n]))
        copies.append(pltpu.make_async_copy(cut.at[other + n], away, sems.at[4 + n]))
    for copy in copies:
        copy.start()
    for copy in copies:
        copy.wait()


def join_kernel(place_ref, keep_ref, one_ref, two_ref, out_ref):
    own = place_ref[0]
    for n in range(4):
        out_ref[n, own] = keep_ref[n]
        out_ref[n, 1 - own] = (one_ref, two_ref)[n // 2][n % 2]


def near_kernel(place_ref, row_ref, out_ref, rows):
    for block in range(4):
        for part in range(2):
            low = (block * 2 + part) * 30
            piece = row_ref[block * 8 + 2 * place_ref[0] + part].astype(F32)
            rows[low : low + 30] = piece[:30]
    out_ref[...] = rows[...].astype(BF16)


def up_kernel(x_ref, w_ref, out_ref, rows, picked):
    rows[...] = x_ref[...].astype(F32)
    picked[320:] = jnp.zeros((64, picked.shape[1]), BF16)
    for i in range(5):
        for part in range(2):
            for tile in range(6):
                piece = rows[pl.ds(part * 30 + i * 6 + tile, 64, stride=60), :]
                low = (part * 6 + tile) * LANES
                picked[i * 64 : i * 64 + 64, low : low + LANES] = piece.astype(BF16)
    out_ref[...] = lax.dot_general(
        w_ref[...], picked[...], (((1,), (1,)), ((), ())), preferred_element_type=F32
    ).astype(BF16)


def act_kernel(in_ref, out_ref):
    up = in_ref[0].astype(F32)
    for part in range(1, in_ref.shape[0]):
        up = up + in_ref[part].astype(F32)
    out_ref[...] = (up / (1.0 + jnp.exp(-up))).astype(BF16)


def down_kernel(h_ref, w_ref, out_ref, rows, whole):
    columns = w_ref.shape[2]
    for y in range(4):
        for pair in range(2):
            low = (pair * 4 + y) * columns
            whole[low : low + columns] = w_ref[y, pair]
    for slot in (30, 31):
        rows[pl.ds(slot, 64, stride=SLOTS), :] = jnp.zeros((64, LANES), F32)
    out = lax.dot_general(
        h_ref[...], whole[...], (((0,), (1,)), ((), ())), preferred_element_type=F32
    )
    for i in range(5):
        for tile in range(6):
            rows[pl.ds(i * 6 + tile, 64, stride=SLOTS), :] = out[
                i * 64 : i * 64 + 64, tile * LANES : (tile + 1) * LANES
            ]
    for block in range(64):
        z, y = divmod(block, 4)
        out_ref[y * 16 + z] = rows[block * SLOTS : (block + 1) * SLOTS].astype(BF16)


def sum_kernel(in_ref, out_ref):
    total = in_ref[0:16].astype(F32)
    for part in range(1, 4):
        total = total + in_ref[part * 16 : part * 16 + 16].astype(F32)
    out_ref[...] = total.astype(BF16)


def weigh_kernel(place_ref, y_ref, row_ref, router_ref, out_ref):
    products = jnp.zeros((SLOTS, LANES), F32)
    own = place_ref[0] * 8
    for part in range(8):
        products = products + row_ref[own + part].astype(F32) * router_ref[part].astype(F32)
    one = lax.broadcasted_iota(jnp.int32, (SLOTS, SLOTS), 0) // 6
    two = lax.broadcasted_iota(jnp.int32, (SLOTS, SLOTS), 1) // 6
    alike = jnp.where(one == two, 1.0, 0.0)
    sums = jnp.dot(
        alike, products, preferred_element_type=F32, precision=lax.Precision.HIGHEST
    )
    gate = jax.nn.sigmoid(jnp.sum(sums, axis=-1, keepdims=True))
    for group in range(8):
        total = y_ref[group * 2].astype(F32) + y_ref[group * 2 + 1].astype(F32)
        out_ref[group] = (total * gate).astype(BF16)


def add_kernel(attn_ref, y_ref, sel_ref, out_ref, rows, weighted):
    length = attn_ref.shape[0]
    rows[...] = y_ref[...].astype(F32).reshape(8 * SLOTS, LANES)
    weighted[...] = jnp.zeros_like(weighted)
    for i in range(5):
        for tile in range(6):
            weighted[i * 8 : i * 8 + 8, tile * LANES : (tile + 1) * LANES] = rows[
                pl.ds(i * 6 + tile, 8, stride=SLOTS), :
            ]
    place = lax.broadcasted_iota(jnp.int32, (length, LANES), 0)
    chosen = jnp.where(place == sel_ref[...], 1.0, 0.0).astype(BF16)
    added = jnp.dot(chosen, weighted[...].astype(BF16), preferred_element_type=F32)
    out_ref[...] = (attn_ref[...].astype(F32) + added).astype(BF16)


def shape(dims, dtype=BF16):
    return jax.ShapeDtypeStruct(dims, dtype)


def in_hbm(array):
    return array if INTERPRET else pltpu.with_memory_space_constraint(array, HBM)


def body(queries, keys, values, selections, router, w_up, w_down):
    length, width = queries.shape
    parts = lax.axis_size("p")
    seq = ("r", "l", "y")
    units = w_up.shape[1]
    quarter = w_up.shape[2] // 4
    place = lax.axis_index("y").astype(jnp.int32)
    columns = w_down.shape[1]
    group = w_down.shape[2] // parts
    sel = selections[0].T.reshape(-1)
    sel_column = sel[:, None]
    sel_row = jnp.pad(sel, (0, LANES - sel.shape[0]), constant_values=-1)[None]
    router_rows = jnp.tile(router.reshape(parts, 6, LANES), (1, 5, 1))
    router_rows = jnp.pad(router_rows, ((0, 0), (0, SLOTS - 30), (0, 0)))

    state = call(
        state_kernel,
        shape((4, 144, LANES)),
        in_hbm(keys),
        in_hbm(values),
        scratch=[pltpu.VMEM((width, width), F32), pltpu.VMEM((4, 144, LANES), F32)],
        name="state",
    )
    quarters = lax.all_to_all(state, "y", 0, 0, tiled=True)
    quarters, queries, w_up, w_down = lax.optimization_barrier((quarters, queries, w_up, w_down))
    totals = call(
        total_kernel,
        shape((16, 16, LANES)),
        quarters,
        scratch=[pltpu.VMEM((152, LANES), F32)],
        name="total",
    )
    totals = lax.all_to_all(totals, ("r", "l"), 0, 0, tiled=True)
    inner = call(
        inner_kernel,
        shape((length, width), F32),
        in_hbm(queries),
        in_hbm(keys),
        in_hbm(values),
        name="inner",
    )
    up_cut = call(
        cut_up_kernel,
        shape((4, units, quarter)),
        w_up[0],
        scratch=[pltpu.SemaphoreType.DMA((4,))],
        spaces=([HBM], HBM),
        name="cut_up",
    )
    totals, inner, up_cut, w_down = lax.optimization_barrier((totals, inner, up_cut, w_down))
    bases = call(prefix_kernel, shape((16, 16, LANES)), totals, name="prefix")
    bases = lax.all_to_all(bases, ("r", "l"), 0, 0, tiled=True)
    pair = lax.axis_index("l").astype(jnp.int32).reshape(1)
    down_keep, down_one, down_two = call(
        cut_down_kernel,
        [HBM((n, columns, group), BF16) for n in (4, 2, 2)],
        pair,
        w_down[0],
        scratch=[pltpu.VMEM((8, columns, group), BF16), pltpu.SemaphoreType.DMA((8,))],
        spaces=([pltpu.SMEM, pltpu.VMEM], [HBM] * 3),
        name="cut_down",
    )
    bases, down_keep, down_one, down_two = lax.optimization_barrier(
        (bases, down_keep, down_one, down_two)
    )
    before = call(
        spread_kernel,
        shape((4, 144, LANES)),
        bases,
        quarters,
        scratch=[pltpu.VMEM((144, LANES), F32)],
        name="spread",
    )
    before, down_one = lax.optimization_barrier((before, down_one))
    before = lax.all_to_all(before, "y", 0, 0, tiled=True)
    down_one = lax.ppermute(down_one, "l", [(0, 1), (1, 0)])
    before, down_one, down_two = lax.optimization_barrier((before, down_one, down_two))
    attn, pay = call(
        attn_kernel,
        (pltpu.HBM((length, width), BF16), shape((32, SLOTS, LANES))),
        queries,
        inner,
        before,
        sel_column,
        scratch=[
            pltpu.VMEM((6 * HEAD, LANES), F32),
            pltpu.VMEM((width, width), BF16),
            pltpu.VMEM((length, width), F32),
            pltpu.VMEM((8 * SLOTS, LANES), F32),
        ],
        name="attn",
    )
    pay, down_two = lax.optimization_barrier((pay, down_two))
    down_two = lax.ppermute(down_two, "l", [(0, 1), (1, 0)])
    whole_rows = lax.all_to_all(pay, ("y", "p"), 0, 0, tiled=True)
    whole_rows, down_two = lax.optimization_barrier((whole_rows, down_two))
    near_rows = call(
        near_kernel,
        shape((240, LANES)),
        place.reshape(1),
        whole_rows,
        scratch=[pltpu.VMEM((240, LANES), F32)],
        spaces=([pltpu.SMEM, pltpu.VMEM], pltpu.VMEM),
        name="near",
    )
    near_rows, up_cut = lax.optimization_barrier((near_rows, up_cut))
    up_mine = lax.all_to_all(up_cut, "y", 0, 0, tiled=True).reshape(4 * units, quarter)
    arrived = lax.all_gather(near_rows, ("r", "l"), axis=0, tiled=True)
    partial = call(
        up_kernel,
        shape((4 * units, 384)),
        arrived,
        up_mine,
        scratch=[pltpu.VMEM((64 * 60, LANES), F32), pltpu.VMEM((384, quarter), BF16)],
        name="up",
    )
    partial, down_keep = lax.optimization_barrier((partial, down_keep))
    sums = lax.all_to_all(partial.reshape(4, units, 384), "y", 0, 0, tiled=True)
    down_cut = call(
        join_kernel,
        shape((4, 2, columns, group)),
        pair,
        down_keep,
        down_one,
        down_two,
        spaces=([pltpu.SMEM] + [pltpu.VMEM] * 3, pltpu.VMEM),
        name="join",
    )
    sums, down_cut = lax.optimization_barrier((sums, down_cut))
    act = call(act_kernel, shape((units, 384)), sums, name="act")
    act, down_cut = lax.optimization_barrier((act, down_cut))
    down_mine = lax.all_to_all(down_cut, "y", 0, 0, tiled=True)
    act = lax.all_gather(act, "r", axis=0, tiled=True)
    out = call(
        down_kernel,
        shape((64, SLOTS, LANES)),
        act,
        down_mine,
        scratch=[
            pltpu.VMEM((64 * SLOTS, LANES), F32),
            pltpu.VMEM((8 * columns, group), BF16),
        ],
        name="down",
    )
    back = lax.all_to_all(out, "y", 0, 0, tiled=True)
    back = call(sum_kernel, shape((16, SLOTS, LANES)), back, name="sum")
    back = lax.all_to_all(back, ("r", "l"), 0, 0, tiled=True)
    weighted = call(
        weigh_kernel,
        shape((8, SLOTS, LANES)),
        place.reshape(1),
        back,
        whole_rows,
        router_rows,
        spaces=([pltpu.SMEM] + [pltpu.VMEM] * 3, pltpu.VMEM),
        name="weigh",
    )
    weighted = lax.all_to_all(weighted, "p", 0, 0, tiled=True)
    return call(
        add_kernel,
        shape((length, width)),
        attn,
        weighted,
        sel_row,
        scratch=[pltpu.VMEM((8 * SLOTS, LANES), F32), pltpu.VMEM((LANES, width), F32)],
        name="add",
    )


def solution(mesh):
    split = Mesh(mesh.devices.reshape(8, 2, 4, 8), ("r", "l", "y", "p"))
    seq = ("r", "l", "y")
    placed = (
        P(seq, "p"),
        P(seq, "p"),
        P(seq, "p"),
        P(seq, None, None),
        P(None, "p"),
        P("p", seq, None),
        P("p", seq, None),
    )
    return jax.shard_map(
        body, mesh=split, in_specs=placed, out_specs=P(seq, "p"), check_vma=False
    )
```

```python
import jax
import jax.numpy as jnp
from jax import lax
from jax.experimental import pallas as pl
from jax.experimental.pallas import tpu as pltpu
from jax.sharding import Mesh, PartitionSpec as P

HEAD = 96
LANES = 128
SLOTS = 32
INTERPRET = False
BF16 = jnp.bfloat16
F32 = jnp.float32


HBM = pltpu.HBM


def call(kernel, out, *args, scratch=(), spaces=None, name=None):
    specs = {}
    if spaces:
        ins, outs = spaces
        specs["in_specs"] = [pl.BlockSpec(memory_space=space) for space in ins]
        specs["out_specs"] = (
            [pl.BlockSpec(memory_space=space) for space in outs]
            if isinstance(outs, list)
            else pl.BlockSpec(memory_space=outs)
        )
    return pl.pallas_call(
        kernel,
        out_shape=out,
        scratch_shapes=list(scratch),
        compiler_params=pltpu.CompilerParams(vmem_limit_bytes=16 * 2**20),
        interpret=INTERPRET,
        name=name,
        **specs,
    )(*args)


def tile_heads(tile):
    first = tile * LANES // HEAD
    return first, (first + 1) * HEAD - tile * LANES


def head_window(head):
    first, last = head * HEAD // LANES, (head * HEAD + HEAD - 1) // LANES
    return first * LANES, (last + 1) * LANES, head * HEAD - first * LANES


def state_kernel(k_ref, v_ref, out_ref, grand, rows):
    grand[...] = lax.dot_general(
        k_ref[...], v_ref[...], (((0,), (0,)), ((), ())), preferred_element_type=F32
    )
    lane = lax.broadcasted_iota(jnp.int32, (HEAD, LANES), 1)
    for tile in range(6):
        head, split = tile_heads(tile)
        at = slice(tile * LANES, (tile + 1) * LANES)
        one = grand[head * HEAD : (head + 1) * HEAD, at]
        two = grand[(head + 1) * HEAD : (head + 2) * HEAD, at]
        block = jnp.where(lane < split, one, two)
        for quarter in range(4):
            rows[quarter, tile * 24 : tile * 24 + 24] = block[quarter * 24 : quarter * 24 + 24]
    out_ref[...] = rows[...].astype(BF16)


def total_kernel(in_ref, out_ref):
    total = in_ref[0].astype(F32)
    for y in range(1, 4):
        total = total + in_ref[y].astype(F32)
    out_ref[...] = total.astype(BF16)


def spread_kernel(place_ref, all_ref, in_ref, out_ref):
    total = jnp.zeros((144, LANES), F32)
    for z in range(16):
        row = all_ref[z * 144 : z * 144 + 144].astype(F32)
        total = total + jnp.where(z < place_ref[0], row, 0.0)
    for y in range(4):
        out_ref[y] = total.astype(BF16)
        total = total + in_ref[y].astype(F32)


def inner_kernel(q_ref, k_ref, v_ref, out_ref):
    length = q_ref.shape[0]
    out_ref[...] = jnp.zeros_like(out_ref)
    below = lax.broadcasted_iota(jnp.int32, (length, length), 0) >= lax.broadcasted_iota(
        jnp.int32, (length, length), 1
    )
    for head in range(8):
        start, stop, low = head_window(head)
        lane = lax.broadcasted_iota(jnp.int32, (1, stop - start), 1)
        mine = (lane >= low) & (lane < low + HEAD)
        q = q_ref[:, start:stop] * mine.astype(F32).astype(BF16)
        scores = lax.dot_general(
            q, k_ref[:, start:stop], (((1,), (1,)), ((), ())), preferred_element_type=F32
        )
        scores = jnp.where(below, scores, 0.0).astype(BF16)
        mixed = jnp.dot(scores, v_ref[:, start:stop], preferred_element_type=F32)
        out_ref[:, start:stop] = jnp.where(mine, mixed, out_ref[:, start:stop])


def attn_kernel(q_ref, inner_ref, p_ref, sel_ref, attn_ref, pay_ref, rows, wide, normed, picks):
    length = q_ref.shape[0]
    for quarter in range(4):
        part = p_ref[quarter].astype(F32)
        for tile in range(6):
            low = tile * HEAD + quarter * 24
            rows[low : low + 24] = part[tile * 24 : tile * 24 + 24]
    wide[...] = jnp.zeros_like(wide)
    lane = lax.broadcasted_iota(jnp.int32, (HEAD, LANES), 1)
    for tile in range(6):
        head, split = tile_heads(tile)
        at = slice(tile * LANES, (tile + 1) * LANES)
        block = rows[tile * HEAD : (tile + 1) * HEAD]
        low = head * HEAD
        wide[low : low + HEAD, at] = jnp.where(lane < split, block, 0.0).astype(BF16)
        low = low + HEAD
        wide[low : low + HEAD, at] = jnp.where(lane < split, 0.0, block).astype(BF16)
    normed[...] = inner_ref[...] + jnp.dot(q_ref[...], wide[...], preferred_element_type=F32)
    for head in range(8):
        start, stop, low = head_window(head)
        lane = lax.broadcasted_iota(jnp.int32, (1, stop - start), 1)
        mine = (lane >= low) & (lane < low + HEAD)
        mixed = normed[:, start:stop]
        power = jnp.sum(jnp.where(mine, mixed * mixed, 0.0), axis=-1, keepdims=True) / HEAD
        normed[:, start:stop] = jnp.where(mine, mixed * lax.rsqrt(power + 1e-06), mixed)
    attn = normed[...].astype(BF16)
    attn_ref[...] = attn
    place = lax.broadcasted_iota(jnp.int32, (40, length), 1)
    chosen = jnp.where(place == sel_ref[...], 1.0, 0.0).astype(BF16)
    picked = jnp.dot(chosen, attn, preferred_element_type=F32)
    picks[...] = jnp.zeros_like(picks)
    for i in range(5):
        for tile in range(6):
            picks[pl.ds(i * 6 + tile, 8, stride=SLOTS), :] = picked[
                i * 8 : i * 8 + 8, tile * LANES : (tile + 1) * LANES
            ]
    pay = picks[...].reshape(8, SLOTS, LANES).astype(BF16)
    for y in range(4):
        pay_ref[y * 8 : y * 8 + 8] = pay


def cut_up_kernel(w_ref, out_ref, sems):
    parts, width = out_ref.shape[0], out_ref.shape[2]
    copies = []
    for part in range(parts):
        source = w_ref.at[:, part * width : (part + 1) * width]
        copies.append(pltpu.make_async_copy(source, out_ref.at[part], sems.at[part]))
        copies[-1].start()
    for copy in copies:
        copy.wait()


def cut_down_kernel(place_ref, w_ref, keep_ref, one_ref, two_ref, cut, sems):
    run = w_ref.shape[1] // 64
    for part in range(8):
        for group in range(8):
            low = (group * 8 + part) * run
            cut[part, :, group * run : (group + 1) * run] = w_ref[:, low : low + run]
    own = place_ref[0] * 4
    other = 4 - own
    copies = []
    for n in range(4):
        away = (one_ref, two_ref)[n // 2].at[n % 2]
        copies.append(pltpu.make_async_copy(cut.at[own + n], keep_ref.at[n], sems.at[n]))
        copies.append(pltpu.make_async_copy(cut.at[other + n], away, sems.at[4 + n]))
    for copy in copies:
        copy.start()
    for copy in copies:
        copy.wait()


def join_kernel(place_ref, keep_ref, one_ref, two_ref, out_ref):
    own = place_ref[0]
    for n in range(4):
        out_ref[n, own] = keep_ref[n]
        out_ref[n, 1 - own] = (one_ref, two_ref)[n // 2][n % 2]


def near_kernel(place_ref, row_ref, out_ref, rows):
    for block in range(4):
        for part in range(2):
            low = (block * 2 + part) * 30
            piece = row_ref[block * 8 + 2 * place_ref[0] + part].astype(F32)
            rows[low : low + 30] = piece[:30]
    out_ref[...] = rows[...].astype(BF16)


def up_kernel(x_ref, w_ref, out_ref, rows, picked):
    rows[...] = x_ref[...].astype(F32)
    picked[320:] = jnp.zeros((64, picked.shape[1]), BF16)
    for i in range(5):
        for part in range(2):
            for tile in range(6):
                piece = rows[pl.ds(part * 30 + i * 6 + tile, 64, stride=60), :]
                low = (part * 6 + tile) * LANES
                picked[i * 64 : i * 64 + 64, low : low + LANES] = piece.astype(BF16)
    out_ref[...] = lax.dot_general(
        w_ref[...], picked[...], (((1,), (1,)), ((), ())), preferred_element_type=F32
    ).astype(BF16)


def act_kernel(in_ref, out_ref):
    up = in_ref[0].astype(F32)
    for part in range(1, in_ref.shape[0]):
        up = up + in_ref[part].astype(F32)
    out_ref[...] = (up / (1.0 + jnp.exp(-up))).astype(BF16)


def down_kernel(h_ref, w_ref, out_ref, rows, whole):
    columns = w_ref.shape[2]
    for y in range(4):
        for pair in range(2):
            low = (pair * 4 + y) * columns
            whole[low : low + columns] = w_ref[y, pair]
    for slot in (30, 31):
        rows[pl.ds(slot, 64, stride=SLOTS), :] = jnp.zeros((64, LANES), F32)
    out = lax.dot_general(
        h_ref[...], whole[...], (((0,), (1,)), ((), ())), preferred_element_type=F32
    )
    for i in range(5):
        for tile in range(6):
            rows[pl.ds(i * 6 + tile, 64, stride=SLOTS), :] = out[
                i * 64 : i * 64 + 64, tile * LANES : (tile + 1) * LANES
            ]
    for block in range(64):
        z, y = divmod(block, 4)
        out_ref[y * 16 + z] = rows[block * SLOTS : (block + 1) * SLOTS].astype(BF16)


def sum_kernel(in_ref, out_ref):
    total = in_ref[0:16].astype(F32)
    for part in range(1, 4):
        total = total + in_ref[part * 16 : part * 16 + 16].astype(F32)
    out_ref[...] = total.astype(BF16)


def weigh_kernel(place_ref, y_ref, row_ref, router_ref, out_ref):
    products = jnp.zeros((SLOTS, LANES), F32)
    own = place_ref[0] * 8
    for part in range(8):
        products = products + row_ref[own + part].astype(F32) * router_ref[part].astype(F32)
    one = lax.broadcasted_iota(jnp.int32, (SLOTS, SLOTS), 0) // 6
    two = lax.broadcasted_iota(jnp.int32, (SLOTS, SLOTS), 1) // 6
    alike = jnp.where(one == two, 1.0, 0.0)
    sums = jnp.dot(
        alike, products, preferred_element_type=F32, precision=lax.Precision.HIGHEST
    )
    gate = jax.nn.sigmoid(jnp.sum(sums, axis=-1, keepdims=True))
    for group in range(8):
        total = y_ref[group * 2].astype(F32) + y_ref[group * 2 + 1].astype(F32)
        out_ref[group] = (total * gate).astype(BF16)


def add_kernel(attn_ref, y_ref, sel_ref, out_ref, rows, weighted):
    length = attn_ref.shape[0]
    rows[...] = y_ref[...].astype(F32).reshape(8 * SLOTS, LANES)
    weighted[...] = jnp.zeros_like(weighted)
    for i in range(5):
        for tile in range(6):
            weighted[i * 8 : i * 8 + 8, tile * LANES : (tile + 1) * LANES] = rows[
                pl.ds(i * 6 + tile, 8, stride=SLOTS), :
            ]
    place = lax.broadcasted_iota(jnp.int32, (length, LANES), 0)
    chosen = jnp.where(place == sel_ref[...], 1.0, 0.0).astype(BF16)
    added = jnp.dot(chosen, weighted[...].astype(BF16), preferred_element_type=F32)
    out_ref[...] = (attn_ref[...].astype(F32) + added).astype(BF16)


def shape(dims, dtype=BF16):
    return jax.ShapeDtypeStruct(dims, dtype)


def in_hbm(array):
    return array if INTERPRET else pltpu.with_memory_space_constraint(array, HBM)


def body(queries, keys, values, selections, router, w_up, w_down):
    length, width = queries.shape
    parts = lax.axis_size("p")
    seq = ("r", "l", "y")
    units = w_up.shape[1]
    quarter = w_up.shape[2] // 4
    place = lax.axis_index("y").astype(jnp.int32)
    columns = w_down.shape[1]
    group = w_down.shape[2] // parts
    sel = selections[0].T.reshape(-1)
    sel_column = sel[:, None]
    sel_row = jnp.pad(sel, (0, LANES - sel.shape[0]), constant_values=-1)[None]
    router_rows = jnp.tile(router.reshape(parts, 6, LANES), (1, 5, 1))
    router_rows = jnp.pad(router_rows, ((0, 0), (0, SLOTS - 30), (0, 0)))

    state = call(
        state_kernel,
        shape((4, 144, LANES)),
        in_hbm(keys),
        in_hbm(values),
        scratch=[pltpu.VMEM((width, width), F32), pltpu.VMEM((4, 144, LANES), F32)],
        name="state",
    )
    w_down, state = lax.optimization_barrier((w_down, state))
    quarters = lax.all_to_all(state, "y", 0, 0, tiled=True)
    pair = lax.axis_index("l").astype(jnp.int32).reshape(1)
    down_keep, down_one, down_two = call(
        cut_down_kernel,
        [HBM((n, columns, group), BF16) for n in (4, 2, 2)],
        pair,
        w_down[0],
        scratch=[pltpu.VMEM((8, columns, group), BF16), pltpu.SemaphoreType.DMA((8,))],
        spaces=([pltpu.SMEM, pltpu.VMEM], [HBM] * 3),
        name="cut_down",
    )
    quarters, down_keep, down_one, down_two = lax.optimization_barrier(
        (quarters, down_keep, down_one, down_two)
    )
    totals = call(total_kernel, shape((144, LANES)), quarters, name="total")
    totals = lax.all_gather(totals, ("r", "l"), axis=0, tiled=True)
    height = (lax.axis_index("r") * 2 + lax.axis_index("l")).astype(jnp.int32).reshape(1)
    before = call(
        spread_kernel,
        shape((4, 144, LANES)),
        height,
        totals,
        quarters,
        spaces=([pltpu.SMEM, pltpu.VMEM, pltpu.VMEM], pltpu.VMEM),
        name="spread",
    )
    before, down_one, queries, w_up = lax.optimization_barrier((before, down_one, queries, w_up))
    before = lax.all_to_all(before, "y", 0, 0, tiled=True)
    down_one = lax.ppermute(down_one, "l", [(0, 1), (1, 0)])
    inner = call(
        inner_kernel,
        shape((length, width), F32),
        in_hbm(queries),
        in_hbm(keys),
        in_hbm(values),
        name="inner",
    )
    up_cut = call(
        cut_up_kernel,
        shape((4, units, quarter)),
        w_up[0],
        scratch=[pltpu.SemaphoreType.DMA((4,))],
        spaces=([HBM], HBM),
        name="cut_up",
    )
    before, down_one, down_two, inner, up_cut = lax.optimization_barrier(
        (before, down_one, down_two, inner, up_cut)
    )
    attn, pay = call(
        attn_kernel,
        (pltpu.HBM((length, width), BF16), shape((32, SLOTS, LANES))),
        queries,
        inner,
        before,
        sel_column,
        scratch=[
            pltpu.VMEM((6 * HEAD, LANES), F32),
            pltpu.VMEM((width, width), BF16),
            pltpu.VMEM((length, width), F32),
            pltpu.VMEM((8 * SLOTS, LANES), F32),
        ],
        name="attn",
    )
    pay, down_two = lax.optimization_barrier((pay, down_two))
    down_two = lax.ppermute(down_two, "l", [(0, 1), (1, 0)])
    whole_rows = lax.all_to_all(pay, ("y", "p"), 0, 0, tiled=True)
    whole_rows, down_two = lax.optimization_barrier((whole_rows, down_two))
    near_rows = call(
        near_kernel,
        shape((240, LANES)),
        place.reshape(1),
        whole_rows,
        scratch=[pltpu.VMEM((240, LANES), F32)],
        spaces=([pltpu.SMEM, pltpu.VMEM], pltpu.VMEM),
        name="near",
    )
    near_rows, up_cut = lax.optimization_barrier((near_rows, up_cut))
    up_mine = lax.all_to_all(up_cut, "y", 0, 0, tiled=True).reshape(4 * units, quarter)
    arrived = lax.all_gather(near_rows, ("r", "l"), axis=0, tiled=True)
    partial = call(
        up_kernel,
        shape((4 * units, 384)),
        arrived,
        up_mine,
        scratch=[pltpu.VMEM((64 * 60, LANES), F32), pltpu.VMEM((384, quarter), BF16)],
        name="up",
    )
    partial, down_keep = lax.optimization_barrier((partial, down_keep))
    sums = lax.all_to_all(partial.reshape(4, units, 384), "y", 0, 0, tiled=True)
    down_cut = call(
        join_kernel,
        shape((4, 2, columns, group)),
        pair,
        down_keep,
        down_one,
        down_two,
        spaces=([pltpu.SMEM] + [pltpu.VMEM] * 3, pltpu.VMEM),
        name="join",
    )
    sums, down_cut = lax.optimization_barrier((sums, down_cut))
    act = call(act_kernel, shape((units, 384)), sums, name="act")
    act, down_cut = lax.optimization_barrier((act, down_cut))
    down_mine = lax.all_to_all(down_cut, "y", 0, 0, tiled=True)
    act = lax.all_gather(act, "r", axis=0, tiled=True)
    out = call(
        down_kernel,
        shape((64, SLOTS, LANES)),
        act,
        down_mine,
        scratch=[
            pltpu.VMEM((64 * SLOTS, LANES), F32),
            pltpu.VMEM((8 * columns, group), BF16),
        ],
        name="down",
    )
    back = lax.all_to_all(out, "y", 0, 0, tiled=True)
    back = call(sum_kernel, shape((16, SLOTS, LANES)), back, name="sum")
    back = lax.all_to_all(back, ("r", "l"), 0, 0, tiled=True)
    weighted = call(
        weigh_kernel,
        shape((8, SLOTS, LANES)),
        place.reshape(1),
        back,
        whole_rows,
        router_rows,
        spaces=([pltpu.SMEM] + [pltpu.VMEM] * 3, pltpu.VMEM),
        name="weigh",
    )
    weighted = lax.all_to_all(weighted, "p", 0, 0, tiled=True)
    return call(
        add_kernel,
        shape((length, width)),
        attn,
        weighted,
        sel_row,
        scratch=[pltpu.VMEM((8 * SLOTS, LANES), F32), pltpu.VMEM((LANES, width), F32)],
        name="add",
    )


def solution(mesh):
    split = Mesh(mesh.devices.reshape(8, 2, 4, 8), ("r", "l", "y", "p"))
    seq = ("r", "l", "y")
    placed = (
        P(seq, "p"),
        P(seq, "p"),
        P(seq, "p"),
        P(seq, None, None),
        P(None, "p"),
        P("p", seq, None),
        P("p", seq, None),
    )
    return jax.shard_map(
        body, mesh=split, in_specs=placed, out_specs=P(seq, "p"), check_vma=False
    )
```
